32 devices in a mesh: band: 8 (over z, x), slab: 4 (over y, core).
Axes of the slice: x: 2, y: 2, z: 4, core: 2. Of those that a mesh axis runs over, the one named last changes fastest.
Arguments:
- orbitals: float32 [32, 48, 2304], P('band', 'slab'), may hold values from -6 to 6
- partners: int32 [8, 2], replicated, may hold values from 0 to 7, as said below
- counts: int32 [8, 2], replicated, may hold values from 1 to 4
Outputs:
- forces: float32 [32, 48, 2304], P('band', 'slab')
- energy: float32 [], replicated
The draws below stay inside these ranges and needn't reach their ends.
Inputs may be any that keep to these rules, and one draw needn't show every extreme that they name: `partners`: row g names two different band groups, neither of them g.
All inputs are finite; a program needn't handle non-finite values.
Results may differ from the reference program's by a relative error of at most 0.0001.
Values sent between devices are 32-bit elements; how exact they have to be, the bound alone decides.
No kernel may reach another device: no remote copies, remote signals or barrier semaphores. Data moves between devices by JAX's collectives and lax.ppermute only.
A program may use at most 64 MiB of HBM per device.

```python
import jax
import jax.numpy as jnp
from jax import lax

NX = 48
NY = 48
NZ = 48
NZP = 96
YZ = 2304
ORB_G = 4
ORBS = 32
N_BAND = 8


def draw_partners(key, part):
    first_key, second_key = jax.random.split(jax.random.fold_in(key, 17))
    groups = jnp.arange(N_BAND, dtype=jnp.int32)
    offset_one = jax.random.randint(first_key, (N_BAND,), 1, N_BAND)
    offset_two = jax.random.randint(second_key, (N_BAND,), 1, N_BAND - 1)
    offset_two = jnp.where(offset_two >= offset_one, offset_two + 1, offset_two)
    pairs = jnp.stack([(groups + offset_one) % N_BAND, (groups + offset_two) % N_BAND], axis=1)
    return pairs.astype(jnp.int32)


def with_ends(drawn, stream_key, least, largest):
    longest = drawn.shape.index(max(drawn.shape))
    spots = []
    for shift in (0, 1):
        where = [jax.random.randint(jax.random.fold_in(stream_key, axis), (), 0, length) for axis, length in enumerate(drawn.shape)]
        where[longest] = (where[longest] + shift) % drawn.shape[longest]
        spots.append(tuple(where))
    return drawn.at[spots[0]].set(least).at[spots[1]].set(largest)


def steps_of(key, shape, shards, smallest, high):
    level = 1.0
    for position, blocks in shards:
        draws = jax.random.uniform(jax.random.fold_in(jax.random.fold_in(key, 6), position), (blocks,), jnp.float32, smallest / len(shards), high / len(shards))
        level = level * jnp.repeat(jnp.exp(draws), shape[position] // blocks).reshape((-1,) + (1,) * (len(shape) - 1 - position))
    return level


def normal_values(rng, extent, spread, bound, shards=(), held_as=jnp.bfloat16):
    loudness = steps_of(rng, extent, shards, -0.22, 0.18) if shards else 1.0
    entries = jax.random.normal(rng, extent, jnp.float32) * spread * loudness
    return jnp.minimum(jnp.maximum(entries, -bound), bound).astype(held_as)


def setup_inputs(seed: int = 0) -> dict:
    seeds = jax.random.split(jax.random.key(seed), 4)
    return {
        "orbitals": normal_values(seeds[0], (ORBS, NX, YZ), 1.0, 6.0, ((0, 8), (1, 4)), jnp.float32),
        "partners": draw_partners(jax.random.fold_in(seeds[3], 71), 0),
        "counts": with_ends(jax.random.randint(seeds[2], (N_BAND, 2), 1, ORB_G + 1), jax.random.fold_in(seeds[2], 1), 1, ORB_G).astype(jnp.int32),
    }


slater_coeff = -(3.0 / 3.141592653589793) ** (1.0 / 3.0)
exchange_mix = 0.25
screening = 0.25


def kernel_grid():
    wave_x = 2.0 * jnp.pi * jnp.fft.fftfreq(NX)
    wave_y = 2.0 * jnp.pi * jnp.fft.fftfreq(NY)
    wave_z = 2.0 * jnp.pi * jnp.fft.fftfreq(NZP)
    total = wave_x[:, None, None] ** 2 + wave_y[None, :, None] ** 2 + wave_z[None, None, :] ** 2
    return 4.0 * jnp.pi / (total + screening * screening)


def screened_potential(pair_density, kernel_table):
    padded = jnp.pad(pair_density, ((0, 0), (0, 0), (0, 0), (0, NZP - NZ)))
    spectrum = jnp.fft.fftn(padded, axes=(1, 2, 3))
    potential = jnp.real(jnp.fft.ifftn(spectrum * kernel_table, axes=(1, 2, 3)))
    return potential[:, :, :, :NZ].astype(pair_density.dtype)


def reference(orbitals, partners, counts):
    orbital_grid = orbitals.reshape(N_BAND, ORB_G, NX, NY, NZ)
    density = (2.0 / ORBS) * jnp.sum(orbitals * orbitals, axis=0)
    local_pot = slater_coeff * jnp.cbrt(density)
    kernel_table = kernel_grid()
    local_rows = jnp.arange(ORB_G, dtype=jnp.int32)

    def visit(visit_step, loop_state):
        exch, energy = loop_state
        band_index = visit_step // 2
        slot_index = visit_step % 2
        partner = partners[band_index, slot_index]
        own_orbs = orbital_grid[band_index]
        partner_orbs = orbital_grid[partner]
        active = (local_rows < counts[band_index, slot_index]).astype(orbitals.dtype)
        pair_density = own_orbs * partner_orbs * active[:, None, None, None]
        pair_pot = screened_potential(pair_density, kernel_table)
        exch = exch.at[band_index].add(-exchange_mix * pair_pot * partner_orbs)
        exch = exch.at[partner].add(-exchange_mix * pair_pot * own_orbs)
        energy = energy + jnp.sum(pair_density * pair_pot)
        return exch, energy

    start = (jnp.zeros(orbital_grid.shape, jnp.float32), jnp.zeros((), jnp.float32))
    exch, energy = lax.fori_loop(0, 2 * N_BAND, visit, start)
    forces = local_pot[None] * orbitals + exch.reshape(ORBS, NX, NY * NZ)
    energy = -energy / (2.0 * ORBS * NX * NY * NZ)
    return forces, energy
```

```python
import math

import jax
import jax.numpy as jnp
from jax import lax
from jax.sharding import PartitionSpec as P

NX = 48
NY = 48
NZ = 48
NZP = 96


slater_coeff = -((3.0 / math.pi) ** (1.0 / 3.0))
exchange_mix = 0.25
screening = 0.25
highest = lax.Precision.HIGHEST


def dft_block(count_in, count_out, length, sign):
    row_iota = lax.broadcasted_iota(jnp.int32, (count_in, count_out), 0)
    col_iota = lax.broadcasted_iota(jnp.int32, (count_in, count_out), 1)
    phase_angle = 2.0 * math.pi / length * (row_iota * col_iota % length).astype(jnp.float32)
    cosine = jnp.cos(phase_angle)
    sine = jnp.sin(phase_angle)
    upper = jnp.stack([cosine, -sign * sine])
    lower = jnp.stack([sign * sine, cosine])
    return jnp.stack([upper, lower])


def wavenumber_sq(length):
    position = jnp.arange(length, dtype=jnp.int32)
    signed = jnp.where(position > length // 2, position - length, position).astype(jnp.float32)
    wave_number = 2.0 * math.pi / length * signed
    return wave_number * wave_number


def screened_potential(fields):
    spectrum = jnp.einsum(
        "coxyz,cdzk->doxyk", fields, dft_block(NZ, NZP, NZP, 1.0), precision=highest
    )
    spectrum = jnp.einsum(
        "coxyk,cdyq->doxqk", spectrum, dft_block(NY, NY, NY, 1.0), precision=highest
    )
    spectrum = jnp.einsum(
        "coxqk,cdxp->dopqk", spectrum, dft_block(NX, NX, NX, 1.0), precision=highest
    )
    total = (
        wavenumber_sq(NX)[:, None, None]
        + wavenumber_sq(NY)[None, :, None]
        + wavenumber_sq(NZP)[None, None, :]
    )
    kernel_table = 4.0 * math.pi / (NX * NY * NZP) / (total + screening * screening)
    spectrum = spectrum * kernel_table
    spectrum = jnp.einsum(
        "copqk,cdpx->doxqk", spectrum, dft_block(NX, NX, NX, -1.0), precision=highest
    )
    spectrum = jnp.einsum(
        "coxqk,cdqy->doxyk", spectrum, dft_block(NY, NY, NY, -1.0), precision=highest
    )
    return jnp.einsum(
        "coxyk,cdkz->doxyz", spectrum, dft_block(NZP, NZ, NZP, -1.0), precision=highest
    )


def pair_terms(own_orbs, visitors, active):
    per_device = own_orbs.shape[0]
    pair_density = own_orbs[None] * visitors * active[:, :, None, None]
    shaped = pair_density.reshape(2, per_device, NX, NY, NZ)
    fields = screened_potential(shaped).reshape(pair_density.shape)
    own_force = -exchange_mix * jnp.sum(fields * visitors, axis=0)
    partner_force = -exchange_mix * fields * own_orbs[None]
    energy_term = jnp.sum(pair_density * fields)
    return (own_force, partner_force, energy_term)


def request_rows(held_rows, partners, width):
    row_index = (partners[:, :, None] * width + jnp.arange(width, dtype=jnp.int32)).reshape(-1)
    return jnp.take(held_rows, row_index, axis=0)


def return_rows(pieces, partners, bands):
    flat = pieces.reshape(bands * 2, -1)
    targets = jnp.arange(bands, dtype=jnp.int32)[:, None]
    onehot = (partners.reshape(-1)[None, :] == targets).astype(jnp.float32)
    summed = jnp.dot(onehot, flat, precision=highest)
    width = pieces.shape[0] // (bands * 2)
    return summed.reshape((bands * width,) + pieces.shape[1:])


def band_sum(value, bands):
    reach = 1
    while reach < bands:
        value = value + lax.ppermute(value, "band", [(i, i ^ reach) for i in range(bands)])
        reach *= 2
    return value


def total_of(value, devices):
    sent = jnp.broadcast_to(value, (devices, 1, 128))
    return jnp.sum(lax.all_to_all(sent, ("band", "slab"), 0, 0)[:, 0, 0])


def body(orbitals, partners, counts):
    bands = lax.axis_size("band")
    slabs = lax.axis_size("slab")
    band_index = lax.axis_index("band")
    slab_index = lax.axis_index("slab")
    orb_group = orbitals.shape[0]
    per_device = orb_group // slabs
    total_orbs = orb_group * bands
    squares = jnp.sum(orbitals * orbitals, axis=0)
    density = 2.0 / total_orbs * band_sum(squares, bands)
    local_pot = slater_coeff * jnp.cbrt(density)
    band_match = jnp.arange(bands, dtype=jnp.int32)[:, None] == band_index
    my_counts = jnp.sum(jnp.where(band_match, counts, 0), axis=0)
    local_rows = slab_index * per_device + jnp.arange(per_device, dtype=jnp.int32)
    active = (local_rows[None, :] < my_counts[:, None]).astype(jnp.float32)
    own_orbs = lax.all_to_all(orbitals, "slab", split_axis=0, concat_axis=1, tiled=True)
    held_rows = lax.all_to_all(own_orbs, "band", split_axis=1, concat_axis=0, tiled=True)
    wanted = request_rows(held_rows, partners, per_device)
    visitors = lax.all_to_all(wanted, "band", split_axis=0, concat_axis=1, tiled=True)
    visitors = visitors.reshape((2, per_device) + own_orbs.shape[1:])
    own_force, partner_force, energy_term = pair_terms(own_orbs, visitors, active)
    outgoing = partner_force.reshape((2 * per_device,) + own_orbs.shape[1:])
    outgoing = lax.all_to_all(outgoing, "band", split_axis=1, concat_axis=0, tiled=True)
    returned = lax.all_to_all(
        return_rows(outgoing, partners, bands), "band", split_axis=0, concat_axis=1, tiled=True
    )
    exchange_force = lax.all_to_all(
        own_force + returned, "slab", split_axis=1, concat_axis=0, tiled=True
    )
    energy_total = total_of(energy_term, bands * slabs)
    energy = -energy_total / (2.0 * total_orbs * NX * NY * NZ)
    forces = local_pot[None] * orbitals + exchange_force
    return (forces, energy)


def solution(mesh):
    placed = (P("band", "slab", None), P(), P())
    return jax.shard_map(
        body, mesh=mesh, in_specs=placed, out_specs=(P("band", "slab", None), P()), check_vma=False
    )
```

```python
import functools
import math

import jax
import jax.numpy as jnp
from jax import lax
from jax.experimental import pallas as pl
from jax.experimental.pallas import tpu as pltpu
from jax.sharding import PartitionSpec as P

NX = 48
NY = 48
NZ = 48
NZP = 96


slater_coeff = -((3.0 / math.pi) ** (1.0 / 3.0))
exchange_mix = 0.25
screening = 0.25
row_row = (((1,), (1,)), ((), ()))


def split(value):
    high = value.astype(jnp.bfloat16)
    low = (value - high.astype(jnp.float32)).astype(jnp.bfloat16)
    return high, low


def cas(rows, cols, length):
    phase_angle = 2.0 * math.pi / length * (rows * cols % length).astype(jnp.float32)
    return jnp.cos(phase_angle) + jnp.sin(phase_angle)


def split_table(matrix):
    high = lax.reduce_precision(matrix, 8, 7)
    return high.astype(jnp.bfloat16), (matrix - high).astype(jnp.bfloat16)


def wide(matrix):
    high, low = split_table(matrix)
    return jnp.concatenate([high, high, low], axis=1)


def tall(matrix):
    high, low = split_table(matrix)
    return jnp.concatenate([high, low], axis=0)


def wavenumber_sq(length):
    position = jnp.arange(length, dtype=jnp.int32)
    signed = jnp.where(position > length // 2, position - length, position).astype(jnp.float32)
    wave_number = 2.0 * math.pi / length * signed
    return wave_number * wave_number


def transform_tables(held_x):
    x_waves = jnp.arange(NX, dtype=jnp.int32)
    y_cells = jnp.arange(NY, dtype=jnp.int32)
    z_cells = jnp.arange(NZ, dtype=jnp.int32)
    z_waves = jnp.arange(NZP, dtype=jnp.int32)
    total = (
        wavenumber_sq(NZP)[:, None, None]
        + wavenumber_sq(NX)[None, :, None]
        + wavenumber_sq(NY)[None, None, :]
    )
    kernel_table = 4.0 * math.pi / (NX * NY * NZP) / (total + screening * screening)
    y_matrix = cas(y_cells[:, None], y_cells[None, :], NY)
    return (
        wide(cas(x_waves[:, None], held_x[None, :], NX)),
        wide(y_matrix),
        tall(cas(z_waves[:, None], z_cells[None, :], NZP)),
        kernel_table.reshape(NZP, NX * NY),
        wide(cas(z_cells[:, None], z_waves[None, :], NZP)),
        tall(y_matrix),
        wide(cas(held_x[:, None], x_waves[None, :], NX)),
    )


def apply_left(matrix, value):
    high, low = split(value)
    stacked = jnp.concatenate([high, low, high], axis=0)
    return jnp.dot(matrix, stacked, preferred_element_type=jnp.float32)


def apply_rows(matrix, high, low):
    half = matrix.shape[0] // 2
    both = lax.dot_general(matrix, high, row_row, preferred_element_type=jnp.float32)
    rest = lax.dot_general(matrix[:half], low, row_row, preferred_element_type=jnp.float32)
    return both[:half] + both[half:] + rest


def pair_kernel(
    slot, weights, own_ref, other_ref, x_fwd, y_fwd, z_fwd, table, z_inv, y_inv, x_inv,
    force_in, energy_in, force_out, energy_out, lines, high_rows, low_rows, field,
):
    total_weight = weights[slot, 0]
    request_weight = weights[slot, 1]

    @pl.when(total_weight == 0.0)
    def _():
        force_out[...] = force_in[...]
        energy_out[...] = energy_in[...]

    @pl.when(total_weight != 0.0)
    def _():
        other = other_ref[...]
        density = own_ref[...] * other
        spectrum = apply_left(x_fwd[...], density)
        for y in range(NY):
            lines[y * NX : (y + 1) * NX, :] = spectrum[:, y * NZ : (y + 1) * NZ]
        for q in range(NX):
            plane = apply_left(y_fwd[...], lines[pl.ds(q, NY, stride=NX), :])
            high, low = split(plane)
            high_rows[q * NY : (q + 1) * NY, :] = high
            low_rows[q * NY : (q + 1) * NY, :] = low
        spectrum = apply_rows(z_fwd[...], high_rows[...], low_rows[...]) * table[...]
        spectrum = apply_left(z_inv[...], spectrum)
        for q in range(NX):
            high, low = split(spectrum[:, q * NY : (q + 1) * NY])
            high_rows[q * NZ : (q + 1) * NZ, :] = high
            low_rows[q * NZ : (q + 1) * NZ, :] = low
        spectrum = apply_rows(y_inv[...], high_rows[...], low_rows[...])
        for q in range(NX):
            lines[q * NY : (q + 1) * NY, :] = spectrum[:, q * NZ : (q + 1) * NZ]
        for y in range(NY):
            field[:, y * NZ : (y + 1) * NZ] = apply_left(
                x_inv[...], lines[pl.ds(y, NX, stride=NY), :]
            )
        potential = field[...]
        force_out[...] = force_in[...] - (exchange_mix * total_weight) * (potential * other)
        products = jnp.sum(density * potential, axis=0, keepdims=True)
        folded = products[:, :128]
        for start in range(128, NY * NZ, 128):
            folded = folded + products[:, start : start + 128]
        energy_out[...] = energy_in[...] + request_weight * folded


def pair_step(slot, weights, own, other, tables, force, energy):
    whole = pl.BlockSpec(memory_space=pltpu.VMEM)
    return pl.pallas_call(
        functools.partial(pair_kernel, slot),
        out_shape=(
            jax.ShapeDtypeStruct(force.shape, jnp.float32),
            jax.ShapeDtypeStruct(energy.shape, jnp.float32),
        ),
        in_specs=[pl.BlockSpec(memory_space=pltpu.SMEM)] + [whole] * (4 + len(tables)),
        out_specs=(whole, whole),
        scratch_shapes=[
            pltpu.VMEM((NX * NY, NZ), jnp.float32),
            pltpu.VMEM((NX * NY, NZ), jnp.bfloat16),
            pltpu.VMEM((NX * NY, NZ), jnp.bfloat16),
            pltpu.VMEM((NX, NY * NZ), jnp.float32),
        ],
        compiler_params=pltpu.CompilerParams(vmem_limit_bytes=32 << 20),
        cost_estimate=pl.CostEstimate(flops=3 << 30, transcendentals=0, bytes_accessed=3 << 20),
        name="pair_step",
    )(weights, own, other, *tables, force, energy)


def fold_of(planes, cells):
    return 2 if (2 * planes) % 8 == 0 and cells % 256 == 0 else 1


def prepare_kernel(fold, place, orbitals, *out_refs):
    squares_ref = out_refs[-1]
    planes, cells = orbitals.shape[1:]
    part = cells // fold
    slabs = len(out_refs) - 1
    squares = jnp.zeros((planes, cells), jnp.float32)
    for r in range(slabs):
        block = orbitals[place[0] ^ r]
        squares = squares + block * block
        for f in range(fold):
            out_refs[r][f * planes : (f + 1) * planes, :] = block[:, f * part : (f + 1) * part]
    for f in range(fold):
        squares_ref[f * planes : (f + 1) * planes, :] = squares[:, f * part : (f + 1) * part]


def prepare(place, orbitals):
    slabs, planes, cells = orbitals.shape
    fold = fold_of(planes, cells)
    piece = jax.ShapeDtypeStruct((planes * fold, cells // fold), jnp.float32)
    return pl.pallas_call(
        functools.partial(prepare_kernel, fold),
        out_shape=[piece] * (slabs + 1),
        in_specs=[pl.BlockSpec(memory_space=pltpu.SMEM), pl.BlockSpec(memory_space=pltpu.VMEM)],
        name="prepare",
    )(place, orbitals)


def assemble_kernel(fold, *refs):
    out_ref = refs[-1]
    planes = refs[0].shape[0] // fold
    part = refs[0].shape[1]
    for r, ref in enumerate(refs[:-1]):
        for f in range(fold):
            out_ref[r * planes : (r + 1) * planes, f * part : (f + 1) * part] = ref[
                f * planes : (f + 1) * planes, :
            ]


def assemble(pieces):
    rows, part = pieces[0].shape
    fold = NY * NZ // part
    return pl.pallas_call(
        functools.partial(assemble_kernel, fold),
        out_shape=jax.ShapeDtypeStruct((NX, NY * NZ), jnp.float32),
        name="assemble",
    )(*pieces)


def cut_kernel(fold, whole_ref, *out_refs):
    planes = out_refs[0].shape[0] // fold
    part = out_refs[0].shape[1]
    for r, ref in enumerate(out_refs):
        for f in range(fold):
            ref[f * planes : (f + 1) * planes, :] = whole_ref[
                r * planes : (r + 1) * planes, f * part : (f + 1) * part
            ]


def cut(whole, slabs):
    planes = whole.shape[0] // slabs
    cells = whole.shape[1]
    fold = fold_of(planes, cells)
    piece = jax.ShapeDtypeStruct((planes * fold, cells // fold), jnp.float32)
    return pl.pallas_call(
        functools.partial(cut_kernel, fold), out_shape=[piece] * slabs, name="cut"
    )(whole)


def finish_kernel(fold, place, orbitals, local_pot, *refs):
    out_ref = refs[-1]
    planes, cells = orbitals.shape[1:]
    part = cells // fold
    for r, ref in enumerate(refs[:-1]):
        target = place[0] ^ r
        block = orbitals[target]
        for f in range(fold):
            rows = slice(f * planes, (f + 1) * planes)
            cols = slice(f * part, (f + 1) * part)
            out_ref[target, :, cols] = local_pot[rows, :] * block[:, cols] + ref[rows, :]


def finish(place, orbitals, local_pot, pieces):
    planes, cells = orbitals.shape[1:]
    fold = fold_of(planes, cells)
    whole = pl.BlockSpec(memory_space=pltpu.VMEM)
    return pl.pallas_call(
        functools.partial(finish_kernel, fold),
        out_shape=jax.ShapeDtypeStruct(orbitals.shape, jnp.float32),
        in_specs=[pl.BlockSpec(memory_space=pltpu.SMEM)] + [whole] * (2 + len(pieces)),
        name="finish",
    )(place, orbitals, local_pot, *pieces)


def swap(value, axis, reach):
    size = lax.axis_size(axis)
    return lax.ppermute(value, axis, [(i, i ^ reach) for i in range(size)])


def band_sum(value, bands):
    reach = 1
    while reach < bands:
        value = value + swap(value, "band", reach)
        reach *= 2
    return value


def total_of(value, devices):
    sent = jnp.broadcast_to(value[None], (devices,) + value.shape)
    return jnp.sum(lax.all_to_all(sent, ("band", "slab"), 0, 0))


def gather_line(own, band_index, bands):
    place = band_index // 2
    inner = (place == 1) | (place == 2)

    def along(value, pairs):
        moves = [(2 * a + side, 2 * b + side) for a, b in pairs for side in (0, 1)]
        return lax.ppermute(value, "band", moves)

    side_own = swap(own, "band", 1)
    near = along(own, [(0, 1), (1, 0), (2, 3), (3, 2)])
    middle = along(own, [(1, 2), (2, 1)])
    side_near = swap(near, "band", 1)
    outward = along(middle, [(1, 0), (2, 3)])
    across = along(near, [(1, 2), (2, 1)])
    second = jnp.where(inner, middle, outward)
    side_second = swap(second, "band", 1)
    outer = along(across, [(1, 0), (2, 3)])
    third = jnp.where(inner, across, outer)
    side_third = swap(third, "band", 1)
    side = band_index % 2
    second_group = jnp.where(place < 2, 2, 1) * 2 + side
    third_group = jnp.where(place < 2, 3, 0) * 2 + side
    near_group = band_index ^ 2
    return [
        (near, near_group),
        (side_own, band_index ^ 1),
        (side_near, near_group ^ 1),
        (second, second_group),
        (third, third_group),
        (side_second, second_group ^ 1),
        (side_third, third_group ^ 1),
    ]


def gather_doubling(own, band_index, bands):
    held = [(own, band_index)]
    reach = 1
    while reach < bands:
        held = held + [(swap(block, "band", reach), group ^ reach) for block, group in held]
        reach *= 2
    return held[1:]


def body(orbitals, partners, counts):
    bands = lax.axis_size("band")
    slabs = lax.axis_size("slab")
    band_index = lax.axis_index("band")
    slab_index = lax.axis_index("slab")
    orb_group = orbitals.shape[0]
    total_orbs = orb_group * bands
    planes = orbitals.shape[1]
    assert orb_group == slabs

    place = slab_index.astype(jnp.int32).reshape(1)
    *sends, squares = prepare(place, orbitals)
    pieces = [sends[0]] + [swap(sends[r], "slab", r) for r in range(1, slabs)]
    own = assemble(pieces)

    gather = gather_line if bands // 2 == 4 else gather_doubling
    others = gather(own, band_index, bands)

    row = jnp.arange(NX, dtype=jnp.int32)
    held_x = (slab_index ^ (row // planes)) * planes + row % planes
    tables = transform_tables(held_x)

    groups = jnp.stack([group for _, group in others]).astype(jnp.int32)
    active = (slab_index < counts).astype(jnp.float32)
    mine = jnp.arange(bands, dtype=jnp.int32)[:, None] == band_index
    my_partners = jnp.sum(jnp.where(mine, partners, 0), axis=0)
    my_active = jnp.sum(jnp.where(mine, active, 0.0), axis=0)
    requested = jnp.sum(
        jnp.where(groups[:, None] == my_partners[None, :], my_active[None, :], 0.0), axis=1
    )
    wanted_by = jnp.sum(jnp.where(partners == band_index, active, 0.0), axis=1)
    chosen = groups[:, None] == jnp.arange(bands, dtype=jnp.int32)[None, :]
    returned = jnp.sum(jnp.where(chosen, wanted_by[None, :], 0.0), axis=1)
    weights = jnp.stack([requested + returned, requested], axis=1)

    density = 2.0 / total_orbs * band_sum(squares, bands)
    local_pot = slater_coeff * jnp.cbrt(density)

    force = jnp.zeros((NX, NY * NZ), jnp.float32)
    energy = jnp.zeros((1, 128), jnp.float32)
    for slot, (other, _) in enumerate(others):
        force, energy = pair_step(slot, weights, own, other, tables, force, energy)

    outgoing = cut(force, slabs)
    arrived = [outgoing[0]] + [swap(outgoing[r], "slab", r) for r in range(1, slabs)]
    energy_total = total_of(energy, bands * slabs)
    forces = finish(place, orbitals, local_pot, arrived)
    return (forces, -energy_total / (2.0 * total_orbs * NX * NY * NZ))


def solution(mesh):
    placed = (P("band", "slab", None), P(), P())
    return jax.shard_map(
        body, mesh=mesh, in_specs=placed, out_specs=(P("band", "slab", None), P()), check_vma=False
    )
```

```python
import functools
import math

import jax
import jax.numpy as jnp
from jax import lax
from jax.experimental import pallas as pl
from jax.experimental.pallas import tpu as pltpu
from jax.sharding import PartitionSpec as P

NX = 48
NY = 48
NZ = 48
NZP = 96


slater_coeff = -((3.0 / math.pi) ** (1.0 / 3.0))
exchange_mix = 0.25
screening = 0.25
row_row = (((1,), (1,)), ((), ()))


def split(value):
    high = value.astype(jnp.bfloat16)
    low = (value - high.astype(jnp.float32)).astype(jnp.bfloat16)
    return high, low


def cas(rows, cols, length):
    phase_angle = 2.0 * math.pi / length * (rows * cols % length).astype(jnp.float32)
    return jnp.cos(phase_angle) + jnp.sin(phase_angle)


def split_table(matrix):
    high = lax.reduce_precision(matrix, 8, 7)
    return high.astype(jnp.bfloat16), (matrix - high).astype(jnp.bfloat16)


def wide(matrix):
    high, low = split_table(matrix)
    return jnp.concatenate([high, high, low], axis=1)


def tall(matrix):
    high, low = split_table(matrix)
    return jnp.concatenate([high, low], axis=0)


def wavenumber_sq(length):
    position = jnp.arange(length, dtype=jnp.int32)
    signed = jnp.where(position > length // 2, position - length, position).astype(jnp.float32)
    wave_number = 2.0 * math.pi / length * signed
    return wave_number * wave_number


def transform_tables(held_x):
    x_waves = jnp.arange(NX, dtype=jnp.int32)
    y_cells = jnp.arange(NY, dtype=jnp.int32)
    z_cells = jnp.arange(NZ, dtype=jnp.int32)
    z_waves = jnp.arange(NZP, dtype=jnp.int32)
    total = (
        wavenumber_sq(NZP)[:, None, None]
        + wavenumber_sq(NX)[None, :, None]
        + wavenumber_sq(NY)[None, None, :]
    )
    kernel_table = 4.0 * math.pi / (NX * NY * NZP) / (total + screening * screening)
    y_matrix = cas(y_cells[:, None], y_cells[None, :], NY)
    return (
        wide(cas(x_waves[:, None], held_x[None, :], NX)),
        wide(y_matrix),
        tall(cas(z_waves[:, None], z_cells[None, :], NZP)),
        kernel_table.reshape(NZP, NX * NY),
        wide(cas(z_cells[:, None], z_waves[None, :], NZP)),
        tall(y_matrix),
        wide(cas(held_x[:, None], x_waves[None, :], NX)),
    )


def apply_left(matrix, value):
    high, low = split(value)
    stacked = jnp.concatenate([high, low, high], axis=0)
    return jnp.dot(matrix, stacked, preferred_element_type=jnp.float32)


def apply_rows(matrix, high, low):
    half = matrix.shape[0] // 2
    both = lax.dot_general(matrix, high, row_row, preferred_element_type=jnp.float32)
    rest = lax.dot_general(matrix[:half], low, row_row, preferred_element_type=jnp.float32)
    return both[:half] + both[half:] + rest


def store_force(force_refs, value):
    if len(force_refs) == 1:
        force_refs[0][...] = value
        return
    planes = NX // len(force_refs)
    fold = force_refs[0].shape[0] // planes
    part = force_refs[0].shape[1]
    for r, ref in enumerate(force_refs):
        for f in range(fold):
            ref[f * planes : (f + 1) * planes, :] = value[
                r * planes : (r + 1) * planes, f * part : (f + 1) * part
            ]


def pair_kernel(
    slot, weights, own_ref, other_ref, x_fwd, y_fwd, z_fwd, table, z_inv, y_inv, x_inv,
    force_in, energy_in, energy_out, *refs,
):
    *force_refs, lines, high_rows, low_rows, field = refs
    total_weight = weights[slot, 0]
    request_weight = weights[slot, 1]

    @pl.when(total_weight == 0.0)
    def _():
        store_force(force_refs, force_in[...])
        energy_out[...] = energy_in[...]

    @pl.when(total_weight != 0.0)
    def _():
        other = other_ref[...]
        density = own_ref[...] * other
        spectrum = apply_left(x_fwd[...], density)
        for y in range(NY):
            lines[y * NX : (y + 1) * NX, :] = spectrum[:, y * NZ : (y + 1) * NZ]
        for q in range(NX):
            plane = apply_left(y_fwd[...], lines[pl.ds(q, NY, stride=NX), :])
            high, low = split(plane)
            high_rows[q * NY : (q + 1) * NY, :] = high
            low_rows[q * NY : (q + 1) * NY, :] = low
        spectrum = apply_rows(z_fwd[...], high_rows[...], low_rows[...])
        weighted = spectrum * table[...]
        products = jnp.sum(spectrum * weighted, axis=0, keepdims=True)
        folded = products[:, :128]
        for start in range(128, NX * NY, 128):
            folded = folded + products[:, start : start + 128]
        energy_out[...] = energy_in[...] + request_weight * folded
        spectrum = apply_left(z_inv[...], weighted)
        for q in range(NX):
            high, low = split(spectrum[:, q * NY : (q + 1) * NY])
            high_rows[q * NZ : (q + 1) * NZ, :] = high
            low_rows[q * NZ : (q + 1) * NZ, :] = low
        spectrum = apply_rows(y_inv[...], high_rows[...], low_rows[...])
        for q in range(NX):
            lines[q * NY : (q + 1) * NY, :] = spectrum[:, q * NZ : (q + 1) * NZ]
        for y in range(NY):
            field[:, y * NZ : (y + 1) * NZ] = apply_left(
                x_inv[...], lines[pl.ds(y, NX, stride=NY), :]
            )
        store_force(
            force_refs, force_in[...] - (exchange_mix * total_weight) * (field[...] * other)
        )


def pair_step(slot, weights, own, other, tables, force, energy, pieces):
    if pieces == 1:
        piece = force.shape
    else:
        planes = NX // pieces
        fold = fold_of(planes, NY * NZ)
        piece = (planes * fold, NY * NZ // fold)
    outs = [jax.ShapeDtypeStruct(energy.shape, jnp.float32)]
    outs += [jax.ShapeDtypeStruct(piece, jnp.float32)] * pieces
    return pl.pallas_call(
        functools.partial(pair_kernel, slot),
        out_shape=outs,
        in_specs=with_scalar(4 + len(tables)),
        out_specs=in_vmem(1 + pieces),
        scratch_shapes=[
            pltpu.VMEM((NX * NY, NZ), jnp.float32),
            pltpu.VMEM((NX * NY, NZ), jnp.bfloat16),
            pltpu.VMEM((NX * NY, NZ), jnp.bfloat16),
            pltpu.VMEM((NX, NY * NZ), jnp.float32),
        ],
        compiler_params=pltpu.CompilerParams(vmem_limit_bytes=32 << 20),
        cost_estimate=pl.CostEstimate(flops=3 << 30, transcendentals=0, bytes_accessed=3 << 20),
        name="pair_step",
    )(weights, own, other, *tables, force, energy)


def fold_of(planes, cells):
    return 2 if (2 * planes) % 8 == 0 and cells % 256 == 0 else 1


def in_vmem(count):
    return [pl.BlockSpec(memory_space=pltpu.VMEM)] * count


def with_scalar(count):
    return [pl.BlockSpec(memory_space=pltpu.SMEM)] + in_vmem(count)


def pick(place, choices):
    chosen = choices[0]
    for index in range(1, len(choices)):
        chosen = jnp.where(place == index, choices[index], chosen)
    return chosen


def prepare_kernel(fold, place, orbitals, *out_refs):
    squares_ref = out_refs[-1]
    planes, slabs, cells = orbitals.shape
    part = cells // fold
    for f in range(fold):
        rows = slice(f * planes, (f + 1) * planes)
        blocks = [orbitals[:, j, f * part : (f + 1) * part] for j in range(slabs)]
        squares_ref[rows, :] = sum(block * block for block in blocks)
        for r in range(slabs):
            out_refs[r][rows, :] = pick(place[0] ^ r, blocks)


def prepare(place, orbitals):
    planes, slabs, cells = orbitals.shape
    fold = fold_of(planes, cells)
    piece = jax.ShapeDtypeStruct((planes * fold, cells // fold), jnp.float32)
    return pl.pallas_call(
        functools.partial(prepare_kernel, fold),
        out_shape=[piece] * (slabs + 1),
        in_specs=with_scalar(1),
        out_specs=in_vmem(slabs + 1),
        compiler_params=pltpu.CompilerParams(vmem_limit_bytes=8 << 20),
        name="prepare",
    )(place, orbitals)


def assemble_kernel(fold, *refs):
    out_ref = refs[-1]
    planes = refs[0].shape[0] // fold
    part = refs[0].shape[1]
    for r, ref in enumerate(refs[:-1]):
        for f in range(fold):
            out_ref[r * planes : (r + 1) * planes, f * part : (f + 1) * part] = ref[
                f * planes : (f + 1) * planes, :
            ]


def assemble(pieces):
    rows, part = pieces[0].shape
    fold = NY * NZ // part
    return pl.pallas_call(
        functools.partial(assemble_kernel, fold),
        out_shape=jax.ShapeDtypeStruct((NX, NY * NZ), jnp.float32),
        in_specs=in_vmem(len(pieces)),
        out_specs=in_vmem(1)[0],
        compiler_params=pltpu.CompilerParams(vmem_limit_bytes=8 << 20),
        name="assemble",
    )(*pieces)


def finish_kernel(fold, place, orbitals, local_pot, *refs):
    out_ref = refs[-1]
    planes, slabs, cells = orbitals.shape
    part = cells // fold
    for f in range(fold):
        rows = slice(f * planes, (f + 1) * planes)
        cols = slice(f * part, (f + 1) * part)
        pieces = [ref[rows, :] for ref in refs[:-1]]
        local = local_pot[rows, :]
        for j in range(slabs):
            out_ref[:, j, cols] = local * orbitals[:, j, cols] + pick(place[0] ^ j, pieces)


def finish(place, orbitals, local_pot, pieces):
    planes, slabs, cells = orbitals.shape
    return pl.pallas_call(
        functools.partial(finish_kernel, fold_of(planes, cells)),
        out_shape=jax.ShapeDtypeStruct(orbitals.shape, jnp.float32),
        in_specs=with_scalar(2 + len(pieces)),
        out_specs=in_vmem(1)[0],
        compiler_params=pltpu.CompilerParams(vmem_limit_bytes=8 << 20),
        name="finish",
    )(place, orbitals, local_pot, *pieces)


def swap(value, axis, reach):
    size = lax.axis_size(axis)
    return lax.ppermute(value, axis, [(i, i ^ reach) for i in range(size)])


def total_of(value, devices):
    sent = jnp.broadcast_to(value[None], (devices,) + value.shape)
    return jnp.sum(lax.all_to_all(sent, ("band", "slab"), 0, 0))


def gather_line(own, squares, band_index, bands):
    place = band_index // 2
    inner = (place == 1) | (place == 2)
    half = own.shape[0] // 2

    def along(value, pairs):
        moves = [(2 * a + side, 2 * b + side) for a, b in pairs for side in (0, 1)]
        return lax.ppermute(value, "band", moves)

    outer_pairs = [(1, 0), (2, 3)]
    inner_pairs = [(1, 2), (2, 1)]
    near = along(own, [(0, 1), (1, 0), (2, 3), (3, 2)])
    side_own = swap(own, "band", 1)
    middle = along(own, inner_pairs)
    near_squares = swap(squares, "band", 2)
    near, near_squares = lax.optimization_barrier((near, near_squares))
    squares = squares + near_squares

    side_near = swap(near, "band", 1)
    across = along(near, inner_pairs)
    outward = along(middle, outer_pairs)
    far_squares = swap(squares, "band", 4)
    outward, far_squares = lax.optimization_barrier((outward, far_squares))
    squares = squares + far_squares

    second = jnp.where(inner, middle, outward)
    side_late = swap(jnp.where(inner, across, outward), "band", 1)
    outer = along(across, outer_pairs)
    side_middle = along(side_own, inner_pairs)
    third = jnp.where(inner, across, outer)

    ends = [(i, i ^ 1) for i in range(bands) if i // 2 in (0, 3)]
    side_head = lax.ppermute(outer[:half], "band", ends)
    side_tail = along(side_late[half:], outer_pairs)
    side_last = jnp.where(inner, side_middle, jnp.concatenate([side_head, side_tail], axis=0))

    side = band_index % 2
    near_group = band_index ^ 2
    second_group = jnp.where(place < 2, 2, 1) * 2 + side
    third_group = jnp.where(place < 2, 3, 0) * 2 + side
    late_group = jnp.where(inner, third_group, second_group) ^ 1
    last_group = jnp.where(inner, second_group, third_group) ^ 1
    blocks = [
        (near, near_group),
        (side_own, band_index ^ 1),
        (side_near, near_group ^ 1),
        (second, second_group),
        (third, third_group),
        (side_late, late_group),
        (side_last, last_group),
    ]
    return blocks, squares


def gather_doubling(own, squares, band_index, bands):
    held = [(own, band_index)]
    reach = 1
    while reach < bands:
        if reach > 1:
            squares = squares + swap(squares, "band", reach)
        held = held + [(swap(block, "band", reach), group ^ reach) for block, group in held]
        reach *= 2
    return held[1:], squares


def body(orbitals, partners, counts):
    bands = lax.axis_size("band")
    slabs = lax.axis_size("slab")
    band_index = lax.axis_index("band")
    slab_index = lax.axis_index("slab")
    orb_group, planes, cells = orbitals.shape
    total_orbs = orb_group * bands
    assert orb_group == slabs

    place = slab_index.astype(jnp.int32).reshape(1)
    by_plane = jnp.transpose(orbitals, (1, 0, 2))
    *sends, squares = prepare(place, by_plane)
    pieces = [sends[0]] + [swap(sends[r], "slab", r) for r in range(1, slabs)]
    side_squares = swap(squares, "band", 1)
    pieces, side_squares = lax.optimization_barrier((pieces, side_squares))
    own = assemble(pieces)

    gather = gather_line if bands // 2 == 4 else gather_doubling
    others, squares = gather(own, squares + side_squares, band_index, bands)

    row = jnp.arange(NX, dtype=jnp.int32)
    held_x = (slab_index ^ (row // planes)) * planes + row % planes
    tables = transform_tables(held_x)

    groups = jnp.stack([group for _, group in others]).astype(jnp.int32)
    active = (slab_index < counts).astype(jnp.float32)
    mine = jnp.arange(bands, dtype=jnp.int32)[:, None] == band_index
    my_partners = jnp.sum(jnp.where(mine, partners, 0), axis=0)
    my_active = jnp.sum(jnp.where(mine, active, 0.0), axis=0)
    requested = jnp.sum(
        jnp.where(groups[:, None] == my_partners[None, :], my_active[None, :], 0.0), axis=1
    )
    wanted_by = jnp.sum(jnp.where(partners == band_index, active, 0.0), axis=1)
    chosen = groups[:, None] == jnp.arange(bands, dtype=jnp.int32)[None, :]
    returned = jnp.sum(jnp.where(chosen, wanted_by[None, :], 0.0), axis=1)
    weights = jnp.stack([requested + returned, requested], axis=1)

    local_pot = slater_coeff * jnp.cbrt(2.0 / total_orbs * squares)

    outgoing = [jnp.zeros((NX, NY * NZ), jnp.float32)]
    energy = jnp.zeros((1, 128), jnp.float32)
    for slot, (other, _) in enumerate(others):
        pieces = slabs if slot == len(others) - 1 else 1
        energy, *outgoing = pair_step(
            slot, weights, own, other, tables, outgoing[0], energy, pieces
        )

    arrived = [outgoing[0]] + [swap(outgoing[r], "slab", r) for r in range(1, slabs)]
    energy_total = total_of(energy, bands * slabs)
    forces = jnp.transpose(finish(place, by_plane, local_pot, arrived), (1, 0, 2))
    return (forces, -energy_total / (2.0 * total_orbs * NX * NY * NZ))


def solution(mesh):
    placed = (P("band", "slab", None), P(), P())
    return jax.shard_map(
        body, mesh=mesh, in_specs=placed, out_specs=(P("band", "slab", None), P()), check_vma=False
    )
```

```python
import functools
import math

import jax
import jax.numpy as jnp
from jax import lax
from jax.experimental import pallas as pl
from jax.experimental.pallas import tpu as pltpu
from jax.sharding import PartitionSpec as P


NX = 48
NY = 48
NZ = 48
NZP = 96


slater_coeff = -((3.0 / math.pi) ** (1.0 / 3.0))
exchange_mix = 0.25
screening = 0.25
row_row = (((1,), (1,)), ((), ()))


def split(value):
    high = value.astype(jnp.bfloat16)
    low = (value - high.astype(jnp.float32)).astype(jnp.bfloat16)
    return high, low


def cas(rows, cols, length):
    phase_angle = 2.0 * math.pi / length * (rows * cols % length).astype(jnp.float32)
    return jnp.cos(phase_angle) + jnp.sin(phase_angle)


def split_table(matrix):
    high = lax.reduce_precision(matrix, 8, 7)
    return high.astype(jnp.bfloat16), (matrix - high).astype(jnp.bfloat16)


def wide(matrix):
    high, low = split_table(matrix)
    return jnp.concatenate([high, high, low], axis=1)


def tall(matrix):
    high, low = split_table(matrix)
    return jnp.concatenate([high, low], axis=0)


def wavenumber_sq(length):
    position = jnp.arange(length, dtype=jnp.int32)
    signed = jnp.where(position > length // 2, position - length, position).astype(jnp.float32)
    wave_number = 2.0 * math.pi / length * signed
    return wave_number * wave_number


def transform_tables(held_x):
    x_waves = jnp.arange(NX, dtype=jnp.int32)
    y_cells = jnp.arange(NY, dtype=jnp.int32)
    z_cells = jnp.arange(NZ, dtype=jnp.int32)
    z_waves = jnp.arange(NZP, dtype=jnp.int32)
    total = (
        wavenumber_sq(NZP)[:, None, None]
        + wavenumber_sq(NX)[None, :, None]
        + wavenumber_sq(NY)[None, None, :]
    )
    kernel_table = 4.0 * math.pi / (NX * NY * NZP) / (total + screening * screening)
    y_matrix = cas(y_cells[:, None], y_cells[None, :], NY)
    return (
        wide(cas(x_waves[:, None], held_x[None, :], NX)),
        wide(y_matrix),
        tall(cas(z_waves[:, None], z_cells[None, :], NZP)),
        kernel_table.reshape(NZP, NX * NY),
        wide(cas(z_cells[:, None], z_waves[None, :], NZP)),
        tall(y_matrix),
        wide(cas(held_x[:, None], x_waves[None, :], NX)),
    )


def apply_left(matrix, value):
    high, low = split(value)
    stacked = jnp.concatenate([high, low, high], axis=0)
    return jnp.dot(matrix, stacked, preferred_element_type=jnp.float32)


def apply_rows(matrix, high, low):
    half = matrix.shape[0] // 2
    both = lax.dot_general(matrix, high, row_row, preferred_element_type=jnp.float32)
    rest = lax.dot_general(matrix[:half], low, row_row, preferred_element_type=jnp.float32)
    return both[:half] + both[half:] + rest


def cut_into(refs, value, part_index):
    planes = NX // len(refs)
    part = refs[0].shape[1]
    fold = NY * NZ // part
    first = part_index * planes * fold
    for r, ref in enumerate(refs):
        for f in range(fold):
            ref[first + f * planes : first + (f + 1) * planes, :] = value[
                r * planes : (r + 1) * planes, f * part : (f + 1) * part
            ]


def store_force(force_refs, value):
    if len(force_refs) == 1:
        force_refs[0][...] = value
    else:
        cut_into(force_refs, value, 0)


def pair_kernel(
    slot, weights, own_ref, other_ref, x_fwd, y_fwd, z_fwd, table, z_inv, y_inv, x_inv,
    force_in, energy_in, *refs,
):
    *refs, lines, high_rows, low_rows, field = refs
    if len(refs) == 2:
        energy_out, *force_refs = refs
    else:
        squares_in, energy_out, *force_refs = refs
        cut_into(force_refs, squares_in[...], 1)
    total_weight = weights[slot, 0]
    request_weight = weights[slot, 1]

    @pl.when(total_weight == 0.0)
    def _():
        store_force(force_refs, force_in[...])
        energy_out[...] = energy_in[...]

    @pl.when(total_weight != 0.0)
    def _():
        other = other_ref[...]
        density = own_ref[...] * other
        spectrum = apply_left(x_fwd[...], density)
        for y in range(NY):
            lines[y * NX : (y + 1) * NX, :] = spectrum[:, y * NZ : (y + 1) * NZ]
        for q in range(NX):
            plane = apply_left(y_fwd[...], lines[pl.ds(q, NY, stride=NX), :])
            high, low = split(plane)
            high_rows[q * NY : (q + 1) * NY, :] = high
            low_rows[q * NY : (q + 1) * NY, :] = low
        spectrum = apply_rows(z_fwd[...], high_rows[...], low_rows[...])
        weighted = spectrum * table[...]
        products = jnp.sum(spectrum * weighted, axis=0, keepdims=True)
        folded = products[:, :128]
        for start in range(128, NX * NY, 128):
            folded = folded + products[:, start : start + 128]
        energy_out[...] = energy_in[...] + request_weight * folded
        spectrum = apply_left(z_inv[...], weighted)
        for q in range(NX):
            high, low = split(spectrum[:, q * NY : (q + 1) * NY])
            high_rows[q * NZ : (q + 1) * NZ, :] = high
            low_rows[q * NZ : (q + 1) * NZ, :] = low
        spectrum = apply_rows(y_inv[...], high_rows[...], low_rows[...])
        for q in range(NX):
            lines[q * NY : (q + 1) * NY, :] = spectrum[:, q * NZ : (q + 1) * NZ]
        for y in range(NY):
            field[:, y * NZ : (y + 1) * NZ] = apply_left(
                x_inv[...], lines[pl.ds(y, NX, stride=NY), :]
            )
        store_force(
            force_refs, force_in[...] - (exchange_mix * total_weight) * (field[...] * other)
        )


def pair_step(slot, weights, own, other, tables, force, energy, pieces=1, squares=None):
    if pieces == 1:
        piece = force.shape
        extra = ()
    else:
        planes = NX // pieces
        fold = fold_of(planes, NY * NZ)
        piece = (2 * planes * fold, NY * NZ // fold)
        extra = (squares,)
    outs = [jax.ShapeDtypeStruct(energy.shape, jnp.float32)]
    outs += [jax.ShapeDtypeStruct(piece, jnp.float32)] * pieces
    return pl.pallas_call(
        functools.partial(pair_kernel, slot),
        out_shape=outs,
        in_specs=with_scalar(4 + len(tables) + len(extra)),
        out_specs=in_vmem(1 + pieces),
        scratch_shapes=[
            pltpu.VMEM((NX * NY, NZ), jnp.float32),
            pltpu.VMEM((NX * NY, NZ), jnp.bfloat16),
            pltpu.VMEM((NX * NY, NZ), jnp.bfloat16),
            pltpu.VMEM((NX, NY * NZ), jnp.float32),
        ],
        compiler_params=pltpu.CompilerParams(vmem_limit_bytes=32 << 20),
        cost_estimate=pl.CostEstimate(flops=3 << 30, transcendentals=0, bytes_accessed=3 << 20),
        name="pair_step",
    )(weights, own, other, *tables, force, energy, *extra)


def fold_of(planes, cells):
    return 2 if (2 * planes) % 8 == 0 and cells % 256 == 0 else 1


def in_vmem(count):
    return [pl.BlockSpec(memory_space=pltpu.VMEM)] * count


def with_scalar(count):
    return [pl.BlockSpec(memory_space=pltpu.SMEM)] + in_vmem(count)


def pick(place, choices):
    chosen = choices[0]
    for index in range(1, len(choices)):
        chosen = jnp.where(place == index, choices[index], chosen)
    return chosen


def prepare_kernel(fold, place, orbitals, *out_refs):
    planes, slabs, cells = orbitals.shape
    part = cells // fold
    for f in range(fold):
        rows = slice(f * planes, (f + 1) * planes)
        blocks = [orbitals[:, j, f * part : (f + 1) * part] for j in range(slabs)]
        for r in range(slabs):
            out_refs[r][rows, :] = pick(place[0] ^ r, blocks)


def prepare(place, orbitals):
    planes, slabs, cells = orbitals.shape
    fold = fold_of(planes, cells)
    piece = jax.ShapeDtypeStruct((planes * fold, cells // fold), jnp.float32)
    return pl.pallas_call(
        functools.partial(prepare_kernel, fold),
        out_shape=[piece] * slabs,
        in_specs=with_scalar(1),
        out_specs=in_vmem(slabs),
        compiler_params=pltpu.CompilerParams(vmem_limit_bytes=8 << 20),
        name="prepare",
    )(place, orbitals)


def assemble_kernel(fold, *refs):
    out_ref = refs[-1]
    planes = refs[0].shape[0] // fold
    part = refs[0].shape[1]
    for r, ref in enumerate(refs[:-1]):
        for f in range(fold):
            out_ref[r * planes : (r + 1) * planes, f * part : (f + 1) * part] = ref[
                f * planes : (f + 1) * planes, :
            ]


def assemble(pieces):
    _, part = pieces[0].shape
    fold = NY * NZ // part
    return pl.pallas_call(
        functools.partial(assemble_kernel, fold),
        out_shape=jax.ShapeDtypeStruct((NX, NY * NZ), jnp.float32),
        in_specs=in_vmem(len(pieces)),
        out_specs=in_vmem(1)[0],
        compiler_params=pltpu.CompilerParams(vmem_limit_bytes=8 << 20),
        name="assemble",
    )(*pieces)


def finish_kernel(fold, place, orbitals, local_pot, *refs):
    out_ref = refs[-1]
    planes, slabs, cells = orbitals.shape
    part = cells // fold
    for f in range(fold):
        rows = slice(f * planes, (f + 1) * planes)
        cols = slice(f * part, (f + 1) * part)
        pieces = [ref[rows, :] for ref in refs[:-1]]
        local = local_pot[rows, :]
        for j in range(slabs):
            out_ref[:, j, cols] = local * orbitals[:, j, cols] + pick(place[0] ^ j, pieces)


def finish(place, orbitals, local_pot, pieces):
    planes, _, cells = orbitals.shape
    return pl.pallas_call(
        functools.partial(finish_kernel, fold_of(planes, cells)),
        out_shape=jax.ShapeDtypeStruct(orbitals.shape, jnp.float32),
        in_specs=with_scalar(2 + len(pieces)),
        out_specs=in_vmem(1)[0],
        compiler_params=pltpu.CompilerParams(vmem_limit_bytes=8 << 20),
        name="finish",
    )(place, orbitals, local_pot, *pieces)


def swap(value, axis, reach):
    size = lax.axis_size(axis)
    return lax.ppermute(value, axis, [(i, i ^ reach) for i in range(size)])


def share(value, devices):
    sent = jnp.broadcast_to(value[None], (devices,) + value.shape)
    return lax.all_to_all(sent, ("band", "slab"), 0, 0)


def gather_line(own, band_index, bands):
    place = band_index // 2
    inner = (place == 1) | (place == 2)
    half = own.shape[0] // 2

    def along(value, pairs):
        moves = [(2 * a + side, 2 * b + side) for a, b in pairs for side in (0, 1)]
        return lax.ppermute(value, "band", moves)

    def across_sides(value, places):
        moves = [(i, i ^ 1) for i in range(bands) if i // 2 in places]
        return lax.ppermute(value, "band", moves)

    outer_pairs = [(1, 0), (2, 3)]
    inner_pairs = [(1, 2), (2, 1)]
    places = (0, 1, 2, 3)
    near = along(own, [(0, 1), (1, 0), (2, 3), (3, 2)])
    side_own = across_sides(own, places)
    middle = along(own, inner_pairs)

    outward = along(middle, outer_pairs)
    side_near = across_sides(near, places)
    across = along(near, inner_pairs)

    outer = along(across, outer_pairs)
    second = jnp.where(inner, middle, outward)
    side_late = across_sides(jnp.where(inner, across, outward), places)
    side_middle = along(side_own, inner_pairs)
    third = jnp.where(inner, across, outer)

    side_head = across_sides(outer[:half], (0, 3))
    side_tail = along(side_late[half:], outer_pairs)
    side_last = jnp.where(inner, side_middle, jnp.concatenate([side_head, side_tail], axis=0))

    side = band_index % 2
    near_group = band_index ^ 2
    second_group = jnp.where(place < 2, 2, 1) * 2 + side
    third_group = jnp.where(place < 2, 3, 0) * 2 + side
    late_group = jnp.where(inner, third_group, second_group) ^ 1
    last_group = jnp.where(inner, second_group, third_group) ^ 1
    blocks = [
        (near, near_group),
        (side_own, band_index ^ 1),
        (side_near, near_group ^ 1),
        (second, second_group),
        (third, third_group),
        (side_late, late_group),
        (side_last, last_group),
    ]
    return blocks


def gather_doubling(own, band_index, bands):
    held = [(own, band_index)]
    reach = 1
    while reach < bands:
        held = held + [(swap(block, "band", reach), group ^ reach) for block, group in held]
        reach *= 2
    return held[1:]


def on_line(bands):
    return bands // 2 == 4


def body(orbitals, partners, counts):
    bands = lax.axis_size("band")
    slabs = lax.axis_size("slab")
    band_index = lax.axis_index("band")
    slab_index = lax.axis_index("slab")
    orb_group, planes, _ = orbitals.shape
    total_orbs = orb_group * bands
    assert orb_group == slabs

    place = slab_index.astype(jnp.int32).reshape(1)
    by_plane = jnp.transpose(orbitals, (1, 0, 2))
    sends = prepare(place, by_plane)
    own = assemble([sends[0]] + [swap(sends[r], "slab", r) for r in range(1, slabs)])

    gather = gather_line if on_line(bands) else gather_doubling
    others = gather(own, band_index, bands)

    row = jnp.arange(NX, dtype=jnp.int32)
    held_x = (slab_index ^ (row // planes)) * planes + row % planes
    tables = transform_tables(held_x)

    groups = jnp.stack([group for _, group in others]).astype(jnp.int32)
    active = (slab_index < counts).astype(jnp.float32)
    mine = jnp.arange(bands, dtype=jnp.int32)[:, None] == band_index
    my_partners = jnp.sum(jnp.where(mine, partners, 0), axis=0)
    my_active = jnp.sum(jnp.where(mine, active, 0.0), axis=0)
    requested = jnp.sum(
        jnp.where(groups[:, None] == my_partners[None, :], my_active[None, :], 0.0), axis=1
    )
    wanted_by = jnp.sum(jnp.where(partners == band_index, active, 0.0), axis=1)
    chosen = groups[:, None] == jnp.arange(bands, dtype=jnp.int32)[None, :]
    returned = jnp.sum(jnp.where(chosen, wanted_by[None, :], 0.0), axis=1)
    weights = jnp.stack([requested + returned, requested], axis=1)

    force = jnp.zeros((NX, NY * NZ), jnp.float32)
    energy = jnp.zeros((1, 128), jnp.float32)
    squares = own * own
    for other, _ in others:
        squares = squares + other * other
    for slot, (other, _) in enumerate(others):
        if slot < len(others) - 1:
            energy, force = pair_step(slot, weights, own, other, tables, force, energy)
        else:
            energy, *outgoing = pair_step(
                slot, weights, own, other, tables, force, energy, slabs, squares
            )

    arrived = [outgoing[0]] + [swap(outgoing[r], "slab", r) for r in range(1, slabs)]
    shared = share(energy, bands * slabs)
    rows = arrived[0].shape[0] // 2
    density = 2.0 / total_orbs * sum(piece[rows:] for piece in arrived)
    local_pot = slater_coeff * jnp.cbrt(density)
    forces = finish(place, by_plane, local_pot, arrived)
    energy_total = jnp.sum(shared)
    return (
        jnp.transpose(forces, (1, 0, 2)),
        -energy_total / (2.0 * total_orbs * NX * NY * NZ),
    )


def solution(mesh):
    placed = (P("band", "slab", None), P(), P())
    return jax.shard_map(
        body, mesh=mesh, in_specs=placed, out_specs=(P("band", "slab", None), P()), check_vma=False
    )
```

```python
import functools
import math

import jax
import jax.numpy as jnp
from jax import lax
from jax.experimental import pallas as pl
from jax.experimental.pallas import tpu as pltpu
from jax.sharding import PartitionSpec as P


NX = 48
NY = 48
NZ = 48
NZP = 96


slater_coeff = -((3.0 / math.pi) ** (1.0 / 3.0))
exchange_mix = 0.25
screening = 0.25
row_row = (((1,), (1,)), ((), ()))


def split(value):
    high = value.astype(jnp.bfloat16)
    low = (value - high.astype(jnp.float32)).astype(jnp.bfloat16)
    return high, low


def cas(rows, cols, length):
    phase_angle = 2.0 * math.pi / length * (rows * cols % length).astype(jnp.float32)
    return jnp.cos(phase_angle) + jnp.sin(phase_angle)


def split_table(matrix):
    high = lax.reduce_precision(matrix, 8, 7)
    return high.astype(jnp.bfloat16), (matrix - high).astype(jnp.bfloat16)


def wide(matrix):
    high, low = split_table(matrix)
    return jnp.concatenate([high, high, low], axis=1)


def tall(matrix):
    high, low = split_table(matrix)
    return jnp.concatenate([high, low], axis=0)


def wavenumber_sq(length):
    position = jnp.arange(length, dtype=jnp.int32)
    signed = jnp.where(position > length // 2, position - length, position).astype(jnp.float32)
    wave_number = 2.0 * math.pi / length * signed
    return wave_number * wave_number


def transform_tables(held_x):
    x_waves = jnp.arange(NX, dtype=jnp.int32)
    y_cells = jnp.arange(NY, dtype=jnp.int32)
    z_cells = jnp.arange(NZ, dtype=jnp.int32)
    z_waves = jnp.arange(NZP, dtype=jnp.int32)
    total = (
        wavenumber_sq(NZP)[:, None, None]
        + wavenumber_sq(NX)[None, :, None]
        + wavenumber_sq(NY)[None, None, :]
    )
    kernel_table = 4.0 * math.pi / (NX * NY * NZP) / (total + screening * screening)
    y_matrix = cas(y_cells[:, None], y_cells[None, :], NY)
    return (
        wide(cas(x_waves[:, None], held_x[None, :], NX)),
        wide(y_matrix),
        tall(cas(z_waves[:, None], z_cells[None, :], NZP)),
        kernel_table.reshape(NZP, NX * NY),
        wide(cas(z_cells[:, None], z_waves[None, :], NZP)),
        tall(y_matrix),
        wide(cas(held_x[:, None], x_waves[None, :], NX)),
    )


def apply_left(matrix, value):
    high, low = split(value)
    stacked = jnp.concatenate([high, low, high], axis=0)
    return jnp.dot(matrix, stacked, preferred_element_type=jnp.float32)


def apply_rows(matrix, high, low):
    half = matrix.shape[0] // 2
    both = lax.dot_general(matrix, high, row_row, preferred_element_type=jnp.float32)
    rest = lax.dot_general(matrix[:half], low, row_row, preferred_element_type=jnp.float32)
    return both[:half] + both[half:] + rest


def cut_into(refs, value, part_index):
    planes = NX // len(refs)
    part = refs[0].shape[1]
    fold = NY * NZ // part
    first = part_index * planes * fold
    for r, ref in enumerate(refs):
        for f in range(fold):
            ref[first + f * planes : first + (f + 1) * planes, :] = value[
                r * planes : (r + 1) * planes, f * part : (f + 1) * part
            ]


def store_force(force_refs, value):
    if len(force_refs) == 1:
        force_refs[0][...] = value
    else:
        cut_into(force_refs, value, 0)


def pair_kernel(
    slot, weights, own_ref, other_ref, x_fwd, y_fwd, z_fwd, table, z_inv, y_inv, x_inv,
    force_in, energy_in, *refs,
):
    *refs, lines, high_rows, low_rows, field = refs
    if len(refs) == 2:
        energy_out, *force_refs = refs
    else:
        squares_in, energy_out, *force_refs = refs
        cut_into(force_refs, squares_in[...], 1)
    total_weight = weights[slot, 0]
    request_weight = weights[slot, 1]

    @pl.when(total_weight == 0.0)
    def _():
        energy_out[...] = energy_in[...]
        if len(force_refs) > 1:
            store_force(force_refs, force_in[...])

    @pl.when(total_weight != 0.0)
    def _():
        other = other_ref[...]
        density = own_ref[...] * other
        spectrum = apply_left(x_fwd[...], density)
        for y in range(NY):
            lines[y * NX : (y + 1) * NX, :] = spectrum[:, y * NZ : (y + 1) * NZ]
        for q in range(NX):
            plane = apply_left(y_fwd[...], lines[pl.ds(q, NY, stride=NX), :])
            high, low = split(plane)
            high_rows[q * NY : (q + 1) * NY, :] = high
            low_rows[q * NY : (q + 1) * NY, :] = low
        spectrum = apply_rows(z_fwd[...], high_rows[...], low_rows[...])
        weighted = spectrum * table[...]
        products = jnp.sum(spectrum * weighted, axis=0, keepdims=True)
        folded = products[:, :128]
        for start in range(128, NX * NY, 128):
            folded = folded + products[:, start : start + 128]
        energy_out[...] = energy_in[...] + request_weight * folded
        spectrum = apply_left(z_inv[...], weighted)
        for q in range(NX):
            high, low = split(spectrum[:, q * NY : (q + 1) * NY])
            high_rows[q * NZ : (q + 1) * NZ, :] = high
            low_rows[q * NZ : (q + 1) * NZ, :] = low
        spectrum = apply_rows(y_inv[...], high_rows[...], low_rows[...])
        for q in range(NX):
            lines[q * NY : (q + 1) * NY, :] = spectrum[:, q * NZ : (q + 1) * NZ]
        for y in range(NY):
            field[:, y * NZ : (y + 1) * NZ] = apply_left(
                x_inv[...], lines[pl.ds(y, NX, stride=NY), :]
            )
        store_force(
            force_refs, force_in[...] - (exchange_mix * total_weight) * (field[...] * other)
        )


def pair_step(slot, weights, own, other, tables, force, energy, pieces=1, squares=None):
    if pieces == 1:
        piece = force.shape
        extra = ()
    else:
        planes = NX // pieces
        fold = fold_of(planes, NY * NZ)
        piece = (2 * planes * fold, NY * NZ // fold)
        extra = (squares,)
    outs = [jax.ShapeDtypeStruct(energy.shape, jnp.float32)]
    outs += [jax.ShapeDtypeStruct(piece, jnp.float32)] * pieces
    return pl.pallas_call(
        functools.partial(pair_kernel, slot),
        out_shape=outs,
        in_specs=with_scalar(4 + len(tables) + len(extra)),
        out_specs=in_vmem(1 + pieces),
        scratch_shapes=[
            pltpu.VMEM((NX * NY, NZ), jnp.float32),
            pltpu.VMEM((NX * NY, NZ), jnp.bfloat16),
            pltpu.VMEM((NX * NY, NZ), jnp.bfloat16),
            pltpu.VMEM((NX, NY * NZ), jnp.float32),
        ],
        input_output_aliases={3 + len(tables): 1} if pieces == 1 else {},
        compiler_params=pltpu.CompilerParams(vmem_limit_bytes=32 << 20),
        cost_estimate=pl.CostEstimate(flops=3 << 30, transcendentals=0, bytes_accessed=3 << 20),
        name="pair_step",
    )(weights, own, other, *tables, force, energy, *extra)


def fold_of(planes, cells):
    return 2 if (2 * planes) % 8 == 0 and cells % 256 == 0 else 1


def in_vmem(count):
    return [pl.BlockSpec(memory_space=pltpu.VMEM)] * count


def with_scalar(count):
    return [pl.BlockSpec(memory_space=pltpu.SMEM)] + in_vmem(count)


def pick(place, choices):
    chosen = choices[0]
    for index in range(1, len(choices)):
        chosen = jnp.where(place == index, choices[index], chosen)
    return chosen


def prepare_kernel(fold, place, orbitals, *out_refs):
    planes, slabs, cells = orbitals.shape
    part = cells // fold
    for f in range(fold):
        rows = slice(f * planes, (f + 1) * planes)
        blocks = [orbitals[:, j, f * part : (f + 1) * part] for j in range(slabs)]
        for r in range(slabs):
            out_refs[r][rows, :] = pick(place[0] ^ r, blocks)


def prepare(place, orbitals):
    planes, slabs, cells = orbitals.shape
    fold = fold_of(planes, cells)
    piece = jax.ShapeDtypeStruct((planes * fold, cells // fold), jnp.float32)
    return pl.pallas_call(
        functools.partial(prepare_kernel, fold),
        out_shape=[piece] * slabs,
        in_specs=with_scalar(1),
        out_specs=in_vmem(slabs),
        compiler_params=pltpu.CompilerParams(vmem_limit_bytes=8 << 20),
        name="prepare",
    )(place, orbitals)


def assemble_kernel(fold, *refs):
    out_ref = refs[-1]
    planes = refs[0].shape[0] // fold
    part = refs[0].shape[1]
    for r, ref in enumerate(refs[:-1]):
        for f in range(fold):
            out_ref[r * planes : (r + 1) * planes, f * part : (f + 1) * part] = ref[
                f * planes : (f + 1) * planes, :
            ]


def assemble(pieces):
    _, part = pieces[0].shape
    fold = NY * NZ // part
    return pl.pallas_call(
        functools.partial(assemble_kernel, fold),
        out_shape=jax.ShapeDtypeStruct((NX, NY * NZ), jnp.float32),
        in_specs=in_vmem(len(pieces)),
        out_specs=in_vmem(1)[0],
        compiler_params=pltpu.CompilerParams(vmem_limit_bytes=8 << 20),
        name="assemble",
    )(*pieces)


def finish_kernel(fold, place, orbitals, local_pot, *refs):
    out_ref = refs[-1]
    planes, slabs, cells = orbitals.shape
    part = cells // fold
    for f in range(fold):
        rows = slice(f * planes, (f + 1) * planes)
        cols = slice(f * part, (f + 1) * part)
        pieces = [ref[rows, :] for ref in refs[:-1]]
        local = local_pot[rows, :]
        for j in range(slabs):
            out_ref[:, j, cols] = local * orbitals[:, j, cols] + pick(place[0] ^ j, pieces)


def finish(place, orbitals, local_pot, pieces):
    planes, _, cells = orbitals.shape
    return pl.pallas_call(
        functools.partial(finish_kernel, fold_of(planes, cells)),
        out_shape=jax.ShapeDtypeStruct(orbitals.shape, jnp.float32),
        in_specs=with_scalar(2 + len(pieces)),
        out_specs=in_vmem(1)[0],
        compiler_params=pltpu.CompilerParams(vmem_limit_bytes=8 << 20),
        name="finish",
    )(place, orbitals, local_pot, *pieces)


def swap(value, axis, reach):
    size = lax.axis_size(axis)
    return lax.ppermute(value, axis, [(i, i ^ reach) for i in range(size)])


def share(value, devices):
    sent = jnp.broadcast_to(value[None], (devices,) + value.shape)
    return lax.all_to_all(sent, ("band", "slab"), 0, 0)


def gather_line(own, band_index, bands):
    place = band_index // 2
    inner = (place == 1) | (place == 2)
    half = own.shape[0] // 2

    def along(value, pairs):
        moves = [(2 * a + side, 2 * b + side) for a, b in pairs for side in (0, 1)]
        return lax.ppermute(value, "band", moves)

    def across_sides(value, places):
        moves = [(i, i ^ 1) for i in range(bands) if i // 2 in places]
        return lax.ppermute(value, "band", moves)

    outer_pairs = [(1, 0), (2, 3)]
    inner_pairs = [(1, 2), (2, 1)]
    places = (0, 1, 2, 3)
    middle = along(own, inner_pairs)
    near = along(own, [(0, 1), (1, 0), (2, 3), (3, 2)])
    side_own = across_sides(own, places)

    across = along(near, inner_pairs)
    outward = along(middle, outer_pairs)
    side_near = across_sides(near, places)

    second = jnp.where(inner, middle, outward)
    second, outward = lax.optimization_barrier((second, outward))
    late = jnp.where(inner, across, outward)
    outer = along(across, outer_pairs)
    side_late = across_sides(late, places)
    side_middle = along(side_own, inner_pairs)
    late, outer = lax.optimization_barrier((late, outer))
    third = lax.optimization_barrier(jnp.where(inner, across, outer))

    side_head = across_sides(outer[:half], (0, 3))
    side_tail = along(side_late[half:], outer_pairs)
    side_last = jnp.where(inner, side_middle, jnp.concatenate([side_head, side_tail], axis=0))

    side = band_index % 2
    near_group = band_index ^ 2
    second_group = jnp.where(place < 2, 2, 1) * 2 + side
    third_group = jnp.where(place < 2, 3, 0) * 2 + side
    late_group = jnp.where(inner, third_group, second_group) ^ 1
    last_group = jnp.where(inner, second_group, third_group) ^ 1
    blocks = [
        (near, near_group),
        (side_own, band_index ^ 1),
        (side_near, near_group ^ 1),
        (second, second_group),
        (third, third_group),
        (side_late, late_group),
        (side_last, last_group),
    ]
    return blocks


def gather_doubling(own, band_index, bands):
    held = [(own, band_index)]
    reach = 1
    while reach < bands:
        held = held + [(swap(block, "band", reach), group ^ reach) for block, group in held]
        reach *= 2
    return held[1:]


def on_line(bands):
    return bands // 2 == 4


def body(orbitals, partners, counts):
    bands = lax.axis_size("band")
    slabs = lax.axis_size("slab")
    band_index = lax.axis_index("band")
    slab_index = lax.axis_index("slab")
    orb_group, planes, _ = orbitals.shape
    total_orbs = orb_group * bands
    assert orb_group == slabs

    place = slab_index.astype(jnp.int32).reshape(1)
    by_plane = jnp.transpose(orbitals, (1, 0, 2))
    sends = prepare(place, by_plane)
    own = assemble([sends[0]] + [swap(sends[r], "slab", r) for r in range(1, slabs)])

    gather = gather_line if on_line(bands) else gather_doubling
    others = gather(own, band_index, bands)

    row = jnp.arange(NX, dtype=jnp.int32)
    held_x = (slab_index ^ (row // planes)) * planes + row % planes
    tables = transform_tables(held_x)

    groups = jnp.stack([group for _, group in others]).astype(jnp.int32)
    active = (slab_index < counts).astype(jnp.float32)
    mine = jnp.arange(bands, dtype=jnp.int32)[:, None] == band_index
    my_partners = jnp.sum(jnp.where(mine, partners, 0), axis=0)
    my_active = jnp.sum(jnp.where(mine, active, 0.0), axis=0)
    requested = jnp.sum(
        jnp.where(groups[:, None] == my_partners[None, :], my_active[None, :], 0.0), axis=1
    )
    wanted_by = jnp.sum(jnp.where(partners == band_index, active, 0.0), axis=1)
    chosen = groups[:, None] == jnp.arange(bands, dtype=jnp.int32)[None, :]
    returned = jnp.sum(jnp.where(chosen, wanted_by[None, :], 0.0), axis=1)
    weights = jnp.stack([requested + returned, requested], axis=1)

    force = jnp.zeros((NX, NY * NZ), jnp.float32)
    energy = jnp.zeros((1, 128), jnp.float32)
    squares = own * own
    for other, _ in others:
        squares = squares + other * other
    for slot, (other, _) in enumerate(others):
        if slot < len(others) - 1:
            energy, force = pair_step(slot, weights, own, other, tables, force, energy)
        else:
            energy, *outgoing = pair_step(
                slot, weights, own, other, tables, force, energy, slabs, squares
            )

    arrived = [outgoing[0]] + [swap(outgoing[r], "slab", r) for r in range(1, slabs)]
    shared = share(energy, bands * slabs)
    rows = arrived[0].shape[0] // 2
    density = 2.0 / total_orbs * sum(piece[rows:] for piece in arrived)
    local_pot = slater_coeff * jnp.cbrt(density)
    forces = finish(place, by_plane, local_pot, arrived)
    energy_total = jnp.sum(shared)
    return (
        jnp.transpose(forces, (1, 0, 2)),
        -energy_total / (2.0 * total_orbs * NX * NY * NZ),
    )


def solution(mesh):
    placed = (P("band", "slab", None), P(), P())
    return jax.shard_map(
        body, mesh=mesh, in_specs=placed, out_specs=(P("band", "slab", None), P()), check_vma=False
    )
```

```python
import functools
import math

import jax
import jax.numpy as jnp
from jax import lax
from jax.experimental import pallas as pl
from jax.experimental.pallas import tpu as pltpu
from jax.sharding import PartitionSpec as P


NX = 48
NY = 48
NZ = 48
NZP = 96


slater_coeff = -((3.0 / math.pi) ** (1.0 / 3.0))
exchange_mix = 0.25
screening = 0.25
row_row = (((1,), (1,)), ((), ()))


def split(value):
    high = value.astype(jnp.bfloat16)
    low = (value - high.astype(jnp.float32)).astype(jnp.bfloat16)
    return high, low


def cas(rows, cols, length):
    phase_angle = 2.0 * math.pi / length * (rows * cols % length).astype(jnp.float32)
    return jnp.cos(phase_angle) + jnp.sin(phase_angle)


def split_table(matrix):
    high = lax.reduce_precision(matrix, 8, 7)
    return high.astype(jnp.bfloat16), (matrix - high).astype(jnp.bfloat16)


def wide(matrix):
    high, low = split_table(matrix)
    return jnp.concatenate([high, high, low], axis=1)


def tall(matrix):
    high, low = split_table(matrix)
    return jnp.concatenate([high, low], axis=0)


def wavenumber_sq(length):
    position = jnp.arange(length, dtype=jnp.int32)
    signed = jnp.where(position > length // 2, position - length, position).astype(jnp.float32)
    wave_number = 2.0 * math.pi / length * signed
    return wave_number * wave_number


def transform_tables(held_x):
    x_waves = jnp.arange(NX, dtype=jnp.int32)
    y_cells = jnp.arange(NY, dtype=jnp.int32)
    z_cells = jnp.arange(NZ, dtype=jnp.int32)
    z_waves = jnp.arange(NZP, dtype=jnp.int32)
    total = (
        wavenumber_sq(NZP)[:, None, None]
        + wavenumber_sq(NX)[None, :, None]
        + wavenumber_sq(NY)[None, None, :]
    )
    kernel_table = 4.0 * math.pi / (NX * NY * NZP) / (total + screening * screening)
    y_matrix = cas(y_cells[:, None], y_cells[None, :], NY)
    return (
        wide(cas(x_waves[:, None], held_x[None, :], NX)),
        wide(y_matrix),
        tall(cas(z_waves[:, None], z_cells[None, :], NZP)),
        kernel_table.reshape(NZP, NX * NY),
        wide(cas(z_cells[:, None], z_waves[None, :], NZP)),
        tall(y_matrix),
        wide(cas(held_x[:, None], x_waves[None, :], NX)),
    )


def apply_left(matrix, value):
    high, low = split(value)
    stacked = jnp.concatenate([high, low, high], axis=0)
    return jnp.dot(matrix, stacked, preferred_element_type=jnp.float32)


def apply_rows(matrix, high, low):
    half = matrix.shape[0] // 2
    both = lax.dot_general(matrix, high, row_row, preferred_element_type=jnp.float32)
    rest = lax.dot_general(matrix[:half], low, row_row, preferred_element_type=jnp.float32)
    return both[:half] + both[half:] + rest


def cut_into(refs, value, part_index):
    planes = NX // len(refs)
    part = refs[0].shape[1]
    fold = NY * NZ // part
    first = part_index * planes * fold
    for r, ref in enumerate(refs):
        for f in range(fold):
            ref[first + f * planes : first + (f + 1) * planes, :] = value[
                r * planes : (r + 1) * planes, f * part : (f + 1) * part
            ]


def store_force(force_refs, value):
    if len(force_refs) == 1:
        force_refs[0][...] = value
    else:
        cut_into(force_refs, value, 0)


def pair_kernel(
    slot, weights, own_ref, other_ref, x_fwd, y_fwd, z_fwd, table, z_inv, y_inv, x_inv,
    force_in, energy_in, *refs,
):
    *refs, lines, high_rows, low_rows, field = refs
    if len(refs) == 2:
        energy_out, *force_refs = refs
    else:
        squares_in, energy_out, *force_refs = refs
        cut_into(force_refs, squares_in[...], 1)
    total_weight = jnp.max(weights[2 * slot : 2 * slot + 1, :])
    request_weight = weights[2 * slot + 1 : 2 * slot + 2, :]

    @pl.when(total_weight == 0.0)
    def _():
        energy_out[...] = energy_in[...]
        if len(force_refs) > 1:
            store_force(force_refs, force_in[...])

    @pl.when(total_weight != 0.0)
    def _():
        other = other_ref[...]
        density = own_ref[...] * other
        spectrum = apply_left(x_fwd[...], density)
        for y in range(NY):
            lines[y * NX : (y + 1) * NX, :] = spectrum[:, y * NZ : (y + 1) * NZ]
        for q in range(NX):
            plane = apply_left(y_fwd[...], lines[pl.ds(q, NY, stride=NX), :])
            high, low = split(plane)
            high_rows[q * NY : (q + 1) * NY, :] = high
            low_rows[q * NY : (q + 1) * NY, :] = low
        spectrum = apply_rows(z_fwd[...], high_rows[...], low_rows[...])
        weighted = spectrum * table[...]
        products = jnp.sum(spectrum * weighted, axis=0, keepdims=True)
        folded = products[:, :128]
        for start in range(128, NX * NY, 128):
            folded = folded + products[:, start : start + 128]
        energy_out[...] = energy_in[...] + request_weight * folded
        spectrum = apply_left(z_inv[...], weighted)
        for q in range(NX):
            high, low = split(spectrum[:, q * NY : (q + 1) * NY])
            high_rows[q * NZ : (q + 1) * NZ, :] = high
            low_rows[q * NZ : (q + 1) * NZ, :] = low
        spectrum = apply_rows(y_inv[...], high_rows[...], low_rows[...])
        for q in range(NX):
            lines[q * NY : (q + 1) * NY, :] = spectrum[:, q * NZ : (q + 1) * NZ]
        for y in range(NY):
            field[:, y * NZ : (y + 1) * NZ] = apply_left(
                x_inv[...], lines[pl.ds(y, NX, stride=NY), :]
            )
        store_force(
            force_refs, force_in[...] - (exchange_mix * total_weight) * (field[...] * other)
        )


def pair_step(slot, weights, own, other, tables, force, energy, pieces=1, squares=None):
    if pieces == 1:
        piece = force.shape
        extra = ()
    else:
        planes = NX // pieces
        fold = fold_of(planes, NY * NZ)
        piece = (2 * planes * fold, NY * NZ // fold)
        extra = (squares,)
    outs = [jax.ShapeDtypeStruct(energy.shape, jnp.float32)]
    outs += [jax.ShapeDtypeStruct(piece, jnp.float32)] * pieces
    return pl.pallas_call(
        functools.partial(pair_kernel, slot),
        out_shape=outs,
        in_specs=in_vmem(5 + len(tables) + len(extra)),
        out_specs=in_vmem(1 + pieces),
        scratch_shapes=[
            pltpu.VMEM((NX * NY, NZ), jnp.float32),
            pltpu.VMEM((NX * NY, NZ), jnp.bfloat16),
            pltpu.VMEM((NX * NY, NZ), jnp.bfloat16),
            pltpu.VMEM((NX, NY * NZ), jnp.float32),
        ],
        input_output_aliases={3 + len(tables): 1} if pieces == 1 else {},
        compiler_params=pltpu.CompilerParams(vmem_limit_bytes=32 << 20),
        cost_estimate=pl.CostEstimate(flops=3 << 30, transcendentals=0, bytes_accessed=3 << 20),
        name="pair_step",
    )(weights, own, other, *tables, force, energy, *extra)


def fold_of(planes, cells):
    return 2 if (2 * planes) % 8 == 0 and cells % 256 == 0 else 1


def in_vmem(count):
    return [pl.BlockSpec(memory_space=pltpu.VMEM)] * count


def with_scalar(count):
    return [pl.BlockSpec(memory_space=pltpu.SMEM)] + in_vmem(count)


def pick(place, choices):
    chosen = choices[0]
    for index in range(1, len(choices)):
        chosen = jnp.where(place == index, choices[index], chosen)
    return chosen


def prepare_kernel(fold, place, orbitals, *out_refs):
    planes, slabs, cells = orbitals.shape
    part = cells // fold
    for f in range(fold):
        rows = slice(f * planes, (f + 1) * planes)
        blocks = [orbitals[:, j, f * part : (f + 1) * part] for j in range(slabs)]
        for r in range(slabs):
            out_refs[r][rows, :] = pick(place[0] ^ r, blocks)


def prepare(place, orbitals):
    planes, slabs, cells = orbitals.shape
    fold = fold_of(planes, cells)
    piece = jax.ShapeDtypeStruct((planes * fold, cells // fold), jnp.float32)
    return pl.pallas_call(
        functools.partial(prepare_kernel, fold),
        out_shape=[piece] * slabs,
        in_specs=with_scalar(1),
        out_specs=in_vmem(slabs),
        compiler_params=pltpu.CompilerParams(vmem_limit_bytes=8 << 20),
        name="prepare",
    )(place, orbitals)


def assemble_kernel(fold, *refs):
    out_ref = refs[-1]
    planes = refs[0].shape[0] // fold
    part = refs[0].shape[1]
    for r, ref in enumerate(refs[:-1]):
        for f in range(fold):
            out_ref[r * planes : (r + 1) * planes, f * part : (f + 1) * part] = ref[
                f * planes : (f + 1) * planes, :
            ]


def assemble(pieces):
    _, part = pieces[0].shape
    fold = NY * NZ // part
    return pl.pallas_call(
        functools.partial(assemble_kernel, fold),
        out_shape=jax.ShapeDtypeStruct((NX, NY * NZ), jnp.float32),
        in_specs=in_vmem(len(pieces)),
        out_specs=in_vmem(1)[0],
        compiler_params=pltpu.CompilerParams(vmem_limit_bytes=8 << 20),
        name="assemble",
    )(*pieces)


def finish_kernel(fold, place, orbitals, local_pot, *refs):
    out_ref = refs[-1]
    planes, slabs, cells = orbitals.shape
    part = cells // fold
    for f in range(fold):
        rows = slice(f * planes, (f + 1) * planes)
        cols = slice(f * part, (f + 1) * part)
        pieces = [ref[rows, :] for ref in refs[:-1]]
        local = local_pot[rows, :]
        for j in range(slabs):
            out_ref[:, j, cols] = local * orbitals[:, j, cols] + pick(place[0] ^ j, pieces)


def finish(place, orbitals, local_pot, pieces):
    planes, _, cells = orbitals.shape
    return pl.pallas_call(
        functools.partial(finish_kernel, fold_of(planes, cells)),
        out_shape=jax.ShapeDtypeStruct(orbitals.shape, jnp.float32),
        in_specs=with_scalar(2 + len(pieces)),
        out_specs=in_vmem(1)[0],
        compiler_params=pltpu.CompilerParams(vmem_limit_bytes=8 << 20),
        name="finish",
    )(place, orbitals, local_pot, *pieces)


def swap(value, axis, reach):
    size = lax.axis_size(axis)
    return lax.ppermute(value, axis, [(i, i ^ reach) for i in range(size)])


def share(value, devices):
    sent = jnp.broadcast_to(value[None], (devices,) + value.shape)
    return lax.all_to_all(sent, ("band", "slab"), 0, 0)


def gather_line(own, band_index, bands):
    place = band_index // 2
    inner = (place == 1) | (place == 2)
    half = own.shape[0] // 2

    def along(value, pairs):
        moves = [(2 * a + side, 2 * b + side) for a, b in pairs for side in (0, 1)]
        return lax.ppermute(value, "band", moves)

    def across_sides(value, places):
        moves = [(i, i ^ 1) for i in range(bands) if i // 2 in places]
        return lax.ppermute(value, "band", moves)

    outer_pairs = [(1, 0), (2, 3)]
    inner_pairs = [(1, 2), (2, 1)]
    places = (0, 1, 2, 3)
    middle = along(own, inner_pairs)
    near = along(own, [(0, 1), (1, 0), (2, 3), (3, 2)])
    side_own = across_sides(own, places)

    across = along(near, inner_pairs)
    outward = along(middle, outer_pairs)
    side_near = across_sides(near, places)

    second = jnp.where(inner, middle, outward)
    second, outward = lax.optimization_barrier((second, outward))
    late = jnp.where(inner, across, outward)
    outer = along(across, outer_pairs)
    side_late = across_sides(late, places)
    side_middle = along(side_own, inner_pairs)
    late, outer = lax.optimization_barrier((late, outer))
    third = lax.optimization_barrier(jnp.where(inner, across, outer))

    side_head = across_sides(outer[:half], (0, 3))
    side_tail = along(side_late[half:], outer_pairs)
    side_last = jnp.where(inner, side_middle, jnp.concatenate([side_head, side_tail], axis=0))

    side = band_index % 2
    near_group = band_index ^ 2
    second_group = jnp.where(place < 2, 2, 1) * 2 + side
    third_group = jnp.where(place < 2, 3, 0) * 2 + side
    late_group = jnp.where(inner, third_group, second_group) ^ 1
    last_group = jnp.where(inner, second_group, third_group) ^ 1
    blocks = [
        (near, near_group),
        (side_own, band_index ^ 1),
        (side_near, near_group ^ 1),
        (second, second_group),
        (third, third_group),
        (side_late, late_group),
        (side_last, last_group),
    ]
    return blocks


def gather_doubling(own, band_index, bands):
    held = [(own, band_index)]
    reach = 1
    while reach < bands:
        held = held + [(swap(block, "band", reach), group ^ reach) for block, group in held]
        reach *= 2
    return held[1:]


def on_line(bands):
    return bands // 2 == 4


def body(orbitals, partners, counts):
    bands = lax.axis_size("band")
    slabs = lax.axis_size("slab")
    band_index = lax.axis_index("band")
    slab_index = lax.axis_index("slab")
    orb_group, planes, _ = orbitals.shape
    total_orbs = orb_group * bands
    assert orb_group == slabs

    place = slab_index.astype(jnp.int32).reshape(1)
    by_plane = jnp.transpose(orbitals, (1, 0, 2))
    sends = prepare(place, by_plane)
    own = assemble([sends[0]] + [swap(sends[r], "slab", r) for r in range(1, slabs)])

    gather = gather_line if on_line(bands) else gather_doubling
    others = gather(own, band_index, bands)

    row = jnp.arange(NX, dtype=jnp.int32)
    held_x = (slab_index ^ (row // planes)) * planes + row % planes
    tables = transform_tables(held_x)

    groups = jnp.stack([group for _, group in others]).astype(jnp.int32)
    active = (slab_index < counts).astype(jnp.float32)
    mine = jnp.arange(bands, dtype=jnp.int32)[:, None] == band_index
    my_partners = jnp.sum(jnp.where(mine, partners, 0), axis=0)
    my_active = jnp.sum(jnp.where(mine, active, 0.0), axis=0)
    requested = jnp.sum(
        jnp.where(groups[:, None] == my_partners[None, :], my_active[None, :], 0.0), axis=1
    )
    wanted_by = jnp.sum(jnp.where(partners == band_index, active, 0.0), axis=1)
    chosen = groups[:, None] == jnp.arange(bands, dtype=jnp.int32)[None, :]
    returned = jnp.sum(jnp.where(chosen, wanted_by[None, :], 0.0), axis=1)
    weights = jnp.stack([requested + returned, requested], axis=1).reshape(-1)
    weights = jnp.broadcast_to(weights[:, None], weights.shape + (128,))

    force = jnp.zeros((NX, NY * NZ), jnp.float32)
    energy = jnp.zeros((1, 128), jnp.float32)
    squares = own * own
    for other, _ in others:
        squares = squares + other * other
    for slot, (other, _) in enumerate(others):
        if slot < len(others) - 1:
            energy, force = pair_step(slot, weights, own, other, tables, force, energy)
        else:
            energy, *outgoing = pair_step(
                slot, weights, own, other, tables, force, energy, slabs, squares
            )

    arrived = [outgoing[0]] + [swap(outgoing[r], "slab", r) for r in range(1, slabs)]
    shared = share(energy, bands * slabs)
    rows = arrived[0].shape[0] // 2
    density = 2.0 / total_orbs * sum(piece[rows:] for piece in arrived)
    local_pot = slater_coeff * jnp.cbrt(density)
    forces = finish(place, by_plane, local_pot, arrived)
    energy_total = jnp.sum(shared)
    return (
        jnp.transpose(forces, (1, 0, 2)),
        -energy_total / (2.0 * total_orbs * NX * NY * NZ),
    )


def solution(mesh):
    placed = (P("band", "slab", None), P(), P())
    return jax.shard_map(
        body, mesh=mesh, in_specs=placed, out_specs=(P("band", "slab", None), P()), check_vma=False
    )
```

```python
import functools
import math

import jax
import jax.numpy as jnp
from jax import lax
from jax.experimental import pallas as pl
from jax.experimental.pallas import tpu as pltpu
from jax.sharding import PartitionSpec as P


NX = 48
NY = 48
NZ = 48
NZP = 96


slater_coeff = -((3.0 / math.pi) ** (1.0 / 3.0))
exchange_mix = 0.25
screening = 0.25
row_row = (((1,), (1,)), ((), ()))


def split(value):
    high = value.astype(jnp.bfloat16)
    low = (value - high.astype(jnp.float32)).astype(jnp.bfloat16)
    return high, low


def cas(rows, cols, length):
    phase_angle = 2.0 * math.pi / length * (rows * cols % length).astype(jnp.float32)
    return jnp.cos(phase_angle) + jnp.sin(phase_angle)


def split_table(matrix):
    high = lax.reduce_precision(matrix, 8, 7)
    return high.astype(jnp.bfloat16), (matrix - high).astype(jnp.bfloat16)


def wide(matrix):
    high, low = split_table(matrix)
    return jnp.concatenate([high, high, low], axis=1)


def tall(matrix):
    high, low = split_table(matrix)
    return jnp.concatenate([high, low], axis=0)


def wavenumber_sq(length):
    position = jnp.arange(length, dtype=jnp.int32)
    signed = jnp.where(position > length // 2, position - length, position).astype(jnp.float32)
    wave_number = 2.0 * math.pi / length * signed
    return wave_number * wave_number


def transform_tables(held_x):
    x_waves = jnp.arange(NX, dtype=jnp.int32)
    y_cells = jnp.arange(NY, dtype=jnp.int32)
    z_cells = jnp.arange(NZ, dtype=jnp.int32)
    z_waves = jnp.arange(NZP, dtype=jnp.int32)
    total = (
        wavenumber_sq(NZP)[:, None, None]
        + wavenumber_sq(NX)[None, :, None]
        + wavenumber_sq(NY)[None, None, :]
    )
    kernel_table = 4.0 * math.pi / (NX * NY * NZP) / (total + screening * screening)
    y_matrix = cas(y_cells[:, None], y_cells[None, :], NY)
    return (
        wide(cas(x_waves[:, None], held_x[None, :], NX)),
        wide(y_matrix),
        tall(cas(z_waves[:, None], z_cells[None, :], NZP)),
        kernel_table.reshape(NZP, NX * NY),
        wide(cas(z_cells[:, None], z_waves[None, :], NZP)),
        tall(y_matrix),
        wide(cas(held_x[:, None], x_waves[None, :], NX)),
    )


def apply_left(matrix, value):
    high, low = split(value)
    stacked = jnp.concatenate([high, low, high], axis=0)
    return jnp.dot(matrix, stacked, preferred_element_type=jnp.float32)


def apply_rows(matrix, high, low):
    half = matrix.shape[0] // 2
    both = lax.dot_general(matrix, high, row_row, preferred_element_type=jnp.float32)
    rest = lax.dot_general(matrix[:half], low, row_row, preferred_element_type=jnp.float32)
    return both[:half] + both[half:] + rest


def cut_into(refs, value, part_index):
    planes = NX // len(refs)
    part = refs[0].shape[1]
    fold = NY * NZ // part
    first = part_index * planes * fold
    for r, ref in enumerate(refs):
        for f in range(fold):
            ref[first + f * planes : first + (f + 1) * planes, :] = value[
                r * planes : (r + 1) * planes, f * part : (f + 1) * part
            ]


def store_force(force_refs, value):
    if len(force_refs) == 1:
        force_refs[0][...] = value
    else:
        cut_into(force_refs, value, 0)


def pair_kernel(
    slot, weights, own_ref, other_ref, x_fwd, y_fwd, z_fwd, table, z_inv, y_inv, x_inv,
    force_in, energy_in, *refs,
):
    *refs, lines, high_rows, low_rows, field = refs
    if len(refs) == 2:
        energy_out, *force_refs = refs
    else:
        squares_in, energy_out, *force_refs = refs
        cut_into(force_refs, squares_in[...], 1)
    total_weight = jnp.max(weights[2 * slot : 2 * slot + 1, :])
    request_weight = weights[2 * slot + 1 : 2 * slot + 2, :]

    @pl.when(total_weight == 0.0)
    def _():
        energy_out[...] = energy_in[...]
        if len(force_refs) > 1:
            store_force(force_refs, force_in[...])

    @pl.when(total_weight != 0.0)
    def _():
        other = other_ref[...]
        density = own_ref[...] * other
        spectrum = apply_left(x_fwd[...], density)
        for y in range(NY):
            lines[y * NX : (y + 1) * NX, :] = spectrum[:, y * NZ : (y + 1) * NZ]
        for q in range(NX):
            plane = apply_left(y_fwd[...], lines[pl.ds(q, NY, stride=NX), :])
            high, low = split(plane)
            high_rows[q * NY : (q + 1) * NY, :] = high
            low_rows[q * NY : (q + 1) * NY, :] = low
        spectrum = apply_rows(z_fwd[...], high_rows[...], low_rows[...])
        weighted = spectrum * table[...]
        products = jnp.sum(spectrum * weighted, axis=0, keepdims=True)
        folded = products[:, :128]
        for start in range(128, NX * NY, 128):
            folded = folded + products[:, start : start + 128]
        energy_out[...] = energy_in[...] + request_weight * folded
        spectrum = apply_left(z_inv[...], weighted)
        for q in range(NX):
            high, low = split(spectrum[:, q * NY : (q + 1) * NY])
            high_rows[q * NZ : (q + 1) * NZ, :] = high
            low_rows[q * NZ : (q + 1) * NZ, :] = low
        spectrum = apply_rows(y_inv[...], high_rows[...], low_rows[...])
        for q in range(NX):
            lines[q * NY : (q + 1) * NY, :] = spectrum[:, q * NZ : (q + 1) * NZ]
        for y in range(NY):
            field[:, y * NZ : (y + 1) * NZ] = apply_left(
                x_inv[...], lines[pl.ds(y, NX, stride=NY), :]
            )
        store_force(
            force_refs, force_in[...] - (exchange_mix * total_weight) * (field[...] * other)
        )


def pair_step(slot, weights, own, other, tables, force, energy, pieces=1, squares=None):
    if pieces == 1:
        piece = force.shape
        extra = ()
    else:
        planes = NX // pieces
        fold = fold_of(planes, NY * NZ)
        piece = (2 * planes * fold, NY * NZ // fold)
        extra = (squares,)
    outs = [jax.ShapeDtypeStruct(energy.shape, jnp.float32)]
    outs += [jax.ShapeDtypeStruct(piece, jnp.float32)] * pieces
    return pl.pallas_call(
        functools.partial(pair_kernel, slot),
        out_shape=outs,
        in_specs=in_vmem(5 + len(tables) + len(extra)),
        out_specs=in_vmem(1 + pieces),
        scratch_shapes=[
            pltpu.VMEM((NX * NY, NZ), jnp.float32),
            pltpu.VMEM((NX * NY, NZ), jnp.bfloat16),
            pltpu.VMEM((NX * NY, NZ), jnp.bfloat16),
            pltpu.VMEM((NX, NY * NZ), jnp.float32),
        ],
        input_output_aliases={3 + len(tables): 1} if pieces == 1 else {},
        compiler_params=pltpu.CompilerParams(vmem_limit_bytes=32 << 20),
        cost_estimate=pl.CostEstimate(flops=3 << 30, transcendentals=0, bytes_accessed=3 << 20),
        name="pair_step",
    )(weights, own, other, *tables, force, energy, *extra)


def fold_of(planes, cells):
    return 2 if (2 * planes) % 8 == 0 and cells % 256 == 0 else 1


def in_vmem(count):
    return [pl.BlockSpec(memory_space=pltpu.VMEM)] * count


def with_scalar(count):
    return [pl.BlockSpec(memory_space=pltpu.SMEM)] + in_vmem(count)


def pick(place, choices):
    chosen = choices[0]
    for index in range(1, len(choices)):
        chosen = jnp.where(place == index, choices[index], chosen)
    return chosen


def prepare_kernel(fold, place, orbitals, *out_refs):
    planes, slabs, cells = orbitals.shape
    part = cells // fold
    for f in range(fold):
        rows = slice(f * planes, (f + 1) * planes)
        blocks = [orbitals[:, j, f * part : (f + 1) * part] for j in range(slabs)]
        for r in range(slabs):
            out_refs[r][rows, :] = pick(place[0] ^ r, blocks)


def prepare(place, orbitals):
    planes, slabs, cells = orbitals.shape
    fold = fold_of(planes, cells)
    piece = jax.ShapeDtypeStruct((planes * fold, cells // fold), jnp.float32)
    return pl.pallas_call(
        functools.partial(prepare_kernel, fold),
        out_shape=[piece] * slabs,
        in_specs=with_scalar(1),
        out_specs=in_vmem(slabs),
        compiler_params=pltpu.CompilerParams(vmem_limit_bytes=8 << 20),
        name="prepare",
    )(place, orbitals)


def assemble_kernel(fold, *refs):
    out_ref = refs[-1]
    planes = refs[0].shape[0] // fold
    part = refs[0].shape[1]
    for r, ref in enumerate(refs[:-1]):
        for f in range(fold):
            out_ref[r * planes : (r + 1) * planes, f * part : (f + 1) * part] = ref[
                f * planes : (f + 1) * planes, :
            ]


def assemble(pieces):
    _, part = pieces[0].shape
    fold = NY * NZ // part
    return pl.pallas_call(
        functools.partial(assemble_kernel, fold),
        out_shape=jax.ShapeDtypeStruct((NX, NY * NZ), jnp.float32),
        in_specs=in_vmem(len(pieces)),
        out_specs=in_vmem(1)[0],
        compiler_params=pltpu.CompilerParams(vmem_limit_bytes=8 << 20),
        name="assemble",
    )(*pieces)


def finish_kernel(fold, place, orbitals, local_pot, *refs):
    out_ref = refs[-1]
    planes, slabs, cells = orbitals.shape
    part = cells // fold
    for f in range(fold):
        rows = slice(f * planes, (f + 1) * planes)
        cols = slice(f * part, (f + 1) * part)
        pieces = [ref[rows, :] for ref in refs[:-1]]
        local = local_pot[rows, :]
        for j in range(slabs):
            out_ref[:, j, cols] = local * orbitals[:, j, cols] + pick(place[0] ^ j, pieces)


def finish(place, orbitals, local_pot, pieces):
    planes, _, cells = orbitals.shape
    return pl.pallas_call(
        functools.partial(finish_kernel, fold_of(planes, cells)),
        out_shape=jax.ShapeDtypeStruct(orbitals.shape, jnp.float32),
        in_specs=with_scalar(2 + len(pieces)),
        out_specs=in_vmem(1)[0],
        compiler_params=pltpu.CompilerParams(vmem_limit_bytes=8 << 20),
        name="finish",
    )(place, orbitals, local_pot, *pieces)


def swap(value, axis, reach):
    size = lax.axis_size(axis)
    return lax.ppermute(value, axis, [(i, i ^ reach) for i in range(size)])


def share(value, devices):
    sent = jnp.broadcast_to(value[None], (devices,) + value.shape)
    return lax.all_to_all(sent, ("band", "slab"), 0, 0)


def gather_ring(own, band_index, bands):
    groups = [2 * p if p < bands // 2 else 2 * (bands - 1 - p) + 1 for p in range(bands)]
    place = band_index // 2
    position = jnp.where(band_index % 2 == 0, place, bands - 1 - place)

    def group_at(position):
        position = position % bands
        return jnp.where(position < bands // 2, 2 * position, 2 * (bands - 1 - position) + 1)

    def shift(value, by):
        moves = [(groups[p], groups[(p + by) % bands]) for p in range(bands)]
        return lax.ppermute(value, "band", moves)

    ahead = behind = own
    blocks = []
    steps = bands // 2 - 1
    for step in range(steps):
        ahead = shift(ahead, 1)
        behind = shift(behind, -1)
        blocks.append((ahead, group_at(position - step - 1)))
        blocks.append((behind, group_at(position + step + 1)))
    half = own.shape[0] // 2
    head = shift(ahead[:half], 1)
    tail = shift(behind[half:], -1)
    blocks.append((jnp.concatenate([head, tail], axis=0), group_at(position + steps + 1)))
    return blocks


def body(orbitals, partners, counts):
    bands = lax.axis_size("band")
    slabs = lax.axis_size("slab")
    band_index = lax.axis_index("band")
    slab_index = lax.axis_index("slab")
    orb_group, planes, _ = orbitals.shape
    total_orbs = orb_group * bands
    assert orb_group == slabs

    place = slab_index.astype(jnp.int32).reshape(1)
    by_plane = jnp.transpose(orbitals, (1, 0, 2))
    sends = prepare(place, by_plane)
    own = assemble([sends[0]] + [swap(sends[r], "slab", r) for r in range(1, slabs)])

    others = gather_ring(own, band_index, bands)

    row = jnp.arange(NX, dtype=jnp.int32)
    held_x = (slab_index ^ (row // planes)) * planes + row % planes
    tables = transform_tables(held_x)

    groups = jnp.stack([group for _, group in others]).astype(jnp.int32)
    active = (slab_index < counts).astype(jnp.float32)
    mine = jnp.arange(bands, dtype=jnp.int32)[:, None] == band_index
    my_partners = jnp.sum(jnp.where(mine, partners, 0), axis=0)
    my_active = jnp.sum(jnp.where(mine, active, 0.0), axis=0)
    requested = jnp.sum(
        jnp.where(groups[:, None] == my_partners[None, :], my_active[None, :], 0.0), axis=1
    )
    wanted_by = jnp.sum(jnp.where(partners == band_index, active, 0.0), axis=1)
    chosen = groups[:, None] == jnp.arange(bands, dtype=jnp.int32)[None, :]
    returned = jnp.sum(jnp.where(chosen, wanted_by[None, :], 0.0), axis=1)
    weights = jnp.stack([requested + returned, requested], axis=1).reshape(-1)
    weights = jnp.broadcast_to(weights[:, None], weights.shape + (128,))

    force = jnp.zeros((NX, NY * NZ), jnp.float32)
    energy = jnp.zeros((1, 128), jnp.float32)
    squares = own * own
    for other, _ in others:
        squares = squares + other * other
    for slot, (other, _) in enumerate(others):
        if slot < len(others) - 1:
            energy, force = pair_step(slot, weights, own, other, tables, force, energy)
        else:
            energy, *outgoing = pair_step(
                slot, weights, own, other, tables, force, energy, slabs, squares
            )

    arrived = [outgoing[0]] + [swap(outgoing[r], "slab", r) for r in range(1, slabs)]
    shared = share(energy, bands * slabs)
    rows = arrived[0].shape[0] // 2
    density = 2.0 / total_orbs * sum(piece[rows:] for piece in arrived)
    local_pot = slater_coeff * jnp.cbrt(density)
    forces = finish(place, by_plane, local_pot, arrived)
    energy_total = jnp.sum(shared)
    return (
        jnp.transpose(forces, (1, 0, 2)),
        -energy_total / (2.0 * total_orbs * NX * NY * NZ),
    )


def solution(mesh):
    placed = (P("band", "slab", None), P(), P())
    return jax.shard_map(
        body, mesh=mesh, in_specs=placed, out_specs=(P("band", "slab", None), P()), check_vma=False
    )
```

```python
import functools
import math

import jax
import jax.numpy as jnp
from jax import lax
from jax.experimental import pallas as pl
from jax.experimental.pallas import tpu as pltpu
from jax.sharding import PartitionSpec as P


NX = 48
NY = 48
NZ = 48
NZP = 96


slater_coeff = -((3.0 / math.pi) ** (1.0 / 3.0))
exchange_mix = 0.25
screening = 0.25
row_row = (((1,), (1,)), ((), ()))


def split(value):
    high = value.astype(jnp.bfloat16)
    low = (value - high.astype(jnp.float32)).astype(jnp.bfloat16)
    return high, low


def cas(rows, cols, length):
    phase_angle = 2.0 * math.pi / length * (rows * cols % length).astype(jnp.float32)
    return jnp.cos(phase_angle) + jnp.sin(phase_angle)


def split_table(matrix):
    high = lax.reduce_precision(matrix, 8, 7)
    return high.astype(jnp.bfloat16), (matrix - high).astype(jnp.bfloat16)


def wide(matrix):
    high, low = split_table(matrix)
    return jnp.concatenate([high, high, low], axis=1)


def tall(matrix):
    high, low = split_table(matrix)
    return jnp.concatenate([high, low], axis=0)


def wavenumber_sq(position):
    length = position.shape[0]
    signed = jnp.where(position > length // 2, position - length, position).astype(jnp.float32)
    wave_number = 2.0 * math.pi / length * signed
    return wave_number * wave_number


def transform_tables(count, held_x):
    x_waves = count[:NX]
    y_cells = count[:NY]
    z_cells = count[:NZ]
    z_waves = count[:NZP]
    total = (
        wavenumber_sq(z_waves)[:, None, None]
        + wavenumber_sq(x_waves)[None, :, None]
        + wavenumber_sq(y_cells)[None, None, :]
    )
    kernel_table = 4.0 * math.pi / (NX * NY * NZP) / (total + screening * screening)
    y_matrix = cas(y_cells[:, None], y_cells[None, :], NY)
    return (
        wide(cas(x_waves[:, None], held_x[None, :], NX)),
        wide(y_matrix),
        tall(cas(z_waves[:, None], z_cells[None, :], NZP)),
        kernel_table.reshape(NZP, NX * NY),
        wide(cas(z_cells[:, None], z_waves[None, :], NZP)),
        tall(y_matrix),
        wide(cas(held_x[:, None], x_waves[None, :], NX)),
    )


def apply_left(matrix, value):
    high, low = split(value)
    stacked = jnp.concatenate([high, low, high], axis=0)
    return jnp.dot(matrix, stacked, preferred_element_type=jnp.float32)


def apply_rows(matrix, high, low):
    half = matrix.shape[0] // 2
    both = lax.dot_general(matrix, high, row_row, preferred_element_type=jnp.float32)
    rest = lax.dot_general(matrix[:half], low, row_row, preferred_element_type=jnp.float32)
    return both[:half] + both[half:] + rest


def cut_into(refs, value, part_index):
    planes = NX // len(refs)
    part = refs[0].shape[1]
    fold = NY * NZ // part
    first = part_index * planes * fold
    for r, ref in enumerate(refs):
        for f in range(fold):
            ref[first + f * planes : first + (f + 1) * planes, :] = value[
                r * planes : (r + 1) * planes, f * part : (f + 1) * part
            ]


def store_force(force_refs, value):
    if len(force_refs) == 1:
        force_refs[0][...] = value
    else:
        cut_into(force_refs, value, 0)


def pair_kernel(
    slot, weights, own_ref, other_ref, x_fwd, y_fwd, z_fwd, table, z_inv, y_inv, x_inv,
    force_in, energy_in, *refs,
):
    *refs, lines, high_rows, low_rows, field = refs
    if len(refs) == 2:
        energy_out, *force_refs = refs
    else:
        squares_in, energy_out, *force_refs = refs
        cut_into(force_refs, squares_in[...], 1)
    total_weight = jnp.max(weights[2 * slot : 2 * slot + 1, :])
    request_weight = weights[2 * slot + 1 : 2 * slot + 2, :]

    @pl.when(total_weight == 0.0)
    def _():
        energy_out[...] = energy_in[...]
        if len(force_refs) > 1:
            store_force(force_refs, force_in[...])

    @pl.when(total_weight != 0.0)
    def _():
        other = other_ref[...]
        density = own_ref[...] * other
        spectrum = apply_left(x_fwd[...], density)
        for y in range(NY):
            lines[y * NX : (y + 1) * NX, :] = spectrum[:, y * NZ : (y + 1) * NZ]
        for q in range(NX):
            plane = apply_left(y_fwd[...], lines[pl.ds(q, NY, stride=NX), :])
            high, low = split(plane)
            high_rows[q * NY : (q + 1) * NY, :] = high
            low_rows[q * NY : (q + 1) * NY, :] = low
        spectrum = apply_rows(z_fwd[...], high_rows[...], low_rows[...])
        weighted = spectrum * table[...]
        products = jnp.sum(spectrum * weighted, axis=0, keepdims=True)
        folded = products[:, :128]
        for start in range(128, NX * NY, 128):
            folded = folded + products[:, start : start + 128]
        energy_out[...] = energy_in[...] + request_weight * folded
        spectrum = apply_left(z_inv[...], weighted)
        for q in range(NX):
            high, low = split(spectrum[:, q * NY : (q + 1) * NY])
            high_rows[q * NZ : (q + 1) * NZ, :] = high
            low_rows[q * NZ : (q + 1) * NZ, :] = low
        spectrum = apply_rows(y_inv[...], high_rows[...], low_rows[...])
        for q in range(NX):
            lines[q * NY : (q + 1) * NY, :] = spectrum[:, q * NZ : (q + 1) * NZ]
        for y in range(NY):
            field[:, y * NZ : (y + 1) * NZ] = apply_left(
                x_inv[...], lines[pl.ds(y, NX, stride=NY), :]
            )
        store_force(
            force_refs, force_in[...] - (exchange_mix * total_weight) * (field[...] * other)
        )


def pair_step(slot, weights, own, other, tables, force, energy, pieces=1, squares=None):
    if pieces == 1:
        piece = force.shape
        extra = ()
    else:
        planes = NX // pieces
        fold = fold_of(planes, NY * NZ)
        piece = (2 * planes * fold, NY * NZ // fold)
        extra = (squares,)
    outs = [jax.ShapeDtypeStruct(energy.shape, jnp.float32)]
    outs += [jax.ShapeDtypeStruct(piece, jnp.float32)] * pieces
    return pl.pallas_call(
        functools.partial(pair_kernel, slot),
        out_shape=outs,
        in_specs=in_vmem(5 + len(tables) + len(extra)),
        out_specs=in_vmem(1 + pieces),
        scratch_shapes=[
            pltpu.VMEM((NX * NY, NZ), jnp.float32),
            pltpu.VMEM((NX * NY, NZ), jnp.bfloat16),
            pltpu.VMEM((NX * NY, NZ), jnp.bfloat16),
            pltpu.VMEM((NX, NY * NZ), jnp.float32),
        ],
        input_output_aliases={3 + len(tables): 1} if pieces == 1 else {},
        compiler_params=pltpu.CompilerParams(vmem_limit_bytes=32 << 20),
        cost_estimate=pl.CostEstimate(flops=3 << 30, transcendentals=0, bytes_accessed=3 << 20),
        name="pair_step",
    )(weights, own, other, *tables, force, energy, *extra)


def fold_of(planes, cells):
    return 2 if (2 * planes) % 8 == 0 and cells % 256 == 0 else 1


def in_vmem(count):
    return [pl.BlockSpec(memory_space=pltpu.VMEM)] * count


def with_scalar(count):
    return [pl.BlockSpec(memory_space=pltpu.SMEM)] + in_vmem(count)


def pick(place, choices):
    chosen = choices[0]
    for index in range(1, len(choices)):
        chosen = jnp.where(place == index, choices[index], chosen)
    return chosen


def prepare_kernel(fold, place, orbitals, *out_refs):
    planes, slabs, cells = orbitals.shape
    part = cells // fold
    for f in range(fold):
        rows = slice(f * planes, (f + 1) * planes)
        blocks = [orbitals[:, j, f * part : (f + 1) * part] for j in range(slabs)]
        for r in range(slabs):
            out_refs[r][rows, :] = pick(place[0] ^ r, blocks)


def prepare(place, orbitals):
    planes, slabs, cells = orbitals.shape
    fold = fold_of(planes, cells)
    piece = jax.ShapeDtypeStruct((planes * fold, cells // fold), jnp.float32)
    return pl.pallas_call(
        functools.partial(prepare_kernel, fold),
        out_shape=[piece] * slabs,
        in_specs=with_scalar(1),
        out_specs=in_vmem(slabs),
        compiler_params=pltpu.CompilerParams(vmem_limit_bytes=8 << 20),
        name="prepare",
    )(place, orbitals)


def assemble_kernel(fold, *refs):
    out_ref = refs[-1]
    planes = refs[0].shape[0] // fold
    part = refs[0].shape[1]
    for r, ref in enumerate(refs[:-1]):
        for f in range(fold):
            out_ref[r * planes : (r + 1) * planes, f * part : (f + 1) * part] = ref[
                f * planes : (f + 1) * planes, :
            ]


def assemble(pieces):
    rows, part = pieces[0].shape
    fold = NY * NZ // part
    return pl.pallas_call(
        functools.partial(assemble_kernel, fold),
        out_shape=jax.ShapeDtypeStruct((rows // fold * len(pieces), NY * NZ), jnp.float32),
        in_specs=in_vmem(len(pieces)),
        out_specs=in_vmem(1)[0],
        compiler_params=pltpu.CompilerParams(vmem_limit_bytes=8 << 20),
        name="assemble",
    )(*pieces)


def clear_kernel(out_ref):
    out_ref[...] = jnp.zeros_like(out_ref)


def clear(shape):
    return pl.pallas_call(
        clear_kernel,
        out_shape=jax.ShapeDtypeStruct(shape, jnp.float32),
        out_specs=in_vmem(1)[0],
        compiler_params=pltpu.CompilerParams(vmem_limit_bytes=8 << 20),
        name="clear",
    )()


def join_kernel(*refs):
    out_ref = refs[-1]
    first = 0
    for ref in refs[:-1]:
        out_ref[first : first + ref.shape[0], :] = ref[...]
        first += ref.shape[0]


def join(*parts):
    rows = sum(part.shape[0] for part in parts)
    return pl.pallas_call(
        join_kernel,
        out_shape=jax.ShapeDtypeStruct((rows,) + parts[0].shape[1:], jnp.float32),
        in_specs=in_vmem(len(parts)),
        out_specs=in_vmem(1)[0],
        compiler_params=pltpu.CompilerParams(vmem_limit_bytes=8 << 20),
        name="join",
    )(*parts)


def finish_kernel(fold, place, orbitals, local_pot, *refs):
    out_ref = refs[-1]
    planes, slabs, cells = orbitals.shape
    part = cells // fold
    for f in range(fold):
        rows = slice(f * planes, (f + 1) * planes)
        cols = slice(f * part, (f + 1) * part)
        pieces = [ref[rows, :] for ref in refs[:-1]]
        local = local_pot[rows, :]
        for j in range(slabs):
            out_ref[:, j, cols] = local * orbitals[:, j, cols] + pick(place[0] ^ j, pieces)


def finish(place, orbitals, local_pot, pieces):
    planes, _, cells = orbitals.shape
    return pl.pallas_call(
        functools.partial(finish_kernel, fold_of(planes, cells)),
        out_shape=jax.ShapeDtypeStruct(orbitals.shape, jnp.float32),
        in_specs=with_scalar(2 + len(pieces)),
        out_specs=in_vmem(1)[0],
        compiler_params=pltpu.CompilerParams(vmem_limit_bytes=8 << 20),
        name="finish",
    )(place, orbitals, local_pot, *pieces)


def slab_swap(value, reach):
    size = lax.axis_size("slab")
    return lax.ppermute(value, "slab", [(i, i ^ reach) for i in range(size)])


def share(value, devices):
    sent = jnp.broadcast_to(value[None], (devices,) + value.shape)
    return lax.all_to_all(sent, ("band", "slab"), 0, 0)


def gather_ring(halves, band_index, bands):
    groups = [2 * p if p < bands // 2 else 2 * (bands - 1 - p) + 1 for p in range(bands)]
    place = band_index // 2
    position = jnp.where(band_index % 2 == 0, place, bands - 1 - place)

    def group_at(position):
        position = position % bands
        return jnp.where(position < bands // 2, 2 * position, 2 * (bands - 1 - position) + 1)

    def shift(value, by):
        moves = [(groups[p], groups[(p + by) % bands]) for p in range(bands)]
        return lax.ppermute(value, "band", moves)

    came = [(shift(half, 1), shift(half, -1)) for half in halves]
    blocks = []
    steps = bands // 2 - 1
    for step in range(steps):
        if step == 0:
            ahead, behind = (join(*pair) for pair in zip(*came))
        else:
            ahead = shift(ahead, 1)
            behind = shift(behind, -1)
        blocks.append((ahead, group_at(position - step - 1)))
        blocks.append((behind, group_at(position + step + 1)))
    half = ahead.shape[0] // 2
    head = shift(ahead[:half], 1)
    tail = shift(behind[half:], -1)
    blocks.append((join(head, tail), group_at(position + steps + 1)))
    return blocks


def body(orbitals, partners, counts):
    bands = lax.axis_size("band")
    slabs = lax.axis_size("slab")
    band_index = lax.axis_index("band")
    slab_index = lax.axis_index("slab")
    orb_group, planes, _ = orbitals.shape
    total_orbs = orb_group * bands
    assert orb_group == slabs

    place = slab_index.astype(jnp.int32).reshape(1)
    by_plane = jnp.transpose(orbitals, (1, 0, 2))
    sends = prepare(place, by_plane)
    pieces = [sends[0]] + [slab_swap(sends[r], r) for r in range(1, slabs)]
    halves = [assemble(pieces[: slabs // 2]), assemble(pieces[slabs // 2 :])]
    own = join(*halves)
    others = gather_ring(halves, band_index, bands)
    force = clear((NX, NY * NZ))

    count = jnp.arange(max(NX, NY, NZP), dtype=jnp.int32)
    own, count, partners, counts = lax.optimization_barrier((own, count, partners, counts))
    row = count[:NX]
    held_x = (slab_index ^ (row // planes)) * planes + row % planes
    tables = transform_tables(count, held_x)

    groups = jnp.stack([group for _, group in others]).astype(jnp.int32)
    active = (slab_index < counts).astype(jnp.float32)
    mine = jnp.arange(bands, dtype=jnp.int32)[:, None] == band_index
    my_partners = jnp.sum(jnp.where(mine, partners, 0), axis=0)
    my_active = jnp.sum(jnp.where(mine, active, 0.0), axis=0)
    requested = jnp.sum(
        jnp.where(groups[:, None] == my_partners[None, :], my_active[None, :], 0.0), axis=1
    )
    wanted_by = jnp.sum(jnp.where(partners == band_index, active, 0.0), axis=1)
    chosen = groups[:, None] == jnp.arange(bands, dtype=jnp.int32)[None, :]
    returned = jnp.sum(jnp.where(chosen, wanted_by[None, :], 0.0), axis=1)
    weights = jnp.stack([requested + returned, requested], axis=1).reshape(-1)
    weights = jnp.broadcast_to(weights[:, None], weights.shape + (128,))

    energy = jnp.zeros((1, 128), jnp.float32)
    squares = own * own
    for other, _ in others:
        squares = squares + other * other
    for slot, (other, _) in enumerate(others):
        if slot < len(others) - 1:
            energy, force = pair_step(slot, weights, own, other, tables, force, energy)
        else:
            energy, *outgoing = pair_step(
                slot, weights, own, other, tables, force, energy, slabs, squares
            )

    arrived = [outgoing[0]] + [slab_swap(outgoing[r], r) for r in range(1, slabs)]
    shared = share(energy, bands * slabs)
    rows = arrived[0].shape[0] // 2
    density = 2.0 / total_orbs * sum(piece[rows:] for piece in arrived)
    local_pot = slater_coeff * jnp.cbrt(density)
    forces = finish(place, by_plane, local_pot, arrived)
    energy_total = jnp.sum(shared)
    return (
        jnp.transpose(forces, (1, 0, 2)),
        -energy_total / (2.0 * total_orbs * NX * NY * NZ),
    )


def solution(mesh):
    placed = (P("band", "slab", None), P(), P())
    return jax.shard_map(
        body, mesh=mesh, in_specs=placed, out_specs=(P("band", "slab", None), P()), check_vma=False
    )
```

```python
import functools
import math

import jax
import jax.numpy as jnp
import ml_dtypes
import numpy as np
from jax import lax
from jax.experimental import pallas as pl
from jax.experimental.pallas import tpu as pltpu
from jax.sharding import PartitionSpec as P


NX = 48
NY = 48
NZ = 48
NZP = 96


slater_coeff = -((3.0 / math.pi) ** (1.0 / 3.0))
exchange_mix = 0.25
screening = 0.25
row_row = (((1,), (1,)), ((), ()))


def split(value):
    high = value.astype(jnp.bfloat16)
    low = (value - high.astype(jnp.float32)).astype(jnp.bfloat16)
    return high, low


def cas(rows, cols, length):
    phase_angle = 2.0 * math.pi / length * (np.outer(rows, cols) % length)
    return np.cos(phase_angle) + np.sin(phase_angle)


def split_table(matrix):
    high = matrix.astype(ml_dtypes.bfloat16)
    return high, (matrix - high.astype(np.float64)).astype(ml_dtypes.bfloat16)


def wide(matrix):
    high, low = split_table(matrix)
    return np.concatenate([high, high, low], axis=1)


def tall(matrix):
    high, low = split_table(matrix)
    return np.concatenate([high, low], axis=0)


def wavenumber_sq(length):
    return (2.0 * np.pi * np.fft.fftfreq(length)) ** 2


def transform_tables(slab_index, slabs):
    x_waves, y_cells, z_cells, z_waves = (np.arange(count) for count in (NX, NY, NZ, NZP))
    planes = NX // slabs
    held_x = [(slab ^ (x_waves // planes)) * planes + x_waves % planes for slab in range(slabs)]
    total = (
        wavenumber_sq(NZP)[:, None, None]
        + wavenumber_sq(NX)[None, :, None]
        + wavenumber_sq(NY)[None, None, :]
    )
    kernel_table = 4.0 * math.pi / (NX * NY * NZP) / (total + screening * screening)
    y_matrix = cas(y_cells, y_cells, NY)
    forward = jnp.asarray(np.stack([wide(cas(x_waves, held, NX)) for held in held_x]))
    backward = jnp.asarray(np.stack([wide(cas(held, x_waves, NX)) for held in held_x]))
    return (
        lax.dynamic_index_in_dim(forward, slab_index, 0, keepdims=False),
        jnp.asarray(wide(y_matrix)),
        jnp.asarray(tall(cas(z_waves, z_cells, NZP))),
        jnp.asarray(kernel_table.reshape(NZP, NX * NY).astype(np.float32)),
        jnp.asarray(wide(cas(z_cells, z_waves, NZP))),
        jnp.asarray(tall(y_matrix)),
        lax.dynamic_index_in_dim(backward, slab_index, 0, keepdims=False),
    )


def apply_left(matrix, value):
    high, low = split(value)
    stacked = jnp.concatenate([high, low, high], axis=0)
    return jnp.dot(matrix, stacked, preferred_element_type=jnp.float32)


def apply_rows(matrix, high, low):
    half = matrix.shape[0] // 2
    both = lax.dot_general(matrix, high, row_row, preferred_element_type=jnp.float32)
    rest = lax.dot_general(matrix[:half], low, row_row, preferred_element_type=jnp.float32)
    return both[:half] + both[half:] + rest


def cut_into(refs, value, part_index):
    planes = NX // len(refs)
    part = refs[0].shape[1]
    fold = NY * NZ // part
    first = part_index * planes * fold
    for r, ref in enumerate(refs):
        for f in range(fold):
            ref[first + f * planes : first + (f + 1) * planes, :] = value[
                r * planes : (r + 1) * planes, f * part : (f + 1) * part
            ]


def store_force(force_refs, value):
    if len(force_refs) == 1:
        force_refs[0][...] = value
    else:
        cut_into(force_refs, value, 0)


def pair_kernel(
    slot, weights, own_ref, other_ref, x_fwd, y_fwd, z_fwd, table, z_inv, y_inv, x_inv,
    force_in, energy_in, *refs,
):
    *refs, lines, high_rows, low_rows, field = refs
    if len(refs) == 2:
        energy_out, *force_refs = refs
    else:
        squares_in, energy_out, *force_refs = refs
        cut_into(force_refs, squares_in[...], 1)
    total_weight = jnp.max(weights[2 * slot : 2 * slot + 1, :])
    request_weight = weights[2 * slot + 1 : 2 * slot + 2, :]

    @pl.when(total_weight == 0.0)
    def _():
        energy_out[...] = energy_in[...]
        if len(force_refs) > 1:
            store_force(force_refs, force_in[...])

    @pl.when(total_weight != 0.0)
    def _():
        other = other_ref[...]
        density = own_ref[...] * other
        spectrum = apply_left(x_fwd[...], density)
        for y in range(NY):
            lines[y * NX : (y + 1) * NX, :] = spectrum[:, y * NZ : (y + 1) * NZ]
        for q in range(NX):
            plane = apply_left(y_fwd[...], lines[pl.ds(q, NY, stride=NX), :])
            high, low = split(plane)
            high_rows[q * NY : (q + 1) * NY, :] = high
            low_rows[q * NY : (q + 1) * NY, :] = low
        spectrum = apply_rows(z_fwd[...], high_rows[...], low_rows[...])
        weighted = spectrum * table[...]
        products = jnp.sum(spectrum * weighted, axis=0, keepdims=True)
        folded = products[:, :128]
        for start in range(128, NX * NY, 128):
            folded = folded + products[:, start : start + 128]
        energy_out[...] = energy_in[...] + request_weight * folded
        spectrum = apply_left(z_inv[...], weighted)
        for q in range(NX):
            high, low = split(spectrum[:, q * NY : (q + 1) * NY])
            high_rows[q * NZ : (q + 1) * NZ, :] = high
            low_rows[q * NZ : (q + 1) * NZ, :] = low
        spectrum = apply_rows(y_inv[...], high_rows[...], low_rows[...])
        for q in range(NX):
            lines[q * NY : (q + 1) * NY, :] = spectrum[:, q * NZ : (q + 1) * NZ]
        for y in range(NY):
            field[:, y * NZ : (y + 1) * NZ] = apply_left(
                x_inv[...], lines[pl.ds(y, NX, stride=NY), :]
            )
        store_force(
            force_refs, force_in[...] - (exchange_mix * total_weight) * (field[...] * other)
        )


def pair_step(slot, weights, own, other, tables, force, energy, pieces=1, squares=None):
    if pieces == 1:
        piece = force.shape
        extra = ()
    else:
        planes = NX // pieces
        fold = fold_of(planes, NY * NZ)
        piece = (2 * planes * fold, NY * NZ // fold)
        extra = (squares,)
    outs = [jax.ShapeDtypeStruct(energy.shape, jnp.float32)]
    outs += [jax.ShapeDtypeStruct(piece, jnp.float32)] * pieces
    return pl.pallas_call(
        functools.partial(pair_kernel, slot),
        out_shape=outs,
        in_specs=in_vmem(5 + len(tables) + len(extra)),
        out_specs=in_vmem(1 + pieces),
        scratch_shapes=[
            pltpu.VMEM((NX * NY, NZ), jnp.float32),
            pltpu.VMEM((NX * NY, NZ), jnp.bfloat16),
            pltpu.VMEM((NX * NY, NZ), jnp.bfloat16),
            pltpu.VMEM((NX, NY * NZ), jnp.float32),
        ],
        input_output_aliases={3 + len(tables): 1} if pieces == 1 else {},
        compiler_params=pltpu.CompilerParams(vmem_limit_bytes=32 << 20),
        cost_estimate=pl.CostEstimate(flops=3 << 30, transcendentals=0, bytes_accessed=3 << 20),
        name="pair_step",
    )(weights, own, other, *tables, force, energy, *extra)


def fold_of(planes, cells):
    return 2 if (2 * planes) % 8 == 0 and cells % 256 == 0 else 1


def in_vmem(count):
    return [pl.BlockSpec(memory_space=pltpu.VMEM)] * count


def with_scalar(count):
    return [pl.BlockSpec(memory_space=pltpu.SMEM)] + in_vmem(count)


def pick(place, choices):
    chosen = choices[0]
    for index in range(1, len(choices)):
        chosen = jnp.where(place == index, choices[index], chosen)
    return chosen


def prepare_kernel(fold, place, orbitals, *out_refs):
    planes, slabs, cells = orbitals.shape
    part = cells // fold
    for f in range(fold):
        rows = slice(f * planes, (f + 1) * planes)
        blocks = [orbitals[:, j, f * part : (f + 1) * part] for j in range(slabs)]
        for r in range(slabs):
            out_refs[r][rows, :] = pick(place[0] ^ r, blocks)


def prepare(place, orbitals):
    planes, slabs, cells = orbitals.shape
    fold = fold_of(planes, cells)
    piece = jax.ShapeDtypeStruct((planes * fold, cells // fold), jnp.float32)
    return pl.pallas_call(
        functools.partial(prepare_kernel, fold),
        out_shape=[piece] * slabs,
        in_specs=with_scalar(1),
        out_specs=in_vmem(slabs),
        compiler_params=pltpu.CompilerParams(vmem_limit_bytes=8 << 20),
        name="prepare",
    )(place, orbitals)


def assemble_kernel(fold, *refs):
    out_ref = refs[-1]
    planes = refs[0].shape[0] // fold
    part = refs[0].shape[1]
    for r, ref in enumerate(refs[:-1]):
        for f in range(fold):
            out_ref[r * planes : (r + 1) * planes, f * part : (f + 1) * part] = ref[
                f * planes : (f + 1) * planes, :
            ]


def assemble(pieces):
    rows, part = pieces[0].shape
    fold = NY * NZ // part
    return pl.pallas_call(
        functools.partial(assemble_kernel, fold),
        out_shape=jax.ShapeDtypeStruct((rows // fold * len(pieces), NY * NZ), jnp.float32),
        in_specs=in_vmem(len(pieces)),
        out_specs=in_vmem(1)[0],
        compiler_params=pltpu.CompilerParams(vmem_limit_bytes=8 << 20),
        name="assemble",
    )(*pieces)


def clear_kernel(out_ref):
    out_ref[...] = jnp.zeros_like(out_ref)


def clear(shape):
    return pl.pallas_call(
        clear_kernel,
        out_shape=jax.ShapeDtypeStruct(shape, jnp.float32),
        out_specs=in_vmem(1)[0],
        compiler_params=pltpu.CompilerParams(vmem_limit_bytes=8 << 20),
        name="clear",
    )()


def join_kernel(*refs):
    out_ref = refs[-1]
    first = 0
    for ref in refs[:-1]:
        out_ref[first : first + ref.shape[0], :] = ref[...]
        first += ref.shape[0]


def join(*parts):
    rows = sum(part.shape[0] for part in parts)
    return pl.pallas_call(
        join_kernel,
        out_shape=jax.ShapeDtypeStruct((rows,) + parts[0].shape[1:], jnp.float32),
        in_specs=in_vmem(len(parts)),
        out_specs=in_vmem(1)[0],
        compiler_params=pltpu.CompilerParams(vmem_limit_bytes=8 << 20),
        name="join",
    )(*parts)


def finish_kernel(fold, place, orbitals, local_pot, *refs):
    out_ref = refs[-1]
    planes, slabs, cells = orbitals.shape
    part = cells // fold
    for f in range(fold):
        rows = slice(f * planes, (f + 1) * planes)
        cols = slice(f * part, (f + 1) * part)
        pieces = [ref[rows, :] for ref in refs[:-1]]
        local = local_pot[rows, :]
        for j in range(slabs):
            out_ref[:, j, cols] = local * orbitals[:, j, cols] + pick(place[0] ^ j, pieces)


def finish(place, orbitals, local_pot, pieces):
    planes, _, cells = orbitals.shape
    return pl.pallas_call(
        functools.partial(finish_kernel, fold_of(planes, cells)),
        out_shape=jax.ShapeDtypeStruct(orbitals.shape, jnp.float32),
        in_specs=with_scalar(2 + len(pieces)),
        out_specs=in_vmem(1)[0],
        compiler_params=pltpu.CompilerParams(vmem_limit_bytes=8 << 20),
        name="finish",
    )(place, orbitals, local_pot, *pieces)


def slab_swap(value, reach):
    size = lax.axis_size("slab")
    return lax.ppermute(value, "slab", [(i, i ^ reach) for i in range(size)])


def share(value, devices):
    sent = jnp.broadcast_to(value[None], (devices,) + value.shape)
    return lax.all_to_all(sent, ("band", "slab"), 0, 0)


def gather_ring(halves, band_index, bands):
    groups = [2 * p if p < bands // 2 else 2 * (bands - 1 - p) + 1 for p in range(bands)]
    place = band_index // 2
    position = jnp.where(band_index % 2 == 0, place, bands - 1 - place)

    def group_at(position):
        position = position % bands
        return jnp.where(position < bands // 2, 2 * position, 2 * (bands - 1 - position) + 1)

    def shift(value, by):
        moves = [(groups[p], groups[(p + by) % bands]) for p in range(bands)]
        return lax.ppermute(value, "band", moves)

    came = [(shift(half, 1), shift(half, -1)) for half in halves]
    blocks = []
    steps = bands // 2 - 1
    for step in range(steps):
        if step == 0:
            ahead, behind = (join(*pair) for pair in zip(*came))
        else:
            ahead = shift(ahead, 1)
            behind = shift(behind, -1)
        blocks.append((ahead, group_at(position - step - 1)))
        blocks.append((behind, group_at(position + step + 1)))
    half = ahead.shape[0] // 2
    head = shift(ahead[:half], 1)
    tail = shift(behind[half:], -1)
    blocks.append((join(head, tail), group_at(position + steps + 1)))
    return blocks


def body(orbitals, partners, counts):
    bands = lax.axis_size("band")
    slabs = lax.axis_size("slab")
    band_index = lax.axis_index("band")
    slab_index = lax.axis_index("slab")
    orb_group, _, _ = orbitals.shape
    total_orbs = orb_group * bands
    assert orb_group == slabs

    place = slab_index.astype(jnp.int32).reshape(1)
    by_plane = jnp.transpose(orbitals, (1, 0, 2))
    sends = prepare(place, by_plane)
    pieces = [sends[0]] + [slab_swap(sends[r], r) for r in range(1, slabs)]
    halves = [assemble(pieces[: slabs // 2]), assemble(pieces[slabs // 2 :])]
    own = join(*halves)
    others = gather_ring(halves, band_index, bands)
    force = clear((NX, NY * NZ))

    own, partners, counts = lax.optimization_barrier((own, partners, counts))
    tables = transform_tables(slab_index, slabs)

    groups = jnp.stack([group for _, group in others]).astype(jnp.int32)
    active = (slab_index < counts).astype(jnp.float32)
    mine = jnp.arange(bands, dtype=jnp.int32)[:, None] == band_index
    my_partners = jnp.sum(jnp.where(mine, partners, 0), axis=0)
    my_active = jnp.sum(jnp.where(mine, active, 0.0), axis=0)
    requested = jnp.sum(
        jnp.where(groups[:, None] == my_partners[None, :], my_active[None, :], 0.0), axis=1
    )
    wanted_by = jnp.sum(jnp.where(partners == band_index, active, 0.0), axis=1)
    chosen = groups[:, None] == jnp.arange(bands, dtype=jnp.int32)[None, :]
    returned = jnp.sum(jnp.where(chosen, wanted_by[None, :], 0.0), axis=1)
    weights = jnp.stack([requested + returned, requested], axis=1).reshape(-1)
    weights = jnp.broadcast_to(weights[:, None], weights.shape + (128,))

    energy = jnp.zeros((1, 128), jnp.float32)
    squares = own * own
    for other, _ in others:
        squares = squares + other * other
    for slot, (other, _) in enumerate(others):
        if slot < len(others) - 1:
            energy, force = pair_step(slot, weights, own, other, tables, force, energy)
        else:
            energy, *outgoing = pair_step(
                slot, weights, own, other, tables, force, energy, slabs, squares
            )

    arrived = [outgoing[0]] + [slab_swap(outgoing[r], r) for r in range(1, slabs)]
    shared = share(energy, bands * slabs)
    rows = arrived[0].shape[0] // 2
    density = 2.0 / total_orbs * sum(piece[rows:] for piece in arrived)
    local_pot = slater_coeff * jnp.cbrt(density)
    forces = finish(place, by_plane, local_pot, arrived)
    energy_total = jnp.sum(shared)
    return (
        jnp.transpose(forces, (1, 0, 2)),
        -energy_total / (2.0 * total_orbs * NX * NY * NZ),
    )


def solution(mesh):
    placed = (P("band", "slab", None), P(), P())
    return jax.shard_map(
        body, mesh=mesh, in_specs=placed, out_specs=(P("band", "slab", None), P()), check_vma=False
    )
```

```python
import functools
import math

import jax
import jax.numpy as jnp
import ml_dtypes
import numpy as np
from jax import lax
from jax.experimental import pallas as pl
from jax.experimental.pallas import tpu as pltpu
from jax.sharding import PartitionSpec as P


NX = 48
NY = 48
NZ = 48
NZP = 96


slater_coeff = -((3.0 / math.pi) ** (1.0 / 3.0))
exchange_mix = 0.25
screening = 0.25
row_row = (((1,), (1,)), ((), ()))


def split(value):
    high = value.astype(jnp.bfloat16)
    low = (value - high.astype(jnp.float32)).astype(jnp.bfloat16)
    return high, low


def cas(rows, cols, length):
    phase_angle = 2.0 * math.pi / length * (np.outer(rows, cols) % length)
    return np.cos(phase_angle) + np.sin(phase_angle)


def split_table(matrix):
    high = matrix.astype(ml_dtypes.bfloat16)
    return high, (matrix - high.astype(np.float64)).astype(ml_dtypes.bfloat16)


def wide(matrix):
    high, low = split_table(matrix)
    return np.concatenate([high, high, low], axis=1)


def tall(matrix):
    high, low = split_table(matrix)
    return np.concatenate([high, low], axis=0)


def wavenumber_sq(length):
    return (2.0 * np.pi * np.fft.fftfreq(length)) ** 2


def transform_tables(slab_index, slabs):
    x_waves, y_cells, z_cells, z_waves = (np.arange(count) for count in (NX, NY, NZ, NZP))
    planes = NX // slabs
    held_x = [(slab ^ (x_waves // planes)) * planes + x_waves % planes for slab in range(slabs)]
    total = (
        wavenumber_sq(NZP)[:, None, None]
        + wavenumber_sq(NX)[None, :, None]
        + wavenumber_sq(NY)[None, None, :]
    )
    kernel_table = 4.0 * math.pi / (NX * NY * NZP) / (total + screening * screening)
    y_matrix = cas(y_cells, y_cells, NY)
    forward = jnp.asarray(np.stack([wide(cas(x_waves, held, NX)) for held in held_x]))
    backward = jnp.asarray(np.stack([wide(cas(held, x_waves, NX)) for held in held_x]))
    return (
        lax.dynamic_index_in_dim(forward, slab_index, 0, keepdims=False),
        jnp.asarray(wide(y_matrix)),
        jnp.asarray(tall(cas(z_waves, z_cells, NZP))),
        jnp.asarray(kernel_table.reshape(NZP, NX * NY).astype(np.float32)),
        jnp.asarray(wide(cas(z_cells, z_waves, NZP))),
        jnp.asarray(tall(y_matrix)),
        lax.dynamic_index_in_dim(backward, slab_index, 0, keepdims=False),
    )


def apply_left(matrix, value):
    high, low = split(value)
    stacked = jnp.concatenate([high, low, high], axis=0)
    return jnp.dot(matrix, stacked, preferred_element_type=jnp.float32)


def apply_rows(matrix, high, low):
    half = matrix.shape[0] // 2
    both = lax.dot_general(matrix, high, row_row, preferred_element_type=jnp.float32)
    rest = lax.dot_general(matrix[:half], low, row_row, preferred_element_type=jnp.float32)
    return both[:half] + both[half:] + rest


def cut_into(refs, value):
    planes = NX // len(refs)
    part = refs[0].shape[1]
    fold = NY * NZ // part
    for r, ref in enumerate(refs):
        for f in range(fold):
            ref[f * planes : (f + 1) * planes, :] = value[
                r * planes : (r + 1) * planes, f * part : (f + 1) * part
            ]


def store_force(force_refs, value):
    if len(force_refs) == 1:
        force_refs[0][...] = value
    else:
        cut_into(force_refs, value)


def pair_kernel(
    slot, weights, own_ref, other_ref, x_fwd, y_fwd, z_fwd, table, z_inv, y_inv, x_inv,
    force_in, energy_in, *refs,
):
    energy_out, *force_refs, lines, high_rows, low_rows, field = refs
    total_weight = jnp.max(weights[2 * slot : 2 * slot + 1, :])
    request_weight = weights[2 * slot + 1 : 2 * slot + 2, :]

    @pl.when(total_weight == 0.0)
    def _():
        energy_out[...] = energy_in[...]
        if len(force_refs) > 1:
            store_force(force_refs, force_in[...])

    @pl.when(total_weight != 0.0)
    def _():
        other = other_ref[...]
        density = own_ref[...] * other
        spectrum = apply_left(x_fwd[...], density)
        for y in range(NY):
            lines[y * NX : (y + 1) * NX, :] = spectrum[:, y * NZ : (y + 1) * NZ]
        for q in range(NX):
            plane = apply_left(y_fwd[...], lines[pl.ds(q, NY, stride=NX), :])
            high, low = split(plane)
            high_rows[q * NY : (q + 1) * NY, :] = high
            low_rows[q * NY : (q + 1) * NY, :] = low
        spectrum = apply_rows(z_fwd[...], high_rows[...], low_rows[...])
        weighted = spectrum * table[...]
        products = jnp.sum(spectrum * weighted, axis=0, keepdims=True)
        folded = products[:, :128]
        for start in range(128, NX * NY, 128):
            folded = folded + products[:, start : start + 128]
        energy_out[...] = energy_in[...] + request_weight * folded
        spectrum = apply_left(z_inv[...], weighted)
        for q in range(NX):
            high, low = split(spectrum[:, q * NY : (q + 1) * NY])
            high_rows[q * NZ : (q + 1) * NZ, :] = high
            low_rows[q * NZ : (q + 1) * NZ, :] = low
        spectrum = apply_rows(y_inv[...], high_rows[...], low_rows[...])
        for q in range(NX):
            lines[q * NY : (q + 1) * NY, :] = spectrum[:, q * NZ : (q + 1) * NZ]
        for y in range(NY):
            field[:, y * NZ : (y + 1) * NZ] = apply_left(
                x_inv[...], lines[pl.ds(y, NX, stride=NY), :]
            )
        store_force(
            force_refs, force_in[...] - (exchange_mix * total_weight) * (field[...] * other)
        )


def piece_shape(planes):
    fold = fold_of(planes, NY * NZ)
    return (planes * fold, NY * NZ // fold)


def pair_step(slot, weights, own, other, tables, force, energy, pieces=1):
    piece = force.shape if pieces == 1 else piece_shape(NX // pieces)
    outs = [jax.ShapeDtypeStruct(energy.shape, jnp.float32)]
    outs += [jax.ShapeDtypeStruct(piece, jnp.float32)] * pieces
    return pl.pallas_call(
        functools.partial(pair_kernel, slot),
        out_shape=outs,
        in_specs=in_vmem(5 + len(tables)),
        out_specs=in_vmem(1 + pieces),
        scratch_shapes=[
            pltpu.VMEM((NX * NY, NZ), jnp.float32),
            pltpu.VMEM((NX * NY, NZ), jnp.bfloat16),
            pltpu.VMEM((NX * NY, NZ), jnp.bfloat16),
            pltpu.VMEM((NX, NY * NZ), jnp.float32),
        ],
        input_output_aliases={3 + len(tables): 1} if pieces == 1 else {},
        compiler_params=pltpu.CompilerParams(vmem_limit_bytes=32 << 20),
        cost_estimate=pl.CostEstimate(flops=3 << 30, transcendentals=0, bytes_accessed=3 << 20),
        name="pair_step",
    )(weights, own, other, *tables, force, energy)


def fold_of(planes, cells):
    return 2 if (2 * planes) % 8 == 0 and cells % 256 == 0 else 1


def in_vmem(count):
    return [pl.BlockSpec(memory_space=pltpu.VMEM)] * count


def with_scalar(count):
    return [pl.BlockSpec(memory_space=pltpu.SMEM)] + in_vmem(count)


def pick(place, choices):
    chosen = choices[0]
    for index in range(1, len(choices)):
        chosen = jnp.where(place == index, choices[index], chosen)
    return chosen


def prepare_kernel(fold, place, orbitals, *out_refs):
    planes, slabs, cells = orbitals.shape
    part = cells // fold
    for f in range(fold):
        rows = slice(f * planes, (f + 1) * planes)
        blocks = [orbitals[:, j, f * part : (f + 1) * part] for j in range(slabs)]
        for r in range(slabs):
            out_refs[r][rows, :] = pick(place[0] ^ r, blocks)


def prepare(place, orbitals):
    planes, slabs, cells = orbitals.shape
    fold = fold_of(planes, cells)
    piece = jax.ShapeDtypeStruct((planes * fold, cells // fold), jnp.float32)
    return pl.pallas_call(
        functools.partial(prepare_kernel, fold),
        out_shape=[piece] * slabs,
        in_specs=with_scalar(1),
        out_specs=in_vmem(slabs),
        compiler_params=pltpu.CompilerParams(vmem_limit_bytes=8 << 20),
        name="prepare",
    )(place, orbitals)


def assemble_kernel(fold, *refs):
    out_ref = refs[-1]
    planes = refs[0].shape[0] // fold
    part = refs[0].shape[1]
    for r, ref in enumerate(refs[:-1]):
        for f in range(fold):
            out_ref[r * planes : (r + 1) * planes, f * part : (f + 1) * part] = ref[
                f * planes : (f + 1) * planes, :
            ]


def assemble(pieces):
    rows, part = pieces[0].shape
    fold = NY * NZ // part
    return pl.pallas_call(
        functools.partial(assemble_kernel, fold),
        out_shape=jax.ShapeDtypeStruct((rows // fold * len(pieces), NY * NZ), jnp.float32),
        in_specs=in_vmem(len(pieces)),
        out_specs=in_vmem(1)[0],
        compiler_params=pltpu.CompilerParams(vmem_limit_bytes=8 << 20),
        name="assemble",
    )(*pieces)


def clear_kernel(out_ref):
    out_ref[...] = jnp.zeros_like(out_ref)


def clear(shape):
    return pl.pallas_call(
        clear_kernel,
        out_shape=jax.ShapeDtypeStruct(shape, jnp.float32),
        out_specs=in_vmem(1)[0],
        compiler_params=pltpu.CompilerParams(vmem_limit_bytes=8 << 20),
        name="clear",
    )()


def squares_kernel(*refs):
    *blocks, even_ref, odd_ref = refs
    slabs = 2 * even_ref.shape[0]
    squares = blocks[0][...] * blocks[0][...]
    for ref in blocks[1:]:
        squares = squares + ref[...] * ref[...]
    pieces = [ref.at[k] for k in range(slabs // 2) for ref in (even_ref, odd_ref)]
    cut_into(pieces, squares)


def squares_of(blocks, slabs):
    stack = jax.ShapeDtypeStruct((slabs // 2,) + piece_shape(NX // slabs), jnp.float32)
    return pl.pallas_call(
        squares_kernel,
        out_shape=[stack, stack],
        in_specs=in_vmem(len(blocks)),
        out_specs=in_vmem(2),
        compiler_params=pltpu.CompilerParams(vmem_limit_bytes=8 << 20),
        name="squares",
    )(*blocks)


def pack_kernel(k, piece, mine, theirs, out_ref):
    rows = piece.shape[0]
    out_ref[:rows, :] = piece[...]
    out_ref[rows:, :] = mine[k] + theirs[k]


def pack(k, piece, mine, theirs):
    rows, part = piece.shape
    return pl.pallas_call(
        functools.partial(pack_kernel, k),
        out_shape=jax.ShapeDtypeStruct((2 * rows, part), jnp.float32),
        in_specs=in_vmem(3),
        out_specs=in_vmem(1)[0],
        compiler_params=pltpu.CompilerParams(vmem_limit_bytes=8 << 20),
        name="pack",
    )(piece, mine, theirs)


def join_kernel(*refs):
    out_ref = refs[-1]
    first = 0
    for ref in refs[:-1]:
        out_ref[first : first + ref.shape[0], :] = ref[...]
        first += ref.shape[0]


def join(*parts):
    rows = sum(part.shape[0] for part in parts)
    return pl.pallas_call(
        join_kernel,
        out_shape=jax.ShapeDtypeStruct((rows,) + parts[0].shape[1:], jnp.float32),
        in_specs=in_vmem(len(parts)),
        out_specs=in_vmem(1)[0],
        compiler_params=pltpu.CompilerParams(vmem_limit_bytes=8 << 20),
        name="join",
    )(*parts)


def finish_kernel(fold, place, orbitals, local_pot, *refs):
    out_ref = refs[-1]
    planes, slabs, cells = orbitals.shape
    part = cells // fold
    for f in range(fold):
        rows = slice(f * planes, (f + 1) * planes)
        cols = slice(f * part, (f + 1) * part)
        pieces = [ref[rows, :] for ref in refs[:-1]]
        local = local_pot[rows, :]
        for j in range(slabs):
            out_ref[:, j, cols] = local * orbitals[:, j, cols] + pick(place[0] ^ j, pieces)


def finish(place, orbitals, local_pot, pieces):
    planes, _, cells = orbitals.shape
    return pl.pallas_call(
        functools.partial(finish_kernel, fold_of(planes, cells)),
        out_shape=jax.ShapeDtypeStruct(orbitals.shape, jnp.float32),
        in_specs=with_scalar(2 + len(pieces)),
        out_specs=in_vmem(1)[0],
        compiler_params=pltpu.CompilerParams(vmem_limit_bytes=8 << 20),
        name="finish",
    )(place, orbitals, local_pot, *pieces)


def slab_swap(value, reach):
    size = lax.axis_size("slab")
    return lax.ppermute(value, "slab", [(i, i ^ reach) for i in range(size)])


def share(value, devices):
    sent = jnp.broadcast_to(value[None], (devices,) + value.shape)
    return lax.all_to_all(sent, ("band", "slab"), 0, 0)


def gather_ring(halves, band_index, bands):
    groups = [2 * p if p < bands // 2 else 2 * (bands - 1 - p) + 1 for p in range(bands)]
    place = band_index // 2
    position = jnp.where(band_index % 2 == 0, place, bands - 1 - place)

    def group_at(position):
        position = position % bands
        return jnp.where(position < bands // 2, 2 * position, 2 * (bands - 1 - position) + 1)

    def shift(value, by):
        moves = [(groups[p], groups[(p + by) % bands]) for p in range(bands)]
        return lax.ppermute(value, "band", moves)

    came = [(shift(half, 1), shift(half, -1)) for half in halves]
    blocks = []
    steps = bands // 2 - 1
    for step in range(steps):
        if step == 0:
            ahead, behind = (join(*pair) for pair in zip(*came))
        else:
            ahead = shift(ahead, 1)
            behind = shift(behind, -1)
        blocks.append((ahead, group_at(position - step - 1)))
        blocks.append((behind, group_at(position + step + 1)))
    half = ahead.shape[0] // 2
    head = shift(ahead[:half], 1)
    tail = shift(behind[half:], -1)
    blocks.append((join(head, tail), group_at(position + steps + 1)))
    return blocks


def body(orbitals, partners, counts):
    bands = lax.axis_size("band")
    slabs = lax.axis_size("slab")
    band_index = lax.axis_index("band")
    slab_index = lax.axis_index("slab")
    orb_group, _, _ = orbitals.shape
    total_orbs = orb_group * bands
    assert orb_group == slabs

    place = slab_index.astype(jnp.int32).reshape(1)
    by_plane = jnp.transpose(orbitals, (1, 0, 2))
    sends = prepare(place, by_plane)
    pieces = [sends[0]] + [slab_swap(sends[r], r) for r in range(1, slabs)]
    halves = [assemble(pieces[: slabs // 2]), assemble(pieces[slabs // 2 :])]
    own = join(*halves)
    others = gather_ring(halves, band_index, bands)
    force = clear((NX, NY * NZ))

    own, partners, counts = lax.optimization_barrier((own, partners, counts))
    tables = transform_tables(slab_index, slabs)

    groups = jnp.stack([group for _, group in others]).astype(jnp.int32)
    active = (slab_index < counts).astype(jnp.float32)
    mine = jnp.arange(bands, dtype=jnp.int32)[:, None] == band_index
    my_partners = jnp.sum(jnp.where(mine, partners, 0), axis=0)
    my_active = jnp.sum(jnp.where(mine, active, 0.0), axis=0)
    requested = jnp.sum(
        jnp.where(groups[:, None] == my_partners[None, :], my_active[None, :], 0.0), axis=1
    )
    wanted_by = jnp.sum(jnp.where(partners == band_index, active, 0.0), axis=1)
    chosen = groups[:, None] == jnp.arange(bands, dtype=jnp.int32)[None, :]
    returned = jnp.sum(jnp.where(chosen, wanted_by[None, :], 0.0), axis=1)
    weights = jnp.stack([requested + returned, requested], axis=1).reshape(-1)
    weights = jnp.broadcast_to(weights[:, None], weights.shape + (128,))

    energy = jnp.zeros((1, 128), jnp.float32)
    even, odd = squares_of([own] + [other for other, _ in others], slabs)
    from_core = slab_swap(odd, 1)
    for slot, (other, _) in enumerate(others):
        if slot < len(others) - 1:
            energy, force = pair_step(slot, weights, own, other, tables, force, energy)
        else:
            energy, *outgoing = pair_step(slot, weights, own, other, tables, force, energy, slabs)

    for r in range(2, slabs, 2):
        outgoing[r] = pack(r // 2, outgoing[r], even, from_core)
    arrived = [outgoing[0]] + [slab_swap(outgoing[r], r) for r in range(1, slabs)]
    shared = share(energy, bands * slabs)
    rows = arrived[0].shape[0]
    squares = even[0] + from_core[0] + sum(arrived[r][rows:] for r in range(2, slabs, 2))
    density = 2.0 / total_orbs * squares
    local_pot = slater_coeff * jnp.cbrt(density)
    forces = finish(place, by_plane, local_pot, arrived)
    energy_total = jnp.sum(shared)
    return (
        jnp.transpose(forces, (1, 0, 2)),
        -energy_total / (2.0 * total_orbs * NX * NY * NZ),
    )


def solution(mesh):
    placed = (P("band", "slab", None), P(), P())
    return jax.shard_map(
        body, mesh=mesh, in_specs=placed, out_specs=(P("band", "slab", None), P()), check_vma=False
    )
```

```python
import functools
import math

import jax
import jax.numpy as jnp
import ml_dtypes
import numpy as np
from jax import lax
from jax.experimental import pallas as pl
from jax.experimental.pallas import tpu as pltpu
from jax.sharding import PartitionSpec as P


NX = 48
NY = 48
NZ = 48
NZP = 96


slater_coeff = -((3.0 / math.pi) ** (1.0 / 3.0))
exchange_mix = 0.25
screening = 0.25
row_row = (((1,), (1,)), ((), ()))


def split(value):
    high = value.astype(jnp.bfloat16)
    low = (value - high.astype(jnp.float32)).astype(jnp.bfloat16)
    return high, low


def cas(rows, cols, length):
    phase_angle = 2.0 * math.pi / length * (np.outer(rows, cols) % length)
    return np.cos(phase_angle) + np.sin(phase_angle)


def split_table(matrix):
    high = matrix.astype(ml_dtypes.bfloat16)
    return high, (matrix - high.astype(np.float64)).astype(ml_dtypes.bfloat16)


def wide(matrix):
    high, low = split_table(matrix)
    return np.concatenate([high, high, low], axis=1)


def tall(matrix):
    high, low = split_table(matrix)
    return np.concatenate([high, low], axis=0)


def wavenumber_sq(length):
    return (2.0 * np.pi * np.fft.fftfreq(length)) ** 2


def transform_tables(slab_index, slabs):
    x_waves, y_cells, z_cells, z_waves = (np.arange(count) for count in (NX, NY, NZ, NZP))
    planes = NX // slabs
    held_x = [(slab ^ (x_waves // planes)) * planes + x_waves % planes for slab in range(slabs)]
    total = (
        wavenumber_sq(NZP)[:, None, None]
        + wavenumber_sq(NX)[None, :, None]
        + wavenumber_sq(NY)[None, None, :]
    )
    kernel_table = 4.0 * math.pi / (NX * NY * NZP) / (total + screening * screening)
    y_matrix = cas(y_cells, y_cells, NY)
    forward = jnp.asarray(np.stack([wide(cas(x_waves, held, NX)) for held in held_x]))
    backward = jnp.asarray(np.stack([wide(cas(held, x_waves, NX)) for held in held_x]))
    return (
        lax.dynamic_index_in_dim(forward, slab_index, 0, keepdims=False),
        jnp.asarray(wide(y_matrix)),
        jnp.asarray(tall(cas(z_waves, z_cells, NZP))),
        jnp.asarray(kernel_table.reshape(NZP, NX * NY).astype(np.float32)),
        jnp.asarray(wide(cas(z_cells, z_waves, NZP))),
        jnp.asarray(tall(y_matrix)),
        lax.dynamic_index_in_dim(backward, slab_index, 0, keepdims=False),
    )


def apply_left(matrix, value):
    high, low = split(value)
    stacked = jnp.concatenate([high, low, high], axis=0)
    return jnp.dot(matrix, stacked, preferred_element_type=jnp.float32)


def apply_rows(matrix, high, low):
    half = matrix.shape[0] // 2
    both = lax.dot_general(matrix, high, row_row, preferred_element_type=jnp.float32)
    rest = lax.dot_general(matrix[:half], low, row_row, preferred_element_type=jnp.float32)
    return both[:half] + both[half:] + rest


def cut_into(refs, value):
    planes = NX // len(refs)
    part = refs[0].shape[1]
    fold = NY * NZ // part
    for r, ref in enumerate(refs):
        for f in range(fold):
            ref[f * planes : (f + 1) * planes, :] = value[
                r * planes : (r + 1) * planes, f * part : (f + 1) * part
            ]


def store_force(force_refs, value):
    if len(force_refs) == 1:
        force_refs[0][...] = value
    else:
        cut_into(force_refs, value)


def pair_kernel(
    slot, weights, own_ref, other_ref, x_fwd, y_fwd, z_fwd, table, z_inv, y_inv, x_inv,
    force_in, energy_in, *refs,
):
    energy_out, *force_refs, lines, high_rows, low_rows, field = refs
    total_weight = jnp.max(weights[2 * slot : 2 * slot + 1, :])
    request_weight = weights[2 * slot + 1 : 2 * slot + 2, :]

    @pl.when(total_weight == 0.0)
    def _():
        energy_out[...] = jnp.broadcast_to(energy_in[...], energy_out.shape)
        if len(force_refs) > 1:
            store_force(force_refs, force_in[...])

    @pl.when(total_weight != 0.0)
    def _():
        other = other_ref[...]
        density = own_ref[...] * other
        spectrum = apply_left(x_fwd[...], density)
        for y in range(NY):
            lines[y * NX : (y + 1) * NX, :] = spectrum[:, y * NZ : (y + 1) * NZ]
        for q in range(NX):
            plane = apply_left(y_fwd[...], lines[pl.ds(q, NY, stride=NX), :])
            high, low = split(plane)
            high_rows[q * NY : (q + 1) * NY, :] = high
            low_rows[q * NY : (q + 1) * NY, :] = low
        spectrum = apply_rows(z_fwd[...], high_rows[...], low_rows[...])
        weighted = spectrum * table[...]
        products = jnp.sum(spectrum * weighted, axis=0, keepdims=True)
        folded = products[:, :128]
        for start in range(128, NX * NY, 128):
            folded = folded + products[:, start : start + 128]
        energy_out[...] = jnp.broadcast_to(
            energy_in[...] + request_weight * folded, energy_out.shape
        )
        spectrum = apply_left(z_inv[...], weighted)
        for q in range(NX):
            high, low = split(spectrum[:, q * NY : (q + 1) * NY])
            high_rows[q * NZ : (q + 1) * NZ, :] = high
            low_rows[q * NZ : (q + 1) * NZ, :] = low
        spectrum = apply_rows(y_inv[...], high_rows[...], low_rows[...])
        for q in range(NX):
            lines[q * NY : (q + 1) * NY, :] = spectrum[:, q * NZ : (q + 1) * NZ]
        for y in range(NY):
            field[:, y * NZ : (y + 1) * NZ] = apply_left(
                x_inv[...], lines[pl.ds(y, NX, stride=NY), :]
            )
        store_force(
            force_refs, force_in[...] - (exchange_mix * total_weight) * (field[...] * other)
        )


def piece_shape(planes):
    fold = fold_of(planes, NY * NZ)
    return (planes * fold, NY * NZ // fold)


def pair_step(slot, weights, own, other, tables, force, energy, pieces=1, copies=None):
    piece = force.shape if pieces == 1 else piece_shape(NX // pieces)
    energy_shape = energy.shape if copies is None else (copies,) + energy.shape
    outs = [jax.ShapeDtypeStruct(energy_shape, jnp.float32)]
    outs += [jax.ShapeDtypeStruct(piece, jnp.float32)] * pieces
    return pl.pallas_call(
        functools.partial(pair_kernel, slot),
        out_shape=outs,
        in_specs=in_vmem(5 + len(tables)),
        out_specs=in_vmem(1 + pieces),
        scratch_shapes=[
            pltpu.VMEM((NX * NY, NZ), jnp.float32),
            pltpu.VMEM((NX * NY, NZ), jnp.bfloat16),
            pltpu.VMEM((NX * NY, NZ), jnp.bfloat16),
            pltpu.VMEM((NX, NY * NZ), jnp.float32),
        ],
        input_output_aliases={3 + len(tables): 1} if pieces == 1 else {},
        compiler_params=pltpu.CompilerParams(vmem_limit_bytes=32 << 20),
        cost_estimate=pl.CostEstimate(flops=3 << 30, transcendentals=0, bytes_accessed=3 << 20),
        name="pair_step",
    )(weights, own, other, *tables, force, energy)


def fold_of(planes, cells):
    return 2 if (2 * planes) % 8 == 0 and cells % 256 == 0 else 1


def in_vmem(count):
    return [pl.BlockSpec(memory_space=pltpu.VMEM)] * count


def with_scalar(count):
    return [pl.BlockSpec(memory_space=pltpu.SMEM)] + in_vmem(count)


def pick(place, choices):
    chosen = choices[0]
    for index in range(1, len(choices)):
        chosen = jnp.where(place == index, choices[index], chosen)
    return chosen


def prepare_kernel(fold, place, orbitals, *out_refs):
    planes, slabs, cells = orbitals.shape
    part = cells // fold
    for f in range(fold):
        rows = slice(f * planes, (f + 1) * planes)
        blocks = [orbitals[:, j, f * part : (f + 1) * part] for j in range(slabs)]
        for r in range(slabs):
            out_refs[r][rows, :] = pick(place[0] ^ r, blocks)


def prepare(place, orbitals):
    planes, slabs, cells = orbitals.shape
    fold = fold_of(planes, cells)
    piece = jax.ShapeDtypeStruct((planes * fold, cells // fold), jnp.float32)
    return pl.pallas_call(
        functools.partial(prepare_kernel, fold),
        out_shape=[piece] * slabs,
        in_specs=with_scalar(1),
        out_specs=in_vmem(slabs),
        compiler_params=pltpu.CompilerParams(vmem_limit_bytes=8 << 20),
        name="prepare",
    )(place, orbitals)


def assemble_kernel(fold, *refs):
    out_ref = refs[-1]
    planes = refs[0].shape[0] // fold
    part = refs[0].shape[1]
    for r, ref in enumerate(refs[:-1]):
        for f in range(fold):
            out_ref[r * planes : (r + 1) * planes, f * part : (f + 1) * part] = ref[
                f * planes : (f + 1) * planes, :
            ]


def assemble(pieces):
    rows, part = pieces[0].shape
    fold = NY * NZ // part
    return pl.pallas_call(
        functools.partial(assemble_kernel, fold),
        out_shape=jax.ShapeDtypeStruct((rows // fold * len(pieces), NY * NZ), jnp.float32),
        in_specs=in_vmem(len(pieces)),
        out_specs=in_vmem(1)[0],
        compiler_params=pltpu.CompilerParams(vmem_limit_bytes=8 << 20),
        name="assemble",
    )(*pieces)


def clear_kernel(out_ref):
    out_ref[...] = jnp.zeros_like(out_ref)


def clear(shape):
    return pl.pallas_call(
        clear_kernel,
        out_shape=jax.ShapeDtypeStruct(shape, jnp.float32),
        out_specs=in_vmem(1)[0],
        compiler_params=pltpu.CompilerParams(vmem_limit_bytes=8 << 20),
        name="clear",
    )()


def squares_kernel(*refs):
    *blocks, even_ref, odd_ref = refs
    slabs = 2 * even_ref.shape[0]
    squares = blocks[0][...] * blocks[0][...]
    for ref in blocks[1:]:
        squares = squares + ref[...] * ref[...]
    pieces = [ref.at[k] for k in range(slabs // 2) for ref in (even_ref, odd_ref)]
    cut_into(pieces, squares)


def squares_of(blocks, slabs):
    stack = jax.ShapeDtypeStruct((slabs // 2,) + piece_shape(NX // slabs), jnp.float32)
    return pl.pallas_call(
        squares_kernel,
        out_shape=[stack, stack],
        in_specs=in_vmem(len(blocks)),
        out_specs=in_vmem(2),
        compiler_params=pltpu.CompilerParams(vmem_limit_bytes=8 << 20),
        name="squares",
    )(*blocks)


def pack_kernel(k, piece, mine, theirs, out_ref):
    rows = piece.shape[0]
    out_ref[:rows, :] = piece[...]
    out_ref[rows:, :] = mine[k] + theirs[k]


def pack(k, piece, mine, theirs):
    rows, part = piece.shape
    return pl.pallas_call(
        functools.partial(pack_kernel, k),
        out_shape=jax.ShapeDtypeStruct((2 * rows, part), jnp.float32),
        in_specs=in_vmem(3),
        out_specs=in_vmem(1)[0],
        compiler_params=pltpu.CompilerParams(vmem_limit_bytes=8 << 20),
        name="pack",
    )(piece, mine, theirs)


def join_kernel(*refs):
    out_ref = refs[-1]
    first = 0
    for ref in refs[:-1]:
        out_ref[first : first + ref.shape[0], :] = ref[...]
        first += ref.shape[0]


def join(*parts):
    rows = sum(part.shape[0] for part in parts)
    return pl.pallas_call(
        join_kernel,
        out_shape=jax.ShapeDtypeStruct((rows,) + parts[0].shape[1:], jnp.float32),
        in_specs=in_vmem(len(parts)),
        out_specs=in_vmem(1)[0],
        compiler_params=pltpu.CompilerParams(vmem_limit_bytes=8 << 20),
        name="join",
    )(*parts)


def finish_kernel(fold, place, orbitals, local_pot, *refs):
    out_ref = refs[-1]
    planes, slabs, cells = orbitals.shape
    part = cells // fold
    for f in range(fold):
        rows = slice(f * planes, (f + 1) * planes)
        cols = slice(f * part, (f + 1) * part)
        pieces = [ref[rows, :] for ref in refs[:-1]]
        local = local_pot[rows, :]
        for j in range(slabs):
            out_ref[:, j, cols] = local * orbitals[:, j, cols] + pick(place[0] ^ j, pieces)


def finish(place, orbitals, local_pot, pieces):
    planes, _, cells = orbitals.shape
    return pl.pallas_call(
        functools.partial(finish_kernel, fold_of(planes, cells)),
        out_shape=jax.ShapeDtypeStruct(orbitals.shape, jnp.float32),
        in_specs=with_scalar(2 + len(pieces)),
        out_specs=in_vmem(1)[0],
        compiler_params=pltpu.CompilerParams(vmem_limit_bytes=8 << 20),
        name="finish",
    )(place, orbitals, local_pot, *pieces)


def slab_swap(value, reach):
    size = lax.axis_size("slab")
    return lax.ppermute(value, "slab", [(i, i ^ reach) for i in range(size)])


def total_kernel(scale, shared, out_ref):
    summed = jnp.sum(shared[...], axis=0)
    out_ref[...] = scale * jnp.sum(summed, axis=1, keepdims=True)


def total_of(shared, scale):
    return pl.pallas_call(
        functools.partial(total_kernel, scale),
        out_shape=jax.ShapeDtypeStruct((1, 1), jnp.float32),
        in_specs=in_vmem(1),
        out_specs=in_vmem(1)[0],
        compiler_params=pltpu.CompilerParams(vmem_limit_bytes=8 << 20),
        name="total",
    )(shared)


def gather_ring(halves, band_index, bands):
    groups = [2 * p if p < bands // 2 else 2 * (bands - 1 - p) + 1 for p in range(bands)]
    place = band_index // 2
    position = jnp.where(band_index % 2 == 0, place, bands - 1 - place)

    def group_at(position):
        position = position % bands
        return jnp.where(position < bands // 2, 2 * position, 2 * (bands - 1 - position) + 1)

    def shift(value, by):
        moves = [(groups[p], groups[(p + by) % bands]) for p in range(bands)]
        return lax.ppermute(value, "band", moves)

    came = [(shift(half, 1), shift(half, -1)) for half in halves]
    blocks = []
    steps = bands // 2 - 1
    for step in range(steps):
        if step == 0:
            ahead, behind = (join(*pair) for pair in zip(*came))
        else:
            ahead = shift(ahead, 1)
            behind = shift(behind, -1)
        blocks.append((ahead, group_at(position - step - 1)))
        blocks.append((behind, group_at(position + step + 1)))
    half = ahead.shape[0] // 2
    head = shift(ahead[:half], 1)
    tail = shift(behind[half:], -1)
    blocks.append((join(head, tail), group_at(position + steps + 1)))
    return blocks


def body(orbitals, partners, counts):
    bands = lax.axis_size("band")
    slabs = lax.axis_size("slab")
    band_index = lax.axis_index("band")
    slab_index = lax.axis_index("slab")
    orb_group, _, _ = orbitals.shape
    total_orbs = orb_group * bands
    assert orb_group == slabs

    place = slab_index.astype(jnp.int32).reshape(1)
    by_plane = jnp.transpose(orbitals, (1, 0, 2))
    sends = prepare(place, by_plane)
    pieces = [sends[0]] + [slab_swap(sends[r], r) for r in range(1, slabs)]
    halves = [assemble(pieces[: slabs // 2]), assemble(pieces[slabs // 2 :])]
    own = join(*halves)
    others = gather_ring(halves, band_index, bands)
    force = clear((NX, NY * NZ))

    own, partners, counts = lax.optimization_barrier((own, partners, counts))
    tables = transform_tables(slab_index, slabs)

    groups = jnp.stack([group for _, group in others]).astype(jnp.int32)
    active = (slab_index < counts).astype(jnp.float32)
    mine = jnp.arange(bands, dtype=jnp.int32)[:, None] == band_index
    my_partners = jnp.sum(jnp.where(mine, partners, 0), axis=0)
    my_active = jnp.sum(jnp.where(mine, active, 0.0), axis=0)
    requested = jnp.sum(
        jnp.where(groups[:, None] == my_partners[None, :], my_active[None, :], 0.0), axis=1
    )
    wanted_by = jnp.sum(jnp.where(partners == band_index, active, 0.0), axis=1)
    chosen = groups[:, None] == jnp.arange(bands, dtype=jnp.int32)[None, :]
    returned = jnp.sum(jnp.where(chosen, wanted_by[None, :], 0.0), axis=1)
    weights = jnp.stack([requested + returned, requested], axis=1).reshape(-1)
    weights = jnp.broadcast_to(weights[:, None], weights.shape + (128,))

    energy = jnp.zeros((1, 128), jnp.float32)
    even, odd = squares_of([own] + [other for other, _ in others], slabs)
    from_core = slab_swap(odd, 1)
    for slot, (other, _) in enumerate(others):
        if slot < len(others) - 1:
            energy, force = pair_step(slot, weights, own, other, tables, force, energy)
        else:
            energy, *outgoing = pair_step(
                slot, weights, own, other, tables, force, energy, slabs, bands * slabs
            )

    for r in range(2, slabs, 2):
        outgoing[r] = pack(r // 2, outgoing[r], even, from_core)
    arrived = [outgoing[0]] + [slab_swap(outgoing[r], r) for r in range(1, slabs)]
    shared = lax.all_to_all(energy, ("band", "slab"), 0, 0)
    rows = arrived[0].shape[0]
    squares = even[0] + from_core[0] + sum(arrived[r][rows:] for r in range(2, slabs, 2))
    density = 2.0 / total_orbs * squares
    local_pot = slater_coeff * jnp.cbrt(density)
    forces = finish(place, by_plane, local_pot, arrived)
    total = total_of(shared, -1.0 / (2.0 * total_orbs * NX * NY * NZ))
    return jnp.transpose(forces, (1, 0, 2)), total.reshape(())


def solution(mesh):
    placed = (P("band", "slab", None), P(), P())
    return jax.shard_map(
        body, mesh=mesh, in_specs=placed, out_specs=(P("band", "slab", None), P()), check_vma=False
    )
```

```python
import functools
import math

import jax
import jax.numpy as jnp
import ml_dtypes
import numpy as np
from jax import lax
from jax.experimental import pallas as pl
from jax.experimental.pallas import tpu as pltpu
from jax.sharding import PartitionSpec as P


NX = 48
NY = 48
NZ = 48
NZP = 96
SIDE_X = NX // 2
GAP = 64


slater_coeff = -((3.0 / math.pi) ** (1.0 / 3.0))
exchange_mix = 0.25
screening = 0.25
row_row = (((1,), (1,)), ((), ()))


def split(value):
    high = value.astype(jnp.bfloat16)
    low = (value - high.astype(jnp.float32)).astype(jnp.bfloat16)
    return high, low


def cas(rows, cols, length):
    phase_angle = 2.0 * math.pi / length * (np.outer(rows, cols) % length)
    return np.cos(phase_angle) + np.sin(phase_angle)


def split_table(matrix):
    high = matrix.astype(ml_dtypes.bfloat16)
    return high, (matrix - high.astype(np.float64)).astype(ml_dtypes.bfloat16)


def wide(matrix):
    high, low = split_table(matrix)
    return np.concatenate([high, high, low], axis=1)


def tall(matrix):
    rows, cols = matrix.shape
    placed = np.zeros((2 * rows, 2 * GAP))
    placed[:rows, :cols] = matrix
    placed[rows:, GAP : GAP + cols] = matrix
    return np.concatenate(split_table(placed), axis=0)


def wavenumber_sq(length):
    return (2.0 * np.pi * np.fft.fftfreq(length)) ** 2


def transform_tables(slab_index, slabs):
    x_waves, y_cells, z_cells, z_waves = (np.arange(count) for count in (NX, NY, NZ, NZP))
    planes = NX // slabs
    held_x = [(slab ^ (x_waves // planes)) * planes + x_waves % planes for slab in range(slabs)]
    total = (
        wavenumber_sq(NZP)[:, None, None]
        + wavenumber_sq(NX)[None, :, None]
        + wavenumber_sq(NY)[None, None, :]
    )
    kernel_table = 4.0 * math.pi / (NX * NY * NZP) / (total + screening * screening)
    y_matrix = cas(y_cells, y_cells, NY)
    forward = jnp.asarray(np.stack([wide(cas(x_waves, held, NX)) for held in held_x]))
    quads = 4 * (x_waves[:SIDE_X] // 2) + x_waves[:SIDE_X] % 2
    kept = np.concatenate([quads, quads + 2])
    backward = jnp.asarray(np.stack([wide(cas(held, kept, NX)) for held in held_x]))
    kernel_table = np.pad(kernel_table, ((0, 0), (0, 0), (0, GAP - NY)))
    return (
        lax.dynamic_index_in_dim(forward, slab_index, 0, keepdims=False),
        jnp.asarray(wide(y_matrix)),
        jnp.asarray(tall(cas(z_waves, z_cells, NZP))),
        jnp.asarray(kernel_table.reshape(NZP, NX * GAP).astype(np.float32)),
        jnp.asarray(wide(cas(z_cells, z_waves, NZP))),
        jnp.asarray(tall(y_matrix)),
        lax.dynamic_index_in_dim(backward, slab_index, 0, keepdims=False),
    )


def apply_left(matrix, value):
    high, low = split(value)
    stacked = jnp.concatenate([high, low, high], axis=0)
    return jnp.dot(matrix, stacked, preferred_element_type=jnp.float32)


def apply_rows(matrix, high, low):
    half = matrix.shape[0] // 2
    both = lax.dot_general(matrix, high, row_row, preferred_element_type=jnp.float32)
    rest = lax.dot_general(matrix[:half], low, row_row, preferred_element_type=jnp.float32)
    return both[:half] + both[half:] + rest


def cut_into(refs, value):
    planes = NX // len(refs)
    part = refs[0].shape[1]
    fold = NY * NZ // part
    for r, ref in enumerate(refs):
        for f in range(fold):
            ref[f * planes : (f + 1) * planes, :] = value[
                r * planes : (r + 1) * planes, f * part : (f + 1) * part
            ]


def store_force(force_refs, value):
    if len(force_refs) == 1:
        force_refs[0][...] = value
    else:
        cut_into(force_refs, value)


def pair_kernel(
    slot, weights, own_ref, other_ref, x_fwd, y_fwd, z_fwd, table, z_inv, y_inv, x_inv,
    force_in, energy_in, *refs,
):
    energy_out, *force_refs, lines, high_rows, low_rows, field = refs
    total_weight = jnp.max(weights[2 * slot : 2 * slot + 1, :])
    request_weight = weights[2 * slot + 1 : 2 * slot + 2, :]

    @pl.when(total_weight == 0.0)
    def _():
        energy_out[...] = jnp.broadcast_to(energy_in[...], energy_out.shape)
        if len(force_refs) > 1:
            store_force(force_refs, force_in[...])

    @pl.when(total_weight != 0.0)
    def _():
        other = other_ref[...]
        density = own_ref[...] * other
        spectrum = apply_left(x_fwd[...], density)
        lines[...] = jnp.zeros_like(lines)
        for y in range(NY):
            rows = slice(y * SIDE_X, (y + 1) * SIDE_X)
            cols = slice(y * NZ, (y + 1) * NZ)
            lines[rows, :NZ] = spectrum[:SIDE_X, cols]
            lines[rows, GAP : GAP + NZ] = spectrum[SIDE_X:, cols]
        for q in range(SIDE_X):
            plane = apply_left(y_fwd[...], lines[pl.ds(q, NY, stride=SIDE_X), :])
            high, low = split(plane)
            rows = slice(q * GAP, q * GAP + NY)
            pad = slice(q * GAP + NY, (q + 1) * GAP)
            high_rows[rows, :] = high
            low_rows[rows, :] = low
            high_rows[pad, :] = jnp.zeros((GAP - NY, 2 * GAP), jnp.bfloat16)
            low_rows[pad, :] = jnp.zeros((GAP - NY, 2 * GAP), jnp.bfloat16)
        both = apply_rows(z_fwd[...], high_rows[...], low_rows[...])
        width = SIDE_X * GAP
        inner = []
        folded = jnp.zeros((1, 128), jnp.float32)
        for side in range(2):
            spectrum = both[side * NZP : (side + 1) * NZP]
            weighted = spectrum * table[:, side * width : (side + 1) * width]
            products = jnp.sum(spectrum * weighted, axis=0, keepdims=True)
            for start in range(0, width, 128):
                folded = folded + products[:, start : start + 128]
            inner.append(apply_left(z_inv[...], weighted))
        energy_out[...] = jnp.broadcast_to(
            energy_in[...] + request_weight * folded, energy_out.shape
        )
        for side in range(2):
            for pair in range(SIDE_X // 2):
                high, low = split(inner[side][:, pair * 2 * GAP : (pair + 1) * 2 * GAP])
                first = (side * (SIDE_X // 2) + pair) * GAP
                high_rows[first : first + NZ, :] = high
                low_rows[first : first + NZ, :] = low
        both = apply_rows(y_inv[...], high_rows[...], low_rows[...])
        for odd in range(2):
            for pair in range(SIDE_X // 2):
                first = (2 * pair + odd) * NY
                lines[first : first + NY, :] = both[
                    odd * NY : (odd + 1) * NY, pair * 2 * GAP : (pair + 1) * 2 * GAP
                ]
        for y in range(NY):
            plane = lines[pl.ds(y, SIDE_X, stride=NY), :]
            cols = slice(y * NZ, (y + 1) * NZ)
            field[:SIDE_X, cols] = plane[:, :NZ]
            field[SIDE_X:, cols] = plane[:, GAP : GAP + NZ]
        potential = apply_left(x_inv[...], field[...])
        store_force(
            force_refs, force_in[...] - (exchange_mix * total_weight) * (potential * other)
        )


def piece_shape(planes):
    fold = fold_of(planes, NY * NZ)
    return (planes * fold, NY * NZ // fold)


def pair_step(slot, weights, own, other, tables, force, energy, pieces=1, copies=None):
    piece = force.shape if pieces == 1 else piece_shape(NX // pieces)
    energy_shape = energy.shape if copies is None else (copies,) + energy.shape
    outs = [jax.ShapeDtypeStruct(energy_shape, jnp.float32)]
    outs += [jax.ShapeDtypeStruct(piece, jnp.float32)] * pieces
    return pl.pallas_call(
        functools.partial(pair_kernel, slot),
        out_shape=outs,
        in_specs=in_vmem(5 + len(tables)),
        out_specs=in_vmem(1 + pieces),
        scratch_shapes=[
            pltpu.VMEM((SIDE_X * NY, 2 * GAP), jnp.float32),
            pltpu.VMEM((SIDE_X * GAP, 2 * GAP), jnp.bfloat16),
            pltpu.VMEM((SIDE_X * GAP, 2 * GAP), jnp.bfloat16),
            pltpu.VMEM((NX, NY * NZ), jnp.float32),
        ],
        input_output_aliases={3 + len(tables): 1} if pieces == 1 else {},
        compiler_params=pltpu.CompilerParams(vmem_limit_bytes=32 << 20),
        cost_estimate=pl.CostEstimate(flops=3 << 30, transcendentals=0, bytes_accessed=3 << 20),
        name="pair_step",
    )(weights, own, other, *tables, force, energy)


def fold_of(planes, cells):
    return 2 if (2 * planes) % 8 == 0 and cells % 256 == 0 else 1


def in_vmem(count):
    return [pl.BlockSpec(memory_space=pltpu.VMEM)] * count


def with_scalar(count):
    return [pl.BlockSpec(memory_space=pltpu.SMEM)] + in_vmem(count)


def pick(place, choices):
    chosen = choices[0]
    for index in range(1, len(choices)):
        chosen = jnp.where(place == index, choices[index], chosen)
    return chosen


def prepare_kernel(fold, place, orbitals, *out_refs):
    planes, slabs, cells = orbitals.shape
    part = cells // fold
    for f in range(fold):
        rows = slice(f * planes, (f + 1) * planes)
        blocks = [orbitals[:, j, f * part : (f + 1) * part] for j in range(slabs)]
        for r in range(slabs):
            out_refs[r][rows, :] = pick(place[0] ^ r, blocks)


def prepare(place, orbitals):
    planes, slabs, cells = orbitals.shape
    fold = fold_of(planes, cells)
    piece = jax.ShapeDtypeStruct((planes * fold, cells // fold), jnp.float32)
    return pl.pallas_call(
        functools.partial(prepare_kernel, fold),
        out_shape=[piece] * slabs,
        in_specs=with_scalar(1),
        out_specs=in_vmem(slabs),
        compiler_params=pltpu.CompilerParams(vmem_limit_bytes=8 << 20),
        name="prepare",
    )(place, orbitals)


def assemble_kernel(fold, *refs):
    out_ref = refs[-1]
    planes = refs[0].shape[0] // fold
    part = refs[0].shape[1]
    for r, ref in enumerate(refs[:-1]):
        for f in range(fold):
            out_ref[r * planes : (r + 1) * planes, f * part : (f + 1) * part] = ref[
                f * planes : (f + 1) * planes, :
            ]


def assemble(pieces):
    rows, part = pieces[0].shape
    fold = NY * NZ // part
    return pl.pallas_call(
        functools.partial(assemble_kernel, fold),
        out_shape=jax.ShapeDtypeStruct((rows // fold * len(pieces), NY * NZ), jnp.float32),
        in_specs=in_vmem(len(pieces)),
        out_specs=in_vmem(1)[0],
        compiler_params=pltpu.CompilerParams(vmem_limit_bytes=8 << 20),
        name="assemble",
    )(*pieces)


def clear_kernel(out_ref):
    out_ref[...] = jnp.zeros_like(out_ref)


def clear(shape):
    return pl.pallas_call(
        clear_kernel,
        out_shape=jax.ShapeDtypeStruct(shape, jnp.float32),
        out_specs=in_vmem(1)[0],
        compiler_params=pltpu.CompilerParams(vmem_limit_bytes=8 << 20),
        name="clear",
    )()


def squares_kernel(*refs):
    *blocks, even_ref, odd_ref = refs
    slabs = 2 * even_ref.shape[0]
    squares = blocks[0][...] * blocks[0][...]
    for ref in blocks[1:]:
        squares = squares + ref[...] * ref[...]
    pieces = [ref.at[k] for k in range(slabs // 2) for ref in (even_ref, odd_ref)]
    cut_into(pieces, squares)


def squares_of(blocks, slabs):
    stack = jax.ShapeDtypeStruct((slabs // 2,) + piece_shape(NX // slabs), jnp.float32)
    return pl.pallas_call(
        squares_kernel,
        out_shape=[stack, stack],
        in_specs=in_vmem(len(blocks)),
        out_specs=in_vmem(2),
        compiler_params=pltpu.CompilerParams(vmem_limit_bytes=8 << 20),
        name="squares",
    )(*blocks)


def pack_kernel(k, piece, mine, theirs, out_ref):
    rows = piece.shape[0]
    out_ref[:rows, :] = piece[...]
    out_ref[rows:, :] = mine[k] + theirs[k]


def pack(k, piece, mine, theirs):
    rows, part = piece.shape
    return pl.pallas_call(
        functools.partial(pack_kernel, k),
        out_shape=jax.ShapeDtypeStruct((2 * rows, part), jnp.float32),
        in_specs=in_vmem(3),
        out_specs=in_vmem(1)[0],
        compiler_params=pltpu.CompilerParams(vmem_limit_bytes=8 << 20),
        name="pack",
    )(piece, mine, theirs)


def join_kernel(*refs):
    out_ref = refs[-1]
    first = 0
    for ref in refs[:-1]:
        out_ref[first : first + ref.shape[0], :] = ref[...]
        first += ref.shape[0]


def join(*parts):
    rows = sum(part.shape[0] for part in parts)
    return pl.pallas_call(
        join_kernel,
        out_shape=jax.ShapeDtypeStruct((rows,) + parts[0].shape[1:], jnp.float32),
        in_specs=in_vmem(len(parts)),
        out_specs=in_vmem(1)[0],
        compiler_params=pltpu.CompilerParams(vmem_limit_bytes=8 << 20),
        name="join",
    )(*parts)


def finish_kernel(fold, place, orbitals, local_pot, *refs):
    out_ref = refs[-1]
    planes, slabs, cells = orbitals.shape
    part = cells // fold
    for f in range(fold):
        rows = slice(f * planes, (f + 1) * planes)
        cols = slice(f * part, (f + 1) * part)
        pieces = [ref[rows, :] for ref in refs[:-1]]
        local = local_pot[rows, :]
        for j in range(slabs):
            out_ref[:, j, cols] = local * orbitals[:, j, cols] + pick(place[0] ^ j, pieces)


def finish(place, orbitals, local_pot, pieces):
    planes, _, cells = orbitals.shape
    return pl.pallas_call(
        functools.partial(finish_kernel, fold_of(planes, cells)),
        out_shape=jax.ShapeDtypeStruct(orbitals.shape, jnp.float32),
        in_specs=with_scalar(2 + len(pieces)),
        out_specs=in_vmem(1)[0],
        compiler_params=pltpu.CompilerParams(vmem_limit_bytes=8 << 20),
        name="finish",
    )(place, orbitals, local_pot, *pieces)


def slab_swap(value, reach):
    size = lax.axis_size("slab")
    return lax.ppermute(value, "slab", [(i, i ^ reach) for i in range(size)])


def total_kernel(scale, shared, out_ref):
    summed = jnp.sum(shared[...], axis=0)
    out_ref[...] = scale * jnp.sum(summed, axis=1, keepdims=True)


def total_of(shared, scale):
    return pl.pallas_call(
        functools.partial(total_kernel, scale),
        out_shape=jax.ShapeDtypeStruct((1, 1), jnp.float32),
        in_specs=in_vmem(1),
        out_specs=in_vmem(1)[0],
        compiler_params=pltpu.CompilerParams(vmem_limit_bytes=8 << 20),
        name="total",
    )(shared)


def gather_ring(halves, band_index, bands):
    groups = [2 * p if p < bands // 2 else 2 * (bands - 1 - p) + 1 for p in range(bands)]
    place = band_index // 2
    position = jnp.where(band_index % 2 == 0, place, bands - 1 - place)

    def group_at(position):
        position = position % bands
        return jnp.where(position < bands // 2, 2 * position, 2 * (bands - 1 - position) + 1)

    def shift(value, by):
        moves = [(groups[p], groups[(p + by) % bands]) for p in range(bands)]
        return lax.ppermute(value, "band", moves)

    came = [(shift(half, 1), shift(half, -1)) for half in halves]
    blocks = []
    steps = bands // 2 - 1
    for step in range(steps):
        if step == 0:
            ahead, behind = (join(*pair) for pair in zip(*came))
        else:
            ahead = shift(ahead, 1)
            behind = shift(behind, -1)
        blocks.append((ahead, group_at(position - step - 1)))
        blocks.append((behind, group_at(position + step + 1)))
    half = ahead.shape[0] // 2
    head = shift(ahead[:half], 1)
    tail = shift(behind[half:], -1)
    blocks.append((join(head, tail), group_at(position + steps + 1)))
    return blocks


def body(orbitals, partners, counts):
    bands = lax.axis_size("band")
    slabs = lax.axis_size("slab")
    band_index = lax.axis_index("band")
    slab_index = lax.axis_index("slab")
    orb_group, _, _ = orbitals.shape
    total_orbs = orb_group * bands
    assert orb_group == slabs

    place = slab_index.astype(jnp.int32).reshape(1)
    by_plane = jnp.transpose(orbitals, (1, 0, 2))
    sends = prepare(place, by_plane)
    pieces = [sends[0]] + [slab_swap(sends[r], r) for r in range(1, slabs)]
    halves = [assemble(pieces[: slabs // 2]), assemble(pieces[slabs // 2 :])]
    own = join(*halves)
    others = gather_ring(halves, band_index, bands)
    force = clear((NX, NY * NZ))

    own, partners, counts = lax.optimization_barrier((own, partners, counts))
    tables = transform_tables(slab_index, slabs)

    groups = jnp.stack([group for _, group in others]).astype(jnp.int32)
    active = (slab_index < counts).astype(jnp.float32)
    mine = jnp.arange(bands, dtype=jnp.int32)[:, None] == band_index
    my_partners = jnp.sum(jnp.where(mine, partners, 0), axis=0)
    my_active = jnp.sum(jnp.where(mine, active, 0.0), axis=0)
    requested = jnp.sum(
        jnp.where(groups[:, None] == my_partners[None, :], my_active[None, :], 0.0), axis=1
    )
    wanted_by = jnp.sum(jnp.where(partners == band_index, active, 0.0), axis=1)
    chosen = groups[:, None] == jnp.arange(bands, dtype=jnp.int32)[None, :]
    returned = jnp.sum(jnp.where(chosen, wanted_by[None, :], 0.0), axis=1)
    weights = jnp.stack([requested + returned, requested], axis=1).reshape(-1)
    weights = jnp.broadcast_to(weights[:, None], weights.shape + (128,))

    energy = jnp.zeros((1, 128), jnp.float32)
    even, odd = squares_of([own] + [other for other, _ in others], slabs)
    from_core = slab_swap(odd, 1)
    for slot, (other, _) in enumerate(others):
        if slot < len(others) - 1:
            energy, force = pair_step(slot, weights, own, other, tables, force, energy)
        else:
            energy, *outgoing = pair_step(
                slot, weights, own, other, tables, force, energy, slabs, bands * slabs
            )

    for r in range(2, slabs, 2):
        outgoing[r] = pack(r // 2, outgoing[r], even, from_core)
    arrived = [outgoing[0]] + [slab_swap(outgoing[r], r) for r in range(1, slabs)]
    shared = lax.all_to_all(energy, ("band", "slab"), 0, 0)
    rows = arrived[0].shape[0]
    squares = even[0] + from_core[0] + sum(arrived[r][rows:] for r in range(2, slabs, 2))
    density = 2.0 / total_orbs * squares
    local_pot = slater_coeff * jnp.cbrt(density)
    forces = finish(place, by_plane, local_pot, arrived)
    total = total_of(shared, -1.0 / (2.0 * total_orbs * NX * NY * NZ))
    return jnp.transpose(forces, (1, 0, 2)), total.reshape(())


def solution(mesh):
    placed = (P("band", "slab", None), P(), P())
    return jax.shard_map(
        body, mesh=mesh, in_specs=placed, out_specs=(P("band", "slab", None), P()), check_vma=False
    )
```

```python
import functools
import math

import jax
import jax.numpy as jnp
import ml_dtypes
import numpy as np
from jax import lax
from jax.experimental import pallas as pl
from jax.experimental.pallas import tpu as pltpu
from jax.sharding import PartitionSpec as P


NX = 48
NY = 48
NZ = 48
NZP = 96
SIDE_X = NX // 2
GAP = 64


slater_coeff = -((3.0 / math.pi) ** (1.0 / 3.0))
exchange_mix = 0.25
screening = 0.25
row_row = (((1,), (1,)), ((), ()))


def split(value):
    high = value.astype(jnp.bfloat16)
    low = (value - high.astype(jnp.float32)).astype(jnp.bfloat16)
    return high, low


def cas(rows, cols, length):
    phase_angle = 2.0 * math.pi / length * (np.outer(rows, cols) % length)
    return np.cos(phase_angle) + np.sin(phase_angle)


def split_table(matrix):
    high = matrix.astype(ml_dtypes.bfloat16)
    return high, (matrix - high.astype(np.float64)).astype(ml_dtypes.bfloat16)


def wide(matrix):
    high, low = split_table(matrix)
    return np.concatenate([high, high, low], axis=1)


def tall(matrix):
    rows, cols = matrix.shape
    placed = np.zeros((2 * rows, 2 * GAP))
    placed[:rows, :cols] = matrix
    placed[rows:, GAP : GAP + cols] = matrix
    return np.concatenate(split_table(placed), axis=0)


def wavenumber_sq(length):
    return (2.0 * np.pi * np.fft.fftfreq(length)) ** 2


def transform_tables(slab_index, slabs):
    x_waves, y_cells, z_cells, z_waves = (np.arange(count) for count in (NX, NY, NZ, NZP))
    planes = NX // slabs
    held_x = [(slab ^ (x_waves // planes)) * planes + x_waves % planes for slab in range(slabs)]
    total = (
        wavenumber_sq(NZP)[:, None, None]
        + wavenumber_sq(NX)[None, :, None]
        + wavenumber_sq(NY)[None, None, :]
    )
    kernel_table = 4.0 * math.pi / (NX * NY * NZP) / (total + screening * screening)
    y_matrix = cas(y_cells, y_cells, NY)
    forward = jnp.asarray(np.stack([wide(cas(x_waves, held, NX)) for held in held_x]))
    quads = 4 * (x_waves[:SIDE_X] // 2) + x_waves[:SIDE_X] % 2
    kept = np.concatenate([quads, quads + 2])
    backward = jnp.asarray(np.stack([wide(cas(held, kept, NX)) for held in held_x]))
    kernel_table = np.pad(kernel_table, ((0, 0), (0, 0), (0, GAP - NY)))
    return (
        lax.dynamic_index_in_dim(forward, slab_index, 0, keepdims=False),
        jnp.asarray(wide(y_matrix)),
        jnp.asarray(tall(cas(z_waves, z_cells, NZP))),
        jnp.asarray(kernel_table.reshape(NZP, NX * GAP).astype(np.float32)),
        jnp.asarray(wide(cas(z_cells, z_waves, NZP))),
        jnp.asarray(tall(y_matrix)),
        lax.dynamic_index_in_dim(backward, slab_index, 0, keepdims=False),
    )


def apply_left(matrix, value):
    high, low = split(value)
    stacked = jnp.concatenate([high, low, high], axis=0)
    return jnp.dot(matrix, stacked, preferred_element_type=jnp.float32)


def apply_rows(matrix, high, low):
    half = matrix.shape[0] // 2
    both = lax.dot_general(matrix, high, row_row, preferred_element_type=jnp.float32)
    rest = lax.dot_general(matrix[:half], low, row_row, preferred_element_type=jnp.float32)
    return both[:half] + both[half:] + rest


def cut_into(refs, value):
    planes = NX // len(refs)
    part = refs[0].shape[1]
    fold = NY * NZ // part
    for r, ref in enumerate(refs):
        for f in range(fold):
            ref[f * planes : (f + 1) * planes, :] = value[
                r * planes : (r + 1) * planes, f * part : (f + 1) * part
            ]


def store_force(force_refs, value):
    if len(force_refs) == 1:
        force_refs[0][...] = value
    else:
        cut_into(force_refs, value)


def pair_kernel(
    slot, weights, own_ref, other_ref, x_fwd, y_fwd, z_fwd, table, z_inv, y_inv, x_inv,
    force_in, energy_in, *refs,
):
    energy_out, *force_refs, lines, high_rows, low_rows, field = refs
    total_weight = jnp.max(weights[2 * slot : 2 * slot + 1, :])
    request_weight = weights[2 * slot + 1 : 2 * slot + 2, :]

    @pl.when(total_weight == 0.0)
    def _():
        energy_out[...] = jnp.broadcast_to(energy_in[...], energy_out.shape)
        if len(force_refs) > 1:
            store_force(force_refs, force_in[...])

    @pl.when(total_weight != 0.0)
    def _():
        other = other_ref[...]
        density = own_ref[...] * other
        spectrum = apply_left(x_fwd[...], density)
        lines[...] = jnp.zeros_like(lines)
        for y in range(NY):
            rows = slice(y * SIDE_X, (y + 1) * SIDE_X)
            cols = slice(y * NZ, (y + 1) * NZ)
            lines[rows, :NZ] = spectrum[:SIDE_X, cols]
            lines[rows, GAP : GAP + NZ] = spectrum[SIDE_X:, cols]
        for q in range(SIDE_X):
            plane = apply_left(y_fwd[...], lines[pl.ds(q, NY, stride=SIDE_X), :])
            high, low = split(plane)
            rows = slice(q * GAP, q * GAP + NY)
            pad = slice(q * GAP + NY, (q + 1) * GAP)
            high_rows[rows, :] = high
            low_rows[rows, :] = low
            high_rows[pad, :] = jnp.zeros((GAP - NY, 2 * GAP), jnp.bfloat16)
            low_rows[pad, :] = jnp.zeros((GAP - NY, 2 * GAP), jnp.bfloat16)
        both = apply_rows(z_fwd[...], high_rows[...], low_rows[...])
        width = SIDE_X * GAP
        inner = []
        folded = jnp.zeros((1, 128), jnp.float32)
        for side in range(2):
            spectrum = both[side * NZP : (side + 1) * NZP]
            weighted = spectrum * table[:, side * width : (side + 1) * width]
            products = jnp.sum(spectrum * weighted, axis=0, keepdims=True)
            for start in range(0, width, 128):
                folded = folded + products[:, start : start + 128]
            inner.append(apply_left(z_inv[...], weighted))
        energy_out[...] = jnp.broadcast_to(
            energy_in[...] + request_weight * folded, energy_out.shape
        )
        for side in range(2):
            for pair in range(SIDE_X // 2):
                high, low = split(inner[side][:, pair * 2 * GAP : (pair + 1) * 2 * GAP])
                first = (side * (SIDE_X // 2) + pair) * GAP
                high_rows[first : first + NZ, :] = high
                low_rows[first : first + NZ, :] = low
        both = apply_rows(y_inv[...], high_rows[...], low_rows[...])
        for odd in range(2):
            for pair in range(SIDE_X // 2):
                first = (2 * pair + odd) * NY
                lines[first : first + NY, :] = both[
                    odd * NY : (odd + 1) * NY, pair * 2 * GAP : (pair + 1) * 2 * GAP
                ]
        for y in range(NY):
            plane = lines[pl.ds(y, SIDE_X, stride=NY), :]
            cols = slice(y * NZ, (y + 1) * NZ)
            field[:SIDE_X, cols] = plane[:, :NZ]
            field[SIDE_X:, cols] = plane[:, GAP : GAP + NZ]
        potential = apply_left(x_inv[...], field[...])
        store_force(
            force_refs, force_in[...] - (exchange_mix * total_weight) * (potential * other)
        )


def piece_shape(planes):
    fold = fold_of(planes, NY * NZ)
    return (planes * fold, NY * NZ // fold)


def pair_step(slot, weights, own, other, tables, force, energy, pieces=1, copies=None):
    piece = force.shape if pieces == 1 else piece_shape(NX // pieces)
    energy_shape = energy.shape if copies is None else (copies,) + energy.shape
    outs = [jax.ShapeDtypeStruct(energy_shape, jnp.float32)]
    outs += [jax.ShapeDtypeStruct(piece, jnp.float32)] * pieces
    return pl.pallas_call(
        functools.partial(pair_kernel, slot),
        out_shape=outs,
        in_specs=in_vmem(5 + len(tables)),
        out_specs=in_vmem(1 + pieces),
        scratch_shapes=[
            pltpu.VMEM((SIDE_X * NY, 2 * GAP), jnp.float32),
            pltpu.VMEM((SIDE_X * GAP, 2 * GAP), jnp.bfloat16),
            pltpu.VMEM((SIDE_X * GAP, 2 * GAP), jnp.bfloat16),
            pltpu.VMEM((NX, NY * NZ), jnp.float32),
        ],
        input_output_aliases={3 + len(tables): 1} if pieces == 1 else {},
        compiler_params=pltpu.CompilerParams(vmem_limit_bytes=32 << 20),
        cost_estimate=pl.CostEstimate(flops=3 << 30, transcendentals=0, bytes_accessed=3 << 20),
        name="pair_step",
    )(weights, own, other, *tables, force, energy)


def fold_of(planes, cells):
    return 2 if (2 * planes) % 8 == 0 and cells % 256 == 0 else 1


def in_vmem(count):
    return [pl.BlockSpec(memory_space=pltpu.VMEM)] * count


def with_scalar(count):
    return [pl.BlockSpec(memory_space=pltpu.SMEM)] + in_vmem(count)


def pick(place, choices):
    chosen = choices[0]
    for index in range(1, len(choices)):
        chosen = jnp.where(place == index, choices[index], chosen)
    return chosen


def prepare_kernel(fold, place, orbitals, *out_refs):
    planes, slabs, cells = orbitals.shape
    part = cells // fold
    for f in range(fold):
        rows = slice(f * planes, (f + 1) * planes)
        blocks = [orbitals[:, j, f * part : (f + 1) * part] for j in range(slabs)]
        for r in range(slabs):
            out_refs[r][rows, :] = pick(place[0] ^ r, blocks)


def prepare(place, orbitals):
    planes, slabs, cells = orbitals.shape
    fold = fold_of(planes, cells)
    piece = jax.ShapeDtypeStruct((planes * fold, cells // fold), jnp.float32)
    return pl.pallas_call(
        functools.partial(prepare_kernel, fold),
        out_shape=[piece] * slabs,
        in_specs=with_scalar(1),
        out_specs=in_vmem(slabs),
        compiler_params=pltpu.CompilerParams(vmem_limit_bytes=8 << 20),
        name="prepare",
    )(place, orbitals)


def assemble_kernel(fold, *refs):
    out_ref = refs[-1]
    planes = refs[0].shape[0] // fold
    part = refs[0].shape[1]
    for r, ref in enumerate(refs[:-1]):
        for f in range(fold):
            out_ref[r * planes : (r + 1) * planes, f * part : (f + 1) * part] = ref[
                f * planes : (f + 1) * planes, :
            ]


def assemble(pieces):
    rows, part = pieces[0].shape
    fold = NY * NZ // part
    return pl.pallas_call(
        functools.partial(assemble_kernel, fold),
        out_shape=jax.ShapeDtypeStruct((rows // fold * len(pieces), NY * NZ), jnp.float32),
        in_specs=in_vmem(len(pieces)),
        out_specs=in_vmem(1)[0],
        compiler_params=pltpu.CompilerParams(vmem_limit_bytes=8 << 20),
        name="assemble",
    )(*pieces)


def clear_kernel(out_ref):
    out_ref[...] = jnp.zeros_like(out_ref)


def clear(shape):
    return pl.pallas_call(
        clear_kernel,
        out_shape=jax.ShapeDtypeStruct(shape, jnp.float32),
        out_specs=in_vmem(1)[0],
        compiler_params=pltpu.CompilerParams(vmem_limit_bytes=8 << 20),
        name="clear",
    )()


def squares_kernel(*refs):
    *blocks, even_ref, odd_ref = refs
    slabs = 2 * even_ref.shape[0]
    squares = blocks[0][...] * blocks[0][...]
    for ref in blocks[1:]:
        squares = squares + ref[...] * ref[...]
    pieces = [ref.at[k] for k in range(slabs // 2) for ref in (even_ref, odd_ref)]
    cut_into(pieces, squares)


def squares_of(blocks, slabs):
    stack = jax.ShapeDtypeStruct((slabs // 2,) + piece_shape(NX // slabs), jnp.float32)
    return pl.pallas_call(
        squares_kernel,
        out_shape=[stack, stack],
        in_specs=in_vmem(len(blocks)),
        out_specs=in_vmem(2),
        compiler_params=pltpu.CompilerParams(vmem_limit_bytes=8 << 20),
        name="squares",
    )(*blocks)


def pack_kernel(k, piece, mine, theirs, out_ref):
    rows = piece.shape[0]
    out_ref[:rows, :] = piece[...]
    out_ref[rows:, :] = mine[k] + theirs[k]


def pack(k, piece, mine, theirs):
    rows, part = piece.shape
    return pl.pallas_call(
        functools.partial(pack_kernel, k),
        out_shape=jax.ShapeDtypeStruct((2 * rows, part), jnp.float32),
        in_specs=in_vmem(3),
        out_specs=in_vmem(1)[0],
        compiler_params=pltpu.CompilerParams(vmem_limit_bytes=8 << 20),
        name="pack",
    )(piece, mine, theirs)


def join_kernel(*refs):
    out_ref = refs[-1]
    first = 0
    for ref in refs[:-1]:
        out_ref[first : first + ref.shape[0], :] = ref[...]
        first += ref.shape[0]


def join(*parts):
    rows = sum(part.shape[0] for part in parts)
    return pl.pallas_call(
        join_kernel,
        out_shape=jax.ShapeDtypeStruct((rows,) + parts[0].shape[1:], jnp.float32),
        in_specs=in_vmem(len(parts)),
        out_specs=in_vmem(1)[0],
        compiler_params=pltpu.CompilerParams(vmem_limit_bytes=8 << 20),
        name="join",
    )(*parts)


def finish_kernel(fold, place, orbitals, local_pot, *refs):
    out_ref = refs[-1]
    planes, slabs, cells = orbitals.shape
    part = cells // fold
    for f in range(fold):
        rows = slice(f * planes, (f + 1) * planes)
        cols = slice(f * part, (f + 1) * part)
        pieces = [ref[rows, :] for ref in refs[:-1]]
        local = local_pot[rows, :]
        for j in range(slabs):
            out_ref[:, j, cols] = local * orbitals[:, j, cols] + pick(place[0] ^ j, pieces)


def finish(place, orbitals, local_pot, pieces):
    planes, _, cells = orbitals.shape
    return pl.pallas_call(
        functools.partial(finish_kernel, fold_of(planes, cells)),
        out_shape=jax.ShapeDtypeStruct(orbitals.shape, jnp.float32),
        in_specs=with_scalar(2 + len(pieces)),
        out_specs=in_vmem(1)[0],
        compiler_params=pltpu.CompilerParams(vmem_limit_bytes=8 << 20),
        name="finish",
    )(place, orbitals, local_pot, *pieces)


def slab_swap(value, reach):
    size = lax.axis_size("slab")
    return lax.ppermute(value, "slab", [(i, i ^ reach) for i in range(size)])


def total_kernel(scale, shared, out_ref):
    summed = jnp.sum(shared[...], axis=0)
    out_ref[...] = scale * jnp.sum(summed, axis=1, keepdims=True)


def total_of(shared, scale):
    return pl.pallas_call(
        functools.partial(total_kernel, scale),
        out_shape=jax.ShapeDtypeStruct((1, 1), jnp.float32),
        in_specs=in_vmem(1),
        out_specs=in_vmem(1)[0],
        compiler_params=pltpu.CompilerParams(vmem_limit_bytes=8 << 20),
        name="total",
    )(shared)


def gather_ring(halves, band_index, bands):
    groups = [2 * p if p < bands // 2 else 2 * (bands - 1 - p) + 1 for p in range(bands)]
    place = band_index // 2
    position = jnp.where(band_index % 2 == 0, place, bands - 1 - place)

    def group_at(position):
        position = position % bands
        return jnp.where(position < bands // 2, 2 * position, 2 * (bands - 1 - position) + 1)

    def shift(value, by):
        moves = [(groups[p], groups[(p + by) % bands]) for p in range(bands)]
        return lax.ppermute(value, "band", moves)

    def pass_on(halves, by):
        return [shift(half, by) for half in halves]

    ahead = behind = halves
    blocks = []
    steps = bands // 2 - 1
    for step in range(steps):
        ahead = pass_on(ahead, 1)
        behind = pass_on(behind, -1)
        blocks.append((join(*ahead), group_at(position - step - 1)))
        blocks.append((join(*behind), group_at(position + step + 1)))
    head = shift(ahead[0], 1)
    tail = shift(behind[1], -1)
    blocks.append((join(head, tail), group_at(position + steps + 1)))
    return blocks


def body(orbitals, partners, counts):
    bands = lax.axis_size("band")
    slabs = lax.axis_size("slab")
    band_index = lax.axis_index("band")
    slab_index = lax.axis_index("slab")
    orb_group, _, _ = orbitals.shape
    total_orbs = orb_group * bands
    assert orb_group == slabs

    place = slab_index.astype(jnp.int32).reshape(1)
    by_plane = jnp.transpose(orbitals, (1, 0, 2))
    sends = prepare(place, by_plane)
    pieces = [sends[0]] + [slab_swap(sends[r], r) for r in range(1, slabs)]
    halves = [assemble(pieces[: slabs // 2]), assemble(pieces[slabs // 2 :])]
    own = join(*halves)
    others = gather_ring(halves, band_index, bands)
    force = clear((NX, NY * NZ))

    own, partners, counts = lax.optimization_barrier((own, partners, counts))
    tables = transform_tables(slab_index, slabs)

    groups = jnp.stack([group for _, group in others]).astype(jnp.int32)
    active = (slab_index < counts).astype(jnp.float32)
    mine = jnp.arange(bands, dtype=jnp.int32)[:, None] == band_index
    my_partners = jnp.sum(jnp.where(mine, partners, 0), axis=0)
    my_active = jnp.sum(jnp.where(mine, active, 0.0), axis=0)
    requested = jnp.sum(
        jnp.where(groups[:, None] == my_partners[None, :], my_active[None, :], 0.0), axis=1
    )
    wanted_by = jnp.sum(jnp.where(partners == band_index, active, 0.0), axis=1)
    chosen = groups[:, None] == jnp.arange(bands, dtype=jnp.int32)[None, :]
    returned = jnp.sum(jnp.where(chosen, wanted_by[None, :], 0.0), axis=1)
    weights = jnp.stack([requested + returned, requested], axis=1).reshape(-1)
    weights = jnp.broadcast_to(weights[:, None], weights.shape + (128,))

    energy = jnp.zeros((1, 128), jnp.float32)
    even, odd = squares_of([own] + [other for other, _ in others], slabs)
    from_core = slab_swap(odd, 1)
    for slot, (other, _) in enumerate(others):
        if slot < len(others) - 1:
            energy, force = pair_step(slot, weights, own, other, tables, force, energy)
        else:
            energy, *outgoing = pair_step(
                slot, weights, own, other, tables, force, energy, slabs, bands * slabs
            )

    for r in range(2, slabs, 2):
        outgoing[r] = pack(r // 2, outgoing[r], even, from_core)
    arrived = [outgoing[0]] + [slab_swap(outgoing[r], r) for r in range(1, slabs)]
    shared = lax.all_to_all(energy, ("band", "slab"), 0, 0)
    rows = arrived[0].shape[0]
    squares = even[0] + from_core[0] + sum(arrived[r][rows:] for r in range(2, slabs, 2))
    density = 2.0 / total_orbs * squares
    local_pot = slater_coeff * jnp.cbrt(density)
    forces = finish(place, by_plane, local_pot, arrived)
    total = total_of(shared, -1.0 / (2.0 * total_orbs * NX * NY * NZ))
    return jnp.transpose(forces, (1, 0, 2)), total.reshape(())


def solution(mesh):
    placed = (P("band", "slab", None), P(), P())
    return jax.shard_map(
        body, mesh=mesh, in_specs=placed, out_specs=(P("band", "slab", None), P()), check_vma=False
    )
```

```python
import functools
import math

import jax
import jax.numpy as jnp
import ml_dtypes
import numpy as np
from jax import lax
from jax.experimental import pallas as pl
from jax.experimental.pallas import tpu as pltpu
from jax.sharding import PartitionSpec as P


NX = 48
NY = 48
NZ = 48
NZP = 96
SIDE_X = NX // 2
GAP = 64


slater_coeff = -((3.0 / math.pi) ** (1.0 / 3.0))
exchange_mix = 0.25
screening = 0.25
row_row = (((1,), (1,)), ((), ()))


def split(value):
    high = value.astype(jnp.bfloat16)
    low = (value - high.astype(jnp.float32)).astype(jnp.bfloat16)
    return high, low


def cas(rows, cols, length):
    phase_angle = 2.0 * math.pi / length * (np.outer(rows, cols) % length)
    return np.cos(phase_angle) + np.sin(phase_angle)


def split_table(matrix):
    high = matrix.astype(ml_dtypes.bfloat16)
    return high, (matrix - high.astype(np.float64)).astype(ml_dtypes.bfloat16)


def wide(matrix):
    high, low = split_table(matrix)
    return np.concatenate([high, high, low], axis=1)


def tall(matrix):
    rows, cols = matrix.shape
    placed = np.zeros((2 * rows, 2 * GAP))
    placed[:rows, :cols] = matrix
    placed[rows:, GAP : GAP + cols] = matrix
    return np.concatenate(split_table(placed), axis=0)


def wavenumber_sq(length):
    return (2.0 * np.pi * np.fft.fftfreq(length)) ** 2


def transform_tables(slab_index, slabs):
    x_waves, y_cells, z_cells, z_waves = (np.arange(count) for count in (NX, NY, NZ, NZP))
    planes = NX // slabs
    held_x = [(slab ^ (x_waves // planes)) * planes + x_waves % planes for slab in range(slabs)]
    total = (
        wavenumber_sq(NZP)[:, None, None]
        + wavenumber_sq(NX)[None, :, None]
        + wavenumber_sq(NY)[None, None, :]
    )
    kernel_table = 4.0 * math.pi / (NX * NY * NZP) / (total + screening * screening)
    y_matrix = cas(y_cells, y_cells, NY)
    forward = jnp.asarray(np.stack([wide(cas(x_waves, held, NX)) for held in held_x]))
    quads = 4 * (x_waves[:SIDE_X] // 2) + x_waves[:SIDE_X] % 2
    kept = np.concatenate([quads, quads + 2])
    backward = jnp.asarray(np.stack([wide(cas(held, kept, NX)) for held in held_x]))
    kernel_table = np.pad(kernel_table, ((0, 0), (0, 0), (0, GAP - NY)))
    return (
        lax.dynamic_index_in_dim(forward, slab_index, 0, keepdims=False),
        jnp.asarray(wide(y_matrix)),
        jnp.asarray(tall(cas(z_waves, z_cells, NZP))),
        jnp.asarray(kernel_table.reshape(NZP, NX * GAP).astype(np.float32)),
        jnp.asarray(wide(cas(z_cells, z_waves, NZP))),
        jnp.asarray(tall(y_matrix)),
        lax.dynamic_index_in_dim(backward, slab_index, 0, keepdims=False),
    )


def apply_left(matrix, value):
    high, low = split(value)
    stacked = jnp.concatenate([high, low, high], axis=0)
    return jnp.dot(matrix, stacked, preferred_element_type=jnp.float32)


def apply_rows(matrix, high, low):
    half = matrix.shape[0] // 2
    both = lax.dot_general(matrix, high, row_row, preferred_element_type=jnp.float32)
    rest = lax.dot_general(matrix[:half], low, row_row, preferred_element_type=jnp.float32)
    return both[:half] + both[half:] + rest


def cut_into(refs, value):
    planes = NX // len(refs)
    part = refs[0].shape[1]
    fold = NY * NZ // part
    for r, ref in enumerate(refs):
        for f in range(fold):
            ref[f * planes : (f + 1) * planes, :] = value[
                r * planes : (r + 1) * planes, f * part : (f + 1) * part
            ]


def store_force(force_refs, value):
    if len(force_refs) == 1:
        force_refs[0][...] = value
    else:
        cut_into(force_refs, value)


def pair_kernel(
    slot, weights, own_ref, other_ref, x_fwd, y_fwd, z_fwd, table, z_inv, y_inv, x_inv,
    force_in, energy_in, *refs,
):
    energy_out, *force_refs, lines, high_rows, low_rows, field = refs
    total_weight = jnp.max(weights[2 * slot : 2 * slot + 1, :])
    request_weight = weights[2 * slot + 1 : 2 * slot + 2, :]

    @pl.when(total_weight == 0.0)
    def _():
        energy_out[...] = jnp.broadcast_to(energy_in[...], energy_out.shape)
        if len(force_refs) > 1:
            store_force(force_refs, force_in[...])

    @pl.when(total_weight != 0.0)
    def _():
        other = other_ref[...]
        density = own_ref[...] * other
        spectrum = apply_left(x_fwd[...], density)
        lines[...] = jnp.zeros_like(lines)
        for y in range(NY):
            rows = slice(y * SIDE_X, (y + 1) * SIDE_X)
            cols = slice(y * NZ, (y + 1) * NZ)
            lines[rows, :NZ] = spectrum[:SIDE_X, cols]
            lines[rows, GAP : GAP + NZ] = spectrum[SIDE_X:, cols]
        for q in range(SIDE_X):
            plane = apply_left(y_fwd[...], lines[pl.ds(q, NY, stride=SIDE_X), :])
            high, low = split(plane)
            rows = slice(q * GAP, q * GAP + NY)
            pad = slice(q * GAP + NY, (q + 1) * GAP)
            high_rows[rows, :] = high
            low_rows[rows, :] = low
            high_rows[pad, :] = jnp.zeros((GAP - NY, 2 * GAP), jnp.bfloat16)
            low_rows[pad, :] = jnp.zeros((GAP - NY, 2 * GAP), jnp.bfloat16)
        both = apply_rows(z_fwd[...], high_rows[...], low_rows[...])
        width = SIDE_X * GAP
        inner = []
        folded = jnp.zeros((1, 128), jnp.float32)
        for side in range(2):
            spectrum = both[side * NZP : (side + 1) * NZP]
            weighted = spectrum * table[:, side * width : (side + 1) * width]
            products = jnp.sum(spectrum * weighted, axis=0, keepdims=True)
            for start in range(0, width, 128):
                folded = folded + products[:, start : start + 128]
            inner.append(apply_left(z_inv[...], weighted))
        energy_out[...] = jnp.broadcast_to(
            energy_in[...] + request_weight * folded, energy_out.shape
        )
        for side in range(2):
            for pair in range(SIDE_X // 2):
                high, low = split(inner[side][:, pair * 2 * GAP : (pair + 1) * 2 * GAP])
                first = (side * (SIDE_X // 2) + pair) * GAP
                high_rows[first : first + NZ, :] = high
                low_rows[first : first + NZ, :] = low
        both = apply_rows(y_inv[...], high_rows[...], low_rows[...])
        for odd in range(2):
            for pair in range(SIDE_X // 2):
                first = (2 * pair + odd) * NY
                lines[first : first + NY, :] = both[
                    odd * NY : (odd + 1) * NY, pair * 2 * GAP : (pair + 1) * 2 * GAP
                ]
        for y in range(NY):
            plane = lines[pl.ds(y, SIDE_X, stride=NY), :]
            cols = slice(y * NZ, (y + 1) * NZ)
            field[:SIDE_X, cols] = plane[:, :NZ]
            field[SIDE_X:, cols] = plane[:, GAP : GAP + NZ]
        potential = apply_left(x_inv[...], field[...])
        store_force(
            force_refs, force_in[...] - (exchange_mix * total_weight) * (potential * other)
        )


def piece_shape(planes):
    fold = fold_of(planes, NY * NZ)
    return (planes * fold, NY * NZ // fold)


def pair_step(slot, weights, own, other, tables, force, energy, pieces=1, copies=None):
    piece = force.shape if pieces == 1 else piece_shape(NX // pieces)
    energy_shape = energy.shape if copies is None else (copies,) + energy.shape
    outs = [jax.ShapeDtypeStruct(energy_shape, jnp.float32)]
    outs += [jax.ShapeDtypeStruct(piece, jnp.float32)] * pieces
    return pl.pallas_call(
        functools.partial(pair_kernel, slot),
        out_shape=outs,
        in_specs=in_vmem(5 + len(tables)),
        out_specs=in_vmem(1 + pieces),
        scratch_shapes=[
            pltpu.VMEM((SIDE_X * NY, 2 * GAP), jnp.float32),
            pltpu.VMEM((SIDE_X * GAP, 2 * GAP), jnp.bfloat16),
            pltpu.VMEM((SIDE_X * GAP, 2 * GAP), jnp.bfloat16),
            pltpu.VMEM((NX, NY * NZ), jnp.float32),
        ],
        input_output_aliases={3 + len(tables): 1} if pieces == 1 else {},
        compiler_params=pltpu.CompilerParams(vmem_limit_bytes=32 << 20),
        cost_estimate=pl.CostEstimate(flops=3 << 30, transcendentals=0, bytes_accessed=3 << 20),
        name="pair_step",
    )(weights, own, other, *tables, force, energy)


def fold_of(planes, cells):
    return 2 if (2 * planes) % 8 == 0 and cells % 256 == 0 else 1


def in_vmem(count):
    return [pl.BlockSpec(memory_space=pltpu.VMEM)] * count


def with_scalar(count):
    return [pl.BlockSpec(memory_space=pltpu.SMEM)] + in_vmem(count)


def pick(place, choices):
    chosen = choices[0]
    for index in range(1, len(choices)):
        chosen = jnp.where(place == index, choices[index], chosen)
    return chosen


def prepare_kernel(fold, place, orbitals, *out_refs):
    planes, slabs, cells = orbitals.shape
    part = cells // fold
    for f in range(fold):
        rows = slice(f * planes, (f + 1) * planes)
        blocks = [orbitals[:, j, f * part : (f + 1) * part] for j in range(slabs)]
        for r in range(slabs):
            out_refs[r][rows, :] = pick(place[0] ^ r, blocks)


def prepare(place, orbitals):
    planes, slabs, cells = orbitals.shape
    fold = fold_of(planes, cells)
    piece = jax.ShapeDtypeStruct((planes * fold, cells // fold), jnp.float32)
    return pl.pallas_call(
        functools.partial(prepare_kernel, fold),
        out_shape=[piece] * slabs,
        in_specs=with_scalar(1),
        out_specs=in_vmem(slabs),
        compiler_params=pltpu.CompilerParams(vmem_limit_bytes=8 << 20),
        name="prepare",
    )(place, orbitals)


def assemble_kernel(fold, *refs):
    out_ref = refs[-1]
    planes = refs[0].shape[0] // fold
    part = refs[0].shape[1]
    for r, ref in enumerate(refs[:-1]):
        for f in range(fold):
            out_ref[r * planes : (r + 1) * planes, f * part : (f + 1) * part] = ref[
                f * planes : (f + 1) * planes, :
            ]


def assemble(pieces):
    rows, part = pieces[0].shape
    fold = NY * NZ // part
    return pl.pallas_call(
        functools.partial(assemble_kernel, fold),
        out_shape=jax.ShapeDtypeStruct((rows // fold * len(pieces), NY * NZ), jnp.float32),
        in_specs=in_vmem(len(pieces)),
        out_specs=in_vmem(1)[0],
        compiler_params=pltpu.CompilerParams(vmem_limit_bytes=8 << 20),
        name="assemble",
    )(*pieces)


def clear_kernel(out_ref):
    out_ref[...] = jnp.zeros_like(out_ref)


def clear(shape):
    return pl.pallas_call(
        clear_kernel,
        out_shape=jax.ShapeDtypeStruct(shape, jnp.float32),
        out_specs=in_vmem(1)[0],
        compiler_params=pltpu.CompilerParams(vmem_limit_bytes=8 << 20),
        name="clear",
    )()


def squares_kernel(*refs):
    *blocks, even_ref, odd_ref = refs
    slabs = 2 * even_ref.shape[0]
    squares = blocks[0][...] * blocks[0][...]
    for ref in blocks[1:]:
        squares = squares + ref[...] * ref[...]
    pieces = [ref.at[k] for k in range(slabs // 2) for ref in (even_ref, odd_ref)]
    cut_into(pieces, squares)


def squares_of(blocks, slabs):
    stack = jax.ShapeDtypeStruct((slabs // 2,) + piece_shape(NX // slabs), jnp.float32)
    return pl.pallas_call(
        squares_kernel,
        out_shape=[stack, stack],
        in_specs=in_vmem(len(blocks)),
        out_specs=in_vmem(2),
        compiler_params=pltpu.CompilerParams(vmem_limit_bytes=8 << 20),
        name="squares",
    )(*blocks)


def pack_kernel(k, piece, mine, theirs, out_ref):
    rows = piece.shape[0]
    out_ref[:rows, :] = piece[...]
    out_ref[rows:, :] = mine[k] + theirs[k]


def pack(k, piece, mine, theirs):
    rows, part = piece.shape
    return pl.pallas_call(
        functools.partial(pack_kernel, k),
        out_shape=jax.ShapeDtypeStruct((2 * rows, part), jnp.float32),
        in_specs=in_vmem(3),
        out_specs=in_vmem(1)[0],
        compiler_params=pltpu.CompilerParams(vmem_limit_bytes=8 << 20),
        name="pack",
    )(piece, mine, theirs)


def stage_kernel(*refs):
    count = len(refs) // 2
    for source, target in zip(refs[:count], refs[count:]):
        target[...] = source[...]


def stage(tables):
    return pl.pallas_call(
        stage_kernel,
        out_shape=[jax.ShapeDtypeStruct(table.shape, table.dtype) for table in tables],
        in_specs=in_vmem(len(tables)),
        out_specs=in_vmem(len(tables)),
        compiler_params=pltpu.CompilerParams(vmem_limit_bytes=8 << 20),
        name="stage",
    )(*tables)


def join_kernel(*refs):
    out_ref = refs[-1]
    first = 0
    for ref in refs[:-1]:
        out_ref[first : first + ref.shape[0], :] = ref[...]
        first += ref.shape[0]


def join(*parts):
    rows = sum(part.shape[0] for part in parts)
    return pl.pallas_call(
        join_kernel,
        out_shape=jax.ShapeDtypeStruct((rows,) + parts[0].shape[1:], jnp.float32),
        in_specs=in_vmem(len(parts)),
        out_specs=in_vmem(1)[0],
        compiler_params=pltpu.CompilerParams(vmem_limit_bytes=8 << 20),
        name="join",
    )(*parts)


def finish_kernel(fold, place, orbitals, local_pot, *refs):
    out_ref = refs[-1]
    planes, slabs, cells = orbitals.shape
    part = cells // fold
    for f in range(fold):
        rows = slice(f * planes, (f + 1) * planes)
        cols = slice(f * part, (f + 1) * part)
        pieces = [ref[rows, :] for ref in refs[:-1]]
        local = local_pot[rows, :]
        for j in range(slabs):
            out_ref[:, j, cols] = local * orbitals[:, j, cols] + pick(place[0] ^ j, pieces)


def finish(place, orbitals, local_pot, pieces):
    planes, _, cells = orbitals.shape
    return pl.pallas_call(
        functools.partial(finish_kernel, fold_of(planes, cells)),
        out_shape=jax.ShapeDtypeStruct(orbitals.shape, jnp.float32),
        in_specs=with_scalar(2 + len(pieces)),
        out_specs=in_vmem(1)[0],
        compiler_params=pltpu.CompilerParams(vmem_limit_bytes=8 << 20),
        name="finish",
    )(place, orbitals, local_pot, *pieces)


def slab_swap(value, reach):
    size = lax.axis_size("slab")
    return lax.ppermute(value, "slab", [(i, i ^ reach) for i in range(size)])


def total_kernel(scale, shared, out_ref):
    summed = jnp.sum(shared[...], axis=0)
    out_ref[...] = scale * jnp.sum(summed, axis=1, keepdims=True)


def total_of(shared, scale):
    return pl.pallas_call(
        functools.partial(total_kernel, scale),
        out_shape=jax.ShapeDtypeStruct((1, 1), jnp.float32),
        in_specs=in_vmem(1),
        out_specs=in_vmem(1)[0],
        compiler_params=pltpu.CompilerParams(vmem_limit_bytes=8 << 20),
        name="total",
    )(shared)


def gather_ring(halves, band_index, bands):
    groups = [2 * p if p < bands // 2 else 2 * (bands - 1 - p) + 1 for p in range(bands)]
    place = band_index // 2
    position = jnp.where(band_index % 2 == 0, place, bands - 1 - place)

    def group_at(position):
        position = position % bands
        return jnp.where(position < bands // 2, 2 * position, 2 * (bands - 1 - position) + 1)

    def shift(value, by):
        moves = [(groups[p], groups[(p + by) % bands]) for p in range(bands)]
        return lax.ppermute(value, "band", moves)

    def pass_on(halves, by):
        return [shift(half, by) for half in halves]

    ahead = behind = halves
    blocks = []
    steps = bands // 2 - 1
    for step in range(steps):
        ahead = pass_on(ahead, 1)
        behind = pass_on(behind, -1)
        blocks.append((join(*ahead), group_at(position - step - 1)))
        blocks.append((join(*behind), group_at(position + step + 1)))
    head = shift(ahead[0], 1)
    tail = shift(behind[1], -1)
    blocks.append((join(head, tail), group_at(position + steps + 1)))
    return blocks


def body(orbitals, partners, counts):
    bands = lax.axis_size("band")
    slabs = lax.axis_size("slab")
    band_index = lax.axis_index("band")
    slab_index = lax.axis_index("slab")
    orb_group, _, _ = orbitals.shape
    total_orbs = orb_group * bands
    assert orb_group == slabs

    place = slab_index.astype(jnp.int32).reshape(1)
    by_plane = jnp.transpose(orbitals, (1, 0, 2))
    sends = prepare(place, by_plane)
    pieces = [sends[0]] + [slab_swap(sends[r], r) for r in range(1, slabs)]
    halves = [assemble(pieces[: slabs // 2]), assemble(pieces[slabs // 2 :])]
    own = join(*halves)
    others = gather_ring(halves, band_index, bands)
    force = clear((NX, NY * NZ))

    own, partners, counts = lax.optimization_barrier((own, partners, counts))
    x_fwd, *tables, x_inv = transform_tables(slab_index, slabs)
    tables = [x_fwd, *stage(tables), x_inv]

    groups = jnp.stack([group for _, group in others]).astype(jnp.int32)
    active = (slab_index < counts).astype(jnp.float32)
    mine = jnp.arange(bands, dtype=jnp.int32)[:, None] == band_index
    my_partners = jnp.sum(jnp.where(mine, partners, 0), axis=0)
    my_active = jnp.sum(jnp.where(mine, active, 0.0), axis=0)
    requested = jnp.sum(
        jnp.where(groups[:, None] == my_partners[None, :], my_active[None, :], 0.0), axis=1
    )
    wanted_by = jnp.sum(jnp.where(partners == band_index, active, 0.0), axis=1)
    chosen = groups[:, None] == jnp.arange(bands, dtype=jnp.int32)[None, :]
    returned = jnp.sum(jnp.where(chosen, wanted_by[None, :], 0.0), axis=1)
    weights = jnp.stack([requested + returned, requested], axis=1).reshape(-1)
    weights = jnp.broadcast_to(weights[:, None], weights.shape + (128,))

    energy = jnp.zeros((1, 128), jnp.float32)
    even, odd = squares_of([own] + [other for other, _ in others], slabs)
    from_core = slab_swap(odd, 1)
    for slot, (other, _) in enumerate(others):
        if slot < len(others) - 1:
            energy, force = pair_step(slot, weights, own, other, tables, force, energy)
        else:
            energy, *outgoing = pair_step(
                slot, weights, own, other, tables, force, energy, slabs, bands * slabs
            )

    for r in range(2, slabs, 2):
        outgoing[r] = pack(r // 2, outgoing[r], even, from_core)
    arrived = [outgoing[0]] + [slab_swap(outgoing[r], r) for r in range(1, slabs)]
    shared = lax.all_to_all(energy, ("band", "slab"), 0, 0)
    rows = arrived[0].shape[0]
    squares = even[0] + from_core[0] + sum(arrived[r][rows:] for r in range(2, slabs, 2))
    density = 2.0 / total_orbs * squares
    local_pot = slater_coeff * jnp.cbrt(density)
    forces = finish(place, by_plane, local_pot, arrived)
    total = total_of(shared, -1.0 / (2.0 * total_orbs * NX * NY * NZ))
    return jnp.transpose(forces, (1, 0, 2)), total.reshape(())


def solution(mesh):
    placed = (P("band", "slab", None), P(), P())
    return jax.shard_map(
        body, mesh=mesh, in_specs=placed, out_specs=(P("band", "slab", None), P()), check_vma=False
    )
```

```python
import functools
import math

import jax
import jax.numpy as jnp
import ml_dtypes
import numpy as np
from jax import lax
from jax.experimental import pallas as pl
from jax.experimental.pallas import tpu as pltpu
from jax.sharding import PartitionSpec as P


NX = 48
NY = 48
NZ = 48
NZP = 96
SIDE_X = NX // 2
GAP = 64


slater_coeff = -((3.0 / math.pi) ** (1.0 / 3.0))
exchange_mix = 0.25
screening = 0.25
row_row = (((1,), (1,)), ((), ()))


def split(value):
    high = value.astype(jnp.bfloat16)
    low = (value - high.astype(jnp.float32)).astype(jnp.bfloat16)
    return high, low


def cas(rows, cols, length):
    phase_angle = 2.0 * math.pi / length * (np.outer(rows, cols) % length)
    return np.cos(phase_angle) + np.sin(phase_angle)


def split_table(matrix):
    high = matrix.astype(ml_dtypes.bfloat16)
    return high, (matrix - high.astype(np.float64)).astype(ml_dtypes.bfloat16)


def wide(matrix):
    high, low = split_table(matrix)
    return np.concatenate([high, high, low], axis=1)


def tall(matrix):
    rows, cols = matrix.shape
    placed = np.zeros((2 * rows, 2 * GAP))
    placed[:rows, :cols] = matrix
    placed[rows:, GAP : GAP + cols] = matrix
    return np.concatenate(split_table(placed), axis=0)


def wavenumber_sq(length):
    return (2.0 * np.pi * np.fft.fftfreq(length)) ** 2


def transform_tables(slabs):
    x_waves, y_cells, z_cells, z_waves = (np.arange(count) for count in (NX, NY, NZ, NZP))
    planes = NX // slabs
    held_x = [(slab ^ (x_waves // planes)) * planes + x_waves % planes for slab in range(slabs)]
    total = (
        wavenumber_sq(NZP)[:, None, None]
        + wavenumber_sq(NX)[None, :, None]
        + wavenumber_sq(NY)[None, None, :]
    )
    kernel_table = 4.0 * math.pi / (NX * NY * NZP) / (total + screening * screening)
    y_matrix = cas(y_cells, y_cells, NY)
    forward = [wide(cas(x_waves, held, NX)) for held in held_x]
    quads = 4 * (x_waves[:SIDE_X] // 2) + x_waves[:SIDE_X] % 2
    kept = np.concatenate([quads, quads + 2])
    backward = [wide(cas(held, kept, NX)) for held in held_x]
    kernel_table = np.pad(kernel_table, ((0, 0), (0, 0), (0, GAP - NY)))
    lanes = 3 * NZP
    wides = [wide(y_matrix), wide(cas(z_cells, z_waves, NZP)), *forward, *backward]
    wides = [np.pad(matrix, ((0, 0), (0, lanes - matrix.shape[1]))) for matrix in wides]
    talls = [tall(cas(z_waves, z_cells, NZP)), tall(y_matrix)]
    flat = kernel_table.reshape(NZP, NX * GAP).astype(np.float32)
    return tuple(jnp.asarray(table) for table in (np.stack(wides), np.concatenate(talls), flat))


def apply_left(matrix, value):
    high, low = split(value)
    stacked = jnp.concatenate([high, low, high], axis=0)
    return jnp.dot(matrix, stacked, preferred_element_type=jnp.float32)


def apply_rows(matrix, high, low):
    half = matrix.shape[0] // 2
    both = lax.dot_general(matrix, high, row_row, preferred_element_type=jnp.float32)
    rest = lax.dot_general(matrix[:half], low, row_row, preferred_element_type=jnp.float32)
    return both[:half] + both[half:] + rest


def cut_into(refs, value):
    planes = NX // len(refs)
    part = refs[0].shape[1]
    fold = NY * NZ // part
    for r, ref in enumerate(refs):
        for f in range(fold):
            ref[f * planes : (f + 1) * planes, :] = value[
                r * planes : (r + 1) * planes, f * part : (f + 1) * part
            ]


def store_force(force_refs, value):
    if len(force_refs) == 1:
        force_refs[0][...] = value
    else:
        cut_into(force_refs, value)


def pair_kernel(
    slot, weights, own_ref, other_ref, x_fwd, y_fwd, z_fwd, table, z_inv, y_inv, x_inv,
    force_in, energy_in, *refs,
):
    energy_out, *force_refs, lines, high_rows, low_rows, field = refs
    total_weight = jnp.max(weights[2 * slot : 2 * slot + 1, :])
    request_weight = weights[2 * slot + 1 : 2 * slot + 2, :]

    @pl.when(total_weight == 0.0)
    def _():
        energy_out[...] = jnp.broadcast_to(energy_in[...], energy_out.shape)
        if len(force_refs) > 1:
            store_force(force_refs, force_in[...])

    @pl.when(total_weight != 0.0)
    def _():
        other = other_ref[...]
        density = own_ref[...] * other
        spectrum = apply_left(x_fwd[...], density)
        lines[...] = jnp.zeros_like(lines)
        for y in range(NY):
            rows = slice(y * SIDE_X, (y + 1) * SIDE_X)
            cols = slice(y * NZ, (y + 1) * NZ)
            lines[rows, :NZ] = spectrum[:SIDE_X, cols]
            lines[rows, GAP : GAP + NZ] = spectrum[SIDE_X:, cols]
        for q in range(SIDE_X):
            plane = apply_left(y_fwd[...], lines[pl.ds(q, NY, stride=SIDE_X), :])
            high, low = split(plane)
            rows = slice(q * GAP, q * GAP + NY)
            pad = slice(q * GAP + NY, (q + 1) * GAP)
            high_rows[rows, :] = high
            low_rows[rows, :] = low
            high_rows[pad, :] = jnp.zeros((GAP - NY, 2 * GAP), jnp.bfloat16)
            low_rows[pad, :] = jnp.zeros((GAP - NY, 2 * GAP), jnp.bfloat16)
        both = apply_rows(z_fwd[...], high_rows[...], low_rows[...])
        width = SIDE_X * GAP
        inner = []
        folded = jnp.zeros((1, 128), jnp.float32)
        for side in range(2):
            spectrum = both[side * NZP : (side + 1) * NZP]
            weighted = spectrum * table[:, side * width : (side + 1) * width]
            products = jnp.sum(spectrum * weighted, axis=0, keepdims=True)
            for start in range(0, width, 128):
                folded = folded + products[:, start : start + 128]
            inner.append(apply_left(z_inv[...], weighted))
        energy_out[...] = jnp.broadcast_to(
            energy_in[...] + request_weight * folded, energy_out.shape
        )
        for side in range(2):
            for pair in range(SIDE_X // 2):
                high, low = split(inner[side][:, pair * 2 * GAP : (pair + 1) * 2 * GAP])
                first = (side * (SIDE_X // 2) + pair) * GAP
                high_rows[first : first + NZ, :] = high
                low_rows[first : first + NZ, :] = low
        both = apply_rows(y_inv[...], high_rows[...], low_rows[...])
        for odd in range(2):
            for pair in range(SIDE_X // 2):
                first = (2 * pair + odd) * NY
                lines[first : first + NY, :] = both[
                    odd * NY : (odd + 1) * NY, pair * 2 * GAP : (pair + 1) * 2 * GAP
                ]
        for y in range(NY):
            plane = lines[pl.ds(y, SIDE_X, stride=NY), :]
            cols = slice(y * NZ, (y + 1) * NZ)
            field[:SIDE_X, cols] = plane[:, :NZ]
            field[SIDE_X:, cols] = plane[:, GAP : GAP + NZ]
        potential = apply_left(x_inv[...], field[...])
        store_force(
            force_refs, force_in[...] - (exchange_mix * total_weight) * (potential * other)
        )


def piece_shape(planes):
    fold = fold_of(planes, NY * NZ)
    return (planes * fold, NY * NZ // fold)


def pair_step(slot, weights, own, other, tables, force, energy, pieces=1, copies=None):
    piece = force.shape if pieces == 1 else piece_shape(NX // pieces)
    energy_shape = energy.shape if copies is None else (copies,) + energy.shape
    outs = [jax.ShapeDtypeStruct(energy_shape, jnp.float32)]
    outs += [jax.ShapeDtypeStruct(piece, jnp.float32)] * pieces
    return pl.pallas_call(
        functools.partial(pair_kernel, slot),
        out_shape=outs,
        in_specs=in_vmem(5 + len(tables)),
        out_specs=in_vmem(1 + pieces),
        scratch_shapes=[
            pltpu.VMEM((SIDE_X * NY, 2 * GAP), jnp.float32),
            pltpu.VMEM((SIDE_X * GAP, 2 * GAP), jnp.bfloat16),
            pltpu.VMEM((SIDE_X * GAP, 2 * GAP), jnp.bfloat16),
            pltpu.VMEM((NX, NY * NZ), jnp.float32),
        ],
        input_output_aliases={3 + len(tables): 1} if pieces == 1 else {},
        compiler_params=pltpu.CompilerParams(vmem_limit_bytes=32 << 20),
        cost_estimate=pl.CostEstimate(flops=3 << 30, transcendentals=0, bytes_accessed=3 << 20),
        name="pair_step",
    )(weights, own, other, *tables, force, energy)


def fold_of(planes, cells):
    return 2 if (2 * planes) % 8 == 0 and cells % 256 == 0 else 1


def in_vmem(count):
    return [pl.BlockSpec(memory_space=pltpu.VMEM)] * count


def with_scalar(count):
    return [pl.BlockSpec(memory_space=pltpu.SMEM)] + in_vmem(count)


def pick(place, choices):
    chosen = choices[0]
    for index in range(1, len(choices)):
        chosen = jnp.where(place == index, choices[index], chosen)
    return chosen


def prepare_kernel(fold, place, orbitals, *out_refs):
    planes, slabs, cells = orbitals.shape
    part = cells // fold
    for f in range(fold):
        rows = slice(f * planes, (f + 1) * planes)
        blocks = [orbitals[:, j, f * part : (f + 1) * part] for j in range(slabs)]
        for r in range(slabs):
            out_refs[r][rows, :] = pick(place[0] ^ r, blocks)


def prepare(place, orbitals):
    planes, slabs, cells = orbitals.shape
    fold = fold_of(planes, cells)
    piece = jax.ShapeDtypeStruct((planes * fold, cells // fold), jnp.float32)
    return pl.pallas_call(
        functools.partial(prepare_kernel, fold),
        out_shape=[piece] * slabs,
        in_specs=with_scalar(1),
        out_specs=in_vmem(slabs),
        compiler_params=pltpu.CompilerParams(vmem_limit_bytes=8 << 20),
        name="prepare",
    )(place, orbitals)


def assemble_kernel(fold, *refs):
    out_ref = refs[-1]
    planes = refs[0].shape[0] // fold
    part = refs[0].shape[1]
    for r, ref in enumerate(refs[:-1]):
        for f in range(fold):
            out_ref[r * planes : (r + 1) * planes, f * part : (f + 1) * part] = ref[
                f * planes : (f + 1) * planes, :
            ]


def assemble(pieces):
    rows, part = pieces[0].shape
    fold = NY * NZ // part
    return pl.pallas_call(
        functools.partial(assemble_kernel, fold),
        out_shape=jax.ShapeDtypeStruct((rows // fold * len(pieces), NY * NZ), jnp.float32),
        in_specs=in_vmem(len(pieces)),
        out_specs=in_vmem(1)[0],
        compiler_params=pltpu.CompilerParams(vmem_limit_bytes=8 << 20),
        name="assemble",
    )(*pieces)


def clear_kernel(out_ref):
    out_ref[...] = jnp.zeros_like(out_ref)


def clear(shape):
    return pl.pallas_call(
        clear_kernel,
        out_shape=jax.ShapeDtypeStruct(shape, jnp.float32),
        out_specs=in_vmem(1)[0],
        compiler_params=pltpu.CompilerParams(vmem_limit_bytes=8 << 20),
        name="clear",
    )()


def squares_kernel(*refs):
    *blocks, even_ref, odd_ref = refs
    slabs = 2 * even_ref.shape[0]
    squares = blocks[0][...] * blocks[0][...]
    for ref in blocks[1:]:
        squares = squares + ref[...] * ref[...]
    pieces = [ref.at[k] for k in range(slabs // 2) for ref in (even_ref, odd_ref)]
    cut_into(pieces, squares)


def squares_of(blocks, slabs):
    stack = jax.ShapeDtypeStruct((slabs // 2,) + piece_shape(NX // slabs), jnp.float32)
    return pl.pallas_call(
        squares_kernel,
        out_shape=[stack, stack],
        in_specs=in_vmem(len(blocks)),
        out_specs=in_vmem(2),
        compiler_params=pltpu.CompilerParams(vmem_limit_bytes=8 << 20),
        name="squares",
    )(*blocks)


def pack_kernel(k, piece, mine, theirs, out_ref):
    rows = piece.shape[0]
    out_ref[:rows, :] = piece[...]
    out_ref[rows:, :] = mine[k] + theirs[k]


def pack(k, piece, mine, theirs):
    rows, part = piece.shape
    return pl.pallas_call(
        functools.partial(pack_kernel, k),
        out_shape=jax.ShapeDtypeStruct((2 * rows, part), jnp.float32),
        in_specs=in_vmem(3),
        out_specs=in_vmem(1)[0],
        compiler_params=pltpu.CompilerParams(vmem_limit_bytes=8 << 20),
        name="pack",
    )(piece, mine, theirs)


def stage_kernel(
    slabs, place, wides, talls, flat, x_fwd, y_fwd, z_fwd, table, z_inv, y_inv, x_inv
):
    y_fwd[...] = wides[0, :, : 3 * NY]
    z_inv[...] = wides[1]
    x_fwd[...] = pick(place[0], [wides[2 + slab, :, : 3 * NX] for slab in range(slabs)])
    x_inv[...] = pick(place[0], [wides[2 + slabs + slab, :, : 3 * NX] for slab in range(slabs)])
    z_fwd[...] = talls[: 4 * NZP]
    y_inv[...] = talls[4 * NZP :]
    table[...] = flat[...]


def stage(place, slabs):
    tables = transform_tables(slabs)
    halves = jnp.bfloat16
    shapes = [
        ((NX, 3 * NX), halves), ((NY, 3 * NY), halves), ((4 * NZP, 2 * GAP), halves),
        ((NZP, NX * GAP), jnp.float32), ((NZ, 3 * NZP), halves), ((4 * NY, 2 * GAP), halves),
        ((NX, 3 * NX), halves),
    ]
    return pl.pallas_call(
        functools.partial(stage_kernel, slabs),
        out_shape=[jax.ShapeDtypeStruct(shape, kind) for shape, kind in shapes],
        in_specs=with_scalar(len(tables)),
        out_specs=in_vmem(len(shapes)),
        compiler_params=pltpu.CompilerParams(vmem_limit_bytes=8 << 20),
        name="stage",
    )(place, *tables)


def join_kernel(*refs):
    out_ref = refs[-1]
    first = 0
    for ref in refs[:-1]:
        out_ref[first : first + ref.shape[0], :] = ref[...]
        first += ref.shape[0]


def join(*parts):
    rows = sum(part.shape[0] for part in parts)
    return pl.pallas_call(
        join_kernel,
        out_shape=jax.ShapeDtypeStruct((rows,) + parts[0].shape[1:], jnp.float32),
        in_specs=in_vmem(len(parts)),
        out_specs=in_vmem(1)[0],
        compiler_params=pltpu.CompilerParams(vmem_limit_bytes=8 << 20),
        name="join",
    )(*parts)


def finish_kernel(fold, place, orbitals, local_pot, *refs):
    out_ref = refs[-1]
    planes, slabs, cells = orbitals.shape
    part = cells // fold
    for f in range(fold):
        rows = slice(f * planes, (f + 1) * planes)
        cols = slice(f * part, (f + 1) * part)
        pieces = [ref[rows, :] for ref in refs[:-1]]
        local = local_pot[rows, :]
        for j in range(slabs):
            out_ref[:, j, cols] = local * orbitals[:, j, cols] + pick(place[0] ^ j, pieces)


def finish(place, orbitals, local_pot, pieces):
    planes, _, cells = orbitals.shape
    return pl.pallas_call(
        functools.partial(finish_kernel, fold_of(planes, cells)),
        out_shape=jax.ShapeDtypeStruct(orbitals.shape, jnp.float32),
        in_specs=with_scalar(2 + len(pieces)),
        out_specs=in_vmem(1)[0],
        compiler_params=pltpu.CompilerParams(vmem_limit_bytes=8 << 20),
        name="finish",
    )(place, orbitals, local_pot, *pieces)


def slab_swap(value, reach):
    size = lax.axis_size("slab")
    return lax.ppermute(value, "slab", [(i, i ^ reach) for i in range(size)])


def total_kernel(scale, shared, out_ref):
    summed = jnp.sum(shared[...], axis=0)
    out_ref[...] = scale * jnp.sum(summed, axis=1, keepdims=True)


def total_of(shared, scale):
    return pl.pallas_call(
        functools.partial(total_kernel, scale),
        out_shape=jax.ShapeDtypeStruct((1, 1), jnp.float32),
        in_specs=in_vmem(1),
        out_specs=in_vmem(1)[0],
        compiler_params=pltpu.CompilerParams(vmem_limit_bytes=8 << 20),
        name="total",
    )(shared)


def gather_ring(halves, band_index, bands):
    groups = [2 * p if p < bands // 2 else 2 * (bands - 1 - p) + 1 for p in range(bands)]
    place = band_index // 2
    position = jnp.where(band_index % 2 == 0, place, bands - 1 - place)

    def group_at(position):
        position = position % bands
        return jnp.where(position < bands // 2, 2 * position, 2 * (bands - 1 - position) + 1)

    def shift(value, by):
        moves = [(groups[p], groups[(p + by) % bands]) for p in range(bands)]
        return lax.ppermute(value, "band", moves)

    def pass_on(halves, by):
        return [shift(half, by) for half in halves]

    ahead = behind = halves
    blocks = []
    steps = bands // 2 - 1
    for step in range(steps):
        ahead = pass_on(ahead, 1)
        behind = pass_on(behind, -1)
        blocks.append((join(*ahead), group_at(position - step - 1)))
        blocks.append((join(*behind), group_at(position + step + 1)))
    head = shift(ahead[0], 1)
    tail = shift(behind[1], -1)
    blocks.append((join(head, tail), group_at(position + steps + 1)))
    return blocks


def body(orbitals, partners, counts):
    bands = lax.axis_size("band")
    slabs = lax.axis_size("slab")
    band_index = lax.axis_index("band")
    slab_index = lax.axis_index("slab")
    orb_group, _, _ = orbitals.shape
    total_orbs = orb_group * bands
    assert orb_group == slabs

    place = slab_index.astype(jnp.int32).reshape(1)
    by_plane = jnp.transpose(orbitals, (1, 0, 2))
    sends = prepare(place, by_plane)
    pieces = [sends[0]] + [slab_swap(sends[r], r) for r in range(1, slabs)]
    halves = [assemble(pieces[: slabs // 2]), assemble(pieces[slabs // 2 :])]
    own = join(*halves)
    others = gather_ring(halves, band_index, bands)
    force = clear((NX, NY * NZ))

    own, partners, counts = lax.optimization_barrier((own, partners, counts))
    tables = stage(place, slabs)

    groups = jnp.stack([group for _, group in others]).astype(jnp.int32)
    active = (slab_index < counts).astype(jnp.float32)
    mine = jnp.arange(bands, dtype=jnp.int32)[:, None] == band_index
    my_partners = jnp.sum(jnp.where(mine, partners, 0), axis=0)
    my_active = jnp.sum(jnp.where(mine, active, 0.0), axis=0)
    requested = jnp.sum(
        jnp.where(groups[:, None] == my_partners[None, :], my_active[None, :], 0.0), axis=1
    )
    wanted_by = jnp.sum(jnp.where(partners == band_index, active, 0.0), axis=1)
    chosen = groups[:, None] == jnp.arange(bands, dtype=jnp.int32)[None, :]
    returned = jnp.sum(jnp.where(chosen, wanted_by[None, :], 0.0), axis=1)
    weights = jnp.stack([requested + returned, requested], axis=1).reshape(-1)
    weights = jnp.broadcast_to(weights[:, None], weights.shape + (128,))

    energy = jnp.zeros((1, 128), jnp.float32)
    even, odd = squares_of([own] + [other for other, _ in others], slabs)
    from_core = slab_swap(odd, 1)
    for slot, (other, _) in enumerate(others):
        if slot < len(others) - 1:
            energy, force = pair_step(slot, weights, own, other, tables, force, energy)
        else:
            energy, *outgoing = pair_step(
                slot, weights, own, other, tables, force, energy, slabs, bands * slabs
            )

    for r in range(2, slabs, 2):
        outgoing[r] = pack(r // 2, outgoing[r], even, from_core)
    arrived = [outgoing[0]] + [slab_swap(outgoing[r], r) for r in range(1, slabs)]
    shared = lax.all_to_all(energy, ("band", "slab"), 0, 0)
    rows = arrived[0].shape[0]
    squares = even[0] + from_core[0] + sum(arrived[r][rows:] for r in range(2, slabs, 2))
    density = 2.0 / total_orbs * squares
    local_pot = slater_coeff * jnp.cbrt(density)
    forces = finish(place, by_plane, local_pot, arrived)
    total = total_of(shared, -1.0 / (2.0 * total_orbs * NX * NY * NZ))
    return jnp.transpose(forces, (1, 0, 2)), total.reshape(())


def solution(mesh):
    placed = (P("band", "slab", None), P(), P())
    return jax.shard_map(
        body, mesh=mesh, in_specs=placed, out_specs=(P("band", "slab", None), P()), check_vma=False
    )
```

```python
import functools
import math

import jax
import jax.numpy as jnp
import ml_dtypes
import numpy as np
from jax import lax
from jax.experimental import pallas as pl
from jax.experimental.pallas import tpu as pltpu
from jax.sharding import PartitionSpec as P


NX = 48
NY = 48
NZ = 48
NZP = 96
SIDE_X = NX // 2
GAP = 64


slater_coeff = -((3.0 / math.pi) ** (1.0 / 3.0))
exchange_mix = 0.25
screening = 0.25
row_row = (((1,), (1,)), ((), ()))


def split(value):
    high = value.astype(jnp.bfloat16)
    low = (value - high.astype(jnp.float32)).astype(jnp.bfloat16)
    return high, low


def cas(rows, cols, length):
    phase_angle = 2.0 * math.pi / length * (np.outer(rows, cols) % length)
    return np.cos(phase_angle) + np.sin(phase_angle)


def split_table(matrix):
    high = matrix.astype(ml_dtypes.bfloat16)
    return high, (matrix - high.astype(np.float64)).astype(ml_dtypes.bfloat16)


def wide(matrix):
    high, low = split_table(matrix)
    return np.concatenate([high, high, low], axis=1)


def tall(matrix):
    rows, cols = matrix.shape
    placed = np.zeros((2 * rows, 2 * GAP))
    placed[:rows, :cols] = matrix
    placed[rows:, GAP : GAP + cols] = matrix
    return np.concatenate(split_table(placed), axis=0)


def wavenumber_sq(length):
    return (2.0 * np.pi * np.fft.fftfreq(length)) ** 2


def transform_tables(slabs):
    x_waves, y_cells, z_cells, z_waves = (np.arange(count) for count in (NX, NY, NZ, NZP))
    planes = NX // slabs
    held_x = [(slab ^ (x_waves // planes)) * planes + x_waves % planes for slab in range(slabs)]
    total = (
        wavenumber_sq(NZP)[:, None, None]
        + wavenumber_sq(NX)[None, :, None]
        + wavenumber_sq(NY)[None, None, :]
    )
    kernel_table = 4.0 * math.pi / (NX * NY * NZP) / (total + screening * screening)
    y_matrix = cas(y_cells, y_cells, NY)
    forward = [wide(cas(x_waves, held, NX)) for held in held_x]
    quads = 4 * (x_waves[:SIDE_X] // 2) + x_waves[:SIDE_X] % 2
    kept = np.concatenate([quads, quads + 2])
    backward = [wide(cas(held, kept, NX)) for held in held_x]
    kernel_table = np.pad(kernel_table, ((0, 0), (0, 0), (0, GAP - NY)))
    lanes = 3 * NZP
    wides = [wide(y_matrix), wide(cas(z_cells, z_waves, NZP)), *forward, *backward]
    wides = [np.pad(matrix, ((0, 0), (0, lanes - matrix.shape[1]))) for matrix in wides]
    talls = [tall(cas(z_waves, z_cells, NZP)), tall(y_matrix)]
    flat = kernel_table.reshape(NZP, NX * GAP).astype(np.float32)
    return tuple(jnp.asarray(table) for table in (np.stack(wides), np.concatenate(talls), flat))


def apply_left(matrix, value):
    high, low = split(value)
    stacked = jnp.concatenate([high, low, high], axis=0)
    return jnp.dot(matrix, stacked, preferred_element_type=jnp.float32)


def apply_rows(matrix, high, low):
    half = matrix.shape[0] // 2
    both = lax.dot_general(matrix, high, row_row, preferred_element_type=jnp.float32)
    rest = lax.dot_general(matrix[:half], low, row_row, preferred_element_type=jnp.float32)
    return both[:half] + both[half:] + rest


def cut_into(refs, value):
    planes = NX // len(refs)
    part = refs[0].shape[1]
    fold = NY * NZ // part
    for r, ref in enumerate(refs):
        for f in range(fold):
            ref[f * planes : (f + 1) * planes, :] = value[
                r * planes : (r + 1) * planes, f * part : (f + 1) * part
            ]


def store_force(force_refs, value):
    if len(force_refs) == 1:
        force_refs[0][...] = value
    else:
        cut_into(force_refs, value)


def pair_kernel(
    slot, weights, own_ref, other_ref, x_fwd, y_fwd, z_fwd, table, z_inv, y_inv, x_inv,
    force_in, energy_in, *refs,
):
    energy_out, *force_refs, lines, high_rows, low_rows, field = refs
    total_weight = jnp.max(weights[2 * slot : 2 * slot + 1, :])
    request_weight = weights[2 * slot + 1 : 2 * slot + 2, :]

    @pl.when(total_weight == 0.0)
    def _():
        energy_out[...] = jnp.broadcast_to(energy_in[...], energy_out.shape)
        if len(force_refs) > 1:
            store_force(force_refs, force_in[...])

    @pl.when(total_weight != 0.0)
    def _():
        other = other_ref[...]
        density = own_ref[...] * other
        spectrum = apply_left(x_fwd[...], density)
        lines[...] = jnp.zeros_like(lines)
        for y in range(NY):
            rows = slice(y * SIDE_X, (y + 1) * SIDE_X)
            cols = slice(y * NZ, (y + 1) * NZ)
            lines[rows, :NZ] = spectrum[:SIDE_X, cols]
            lines[rows, GAP : GAP + NZ] = spectrum[SIDE_X:, cols]
        for q in range(SIDE_X):
            plane = apply_left(y_fwd[...], lines[pl.ds(q, NY, stride=SIDE_X), :])
            high, low = split(plane)
            rows = slice(q * GAP, q * GAP + NY)
            pad = slice(q * GAP + NY, (q + 1) * GAP)
            high_rows[rows, :] = high
            low_rows[rows, :] = low
            high_rows[pad, :] = jnp.zeros((GAP - NY, 2 * GAP), jnp.bfloat16)
            low_rows[pad, :] = jnp.zeros((GAP - NY, 2 * GAP), jnp.bfloat16)
        both = apply_rows(z_fwd[...], high_rows[...], low_rows[...])
        width = SIDE_X * GAP
        inner = []
        folded = jnp.zeros((1, 128), jnp.float32)
        for side in range(2):
            spectrum = both[side * NZP : (side + 1) * NZP]
            weighted = spectrum * table[:, side * width : (side + 1) * width]
            products = jnp.sum(spectrum * weighted, axis=0, keepdims=True)
            for start in range(0, width, 128):
                folded = folded + products[:, start : start + 128]
            inner.append(apply_left(z_inv[...], weighted))
        energy_out[...] = jnp.broadcast_to(
            energy_in[...] + request_weight * folded, energy_out.shape
        )
        for side in range(2):
            for pair in range(SIDE_X // 2):
                high, low = split(inner[side][:, pair * 2 * GAP : (pair + 1) * 2 * GAP])
                first = (side * (SIDE_X // 2) + pair) * GAP
                high_rows[first : first + NZ, :] = high
                low_rows[first : first + NZ, :] = low
        both = apply_rows(y_inv[...], high_rows[...], low_rows[...])
        for odd in range(2):
            for pair in range(SIDE_X // 2):
                first = (2 * pair + odd) * NY
                lines[first : first + NY, :] = both[
                    odd * NY : (odd + 1) * NY, pair * 2 * GAP : (pair + 1) * 2 * GAP
                ]
        for y in range(NY):
            plane = lines[pl.ds(y, SIDE_X, stride=NY), :]
            cols = slice(y * NZ, (y + 1) * NZ)
            field[:SIDE_X, cols] = plane[:, :NZ]
            field[SIDE_X:, cols] = plane[:, GAP : GAP + NZ]
        potential = apply_left(x_inv[...], field[...])
        store_force(
            force_refs, force_in[...] - (exchange_mix * total_weight) * (potential * other)
        )


def piece_shape(planes):
    fold = fold_of(planes, NY * NZ)
    return (planes * fold, NY * NZ // fold)


def pair_step(slot, weights, own, other, tables, force, energy, pieces=1, copies=None):
    piece = force.shape if pieces == 1 else piece_shape(NX // pieces)
    energy_shape = energy.shape if copies is None else (copies,) + energy.shape
    outs = [jax.ShapeDtypeStruct(energy_shape, jnp.float32)]
    outs += [jax.ShapeDtypeStruct(piece, jnp.float32)] * pieces
    return pl.pallas_call(
        functools.partial(pair_kernel, slot),
        out_shape=outs,
        in_specs=in_vmem(5 + len(tables)),
        out_specs=in_vmem(1 + pieces),
        scratch_shapes=[
            pltpu.VMEM((SIDE_X * NY, 2 * GAP), jnp.float32),
            pltpu.VMEM((SIDE_X * GAP, 2 * GAP), jnp.bfloat16),
            pltpu.VMEM((SIDE_X * GAP, 2 * GAP), jnp.bfloat16),
            pltpu.VMEM((NX, NY * NZ), jnp.float32),
        ],
        input_output_aliases={3 + len(tables): 1} if pieces == 1 else {},
        compiler_params=pltpu.CompilerParams(vmem_limit_bytes=16 << 20),
        cost_estimate=pl.CostEstimate(flops=3 << 30, transcendentals=0, bytes_accessed=3 << 20),
        name="pair_step",
    )(weights, own, other, *tables, force, energy)


def fold_of(planes, cells):
    return 2 if (2 * planes) % 8 == 0 and cells % 256 == 0 else 1


def in_vmem(count):
    return [pl.BlockSpec(memory_space=pltpu.VMEM)] * count


def with_scalar(count):
    return [pl.BlockSpec(memory_space=pltpu.SMEM)] + in_vmem(count)


def pick(place, choices):
    chosen = choices[0]
    for index in range(1, len(choices)):
        chosen = jnp.where(place == index, choices[index], chosen)
    return chosen


def prepare_kernel(fold, place, orbitals, *out_refs):
    planes, slabs, cells = orbitals.shape
    part = cells // fold
    for f in range(fold):
        rows = slice(f * planes, (f + 1) * planes)
        blocks = [orbitals[:, j, f * part : (f + 1) * part] for j in range(slabs)]
        for r in range(slabs):
            out_refs[r][rows, :] = pick(place[0] ^ r, blocks)


def prepare(place, orbitals):
    planes, slabs, cells = orbitals.shape
    fold = fold_of(planes, cells)
    piece = jax.ShapeDtypeStruct((planes * fold, cells // fold), jnp.float32)
    return pl.pallas_call(
        functools.partial(prepare_kernel, fold),
        out_shape=[piece] * slabs,
        in_specs=with_scalar(1),
        out_specs=in_vmem(slabs),
        compiler_params=pltpu.CompilerParams(vmem_limit_bytes=8 << 20),
        name="prepare",
    )(place, orbitals)


def assemble_kernel(fold, *refs):
    out_ref = refs[-1]
    planes = refs[0].shape[0] // fold
    part = refs[0].shape[1]
    for r, ref in enumerate(refs[:-1]):
        for f in range(fold):
            out_ref[r * planes : (r + 1) * planes, f * part : (f + 1) * part] = ref[
                f * planes : (f + 1) * planes, :
            ]


def assemble(pieces):
    rows, part = pieces[0].shape
    fold = NY * NZ // part
    return pl.pallas_call(
        functools.partial(assemble_kernel, fold),
        out_shape=jax.ShapeDtypeStruct((rows // fold * len(pieces), NY * NZ), jnp.float32),
        in_specs=in_vmem(len(pieces)),
        out_specs=in_vmem(1)[0],
        compiler_params=pltpu.CompilerParams(vmem_limit_bytes=8 << 20),
        name="assemble",
    )(*pieces)


def clear_kernel(out_ref):
    out_ref[...] = jnp.zeros_like(out_ref)


def clear(shape):
    return pl.pallas_call(
        clear_kernel,
        out_shape=jax.ShapeDtypeStruct(shape, jnp.float32),
        out_specs=in_vmem(1)[0],
        compiler_params=pltpu.CompilerParams(vmem_limit_bytes=8 << 20),
        name="clear",
    )()


def squares_kernel(*refs):
    *blocks, even_ref, odd_ref = refs
    slabs = 2 * even_ref.shape[0]
    squares = blocks[0][...] * blocks[0][...]
    for ref in blocks[1:]:
        squares = squares + ref[...] * ref[...]
    pieces = [ref.at[k] for k in range(slabs // 2) for ref in (even_ref, odd_ref)]
    cut_into(pieces, squares)


def squares_of(blocks, slabs):
    stack = jax.ShapeDtypeStruct((slabs // 2,) + piece_shape(NX // slabs), jnp.float32)
    return pl.pallas_call(
        squares_kernel,
        out_shape=[stack, stack],
        in_specs=in_vmem(len(blocks)),
        out_specs=in_vmem(2),
        compiler_params=pltpu.CompilerParams(vmem_limit_bytes=8 << 20),
        name="squares",
    )(*blocks)


def pack_kernel(k, piece, mine, theirs, out_ref):
    rows = piece.shape[0]
    out_ref[:rows, :] = piece[...]
    out_ref[rows:, :] = mine[k] + theirs[k]


def pack(k, piece, mine, theirs):
    rows, part = piece.shape
    return pl.pallas_call(
        functools.partial(pack_kernel, k),
        out_shape=jax.ShapeDtypeStruct((2 * rows, part), jnp.float32),
        in_specs=in_vmem(3),
        out_specs=in_vmem(1)[0],
        compiler_params=pltpu.CompilerParams(vmem_limit_bytes=8 << 20),
        name="pack",
    )(piece, mine, theirs)


def stage_kernel(
    slabs, place, wides, talls, flat, x_fwd, y_fwd, z_fwd, table, z_inv, y_inv, x_inv
):
    y_fwd[...] = wides[0, :, : 3 * NY]
    z_inv[...] = wides[1]
    x_fwd[...] = pick(place[0], [wides[2 + slab, :, : 3 * NX] for slab in range(slabs)])
    x_inv[...] = pick(place[0], [wides[2 + slabs + slab, :, : 3 * NX] for slab in range(slabs)])
    z_fwd[...] = talls[: 4 * NZP]
    y_inv[...] = talls[4 * NZP :]
    table[...] = flat[...]


def stage(place, slabs):
    tables = transform_tables(slabs)
    halves = jnp.bfloat16
    shapes = [
        ((NX, 3 * NX), halves), ((NY, 3 * NY), halves), ((4 * NZP, 2 * GAP), halves),
        ((NZP, NX * GAP), jnp.float32), ((NZ, 3 * NZP), halves), ((4 * NY, 2 * GAP), halves),
        ((NX, 3 * NX), halves),
    ]
    return pl.pallas_call(
        functools.partial(stage_kernel, slabs),
        out_shape=[jax.ShapeDtypeStruct(shape, kind) for shape, kind in shapes],
        in_specs=with_scalar(len(tables)),
        out_specs=in_vmem(len(shapes)),
        compiler_params=pltpu.CompilerParams(vmem_limit_bytes=8 << 20),
        name="stage",
    )(place, *tables)


def join_kernel(*refs):
    out_ref = refs[-1]
    first = 0
    for ref in refs[:-1]:
        out_ref[first : first + ref.shape[0], :] = ref[...]
        first += ref.shape[0]


def join(*parts):
    rows = sum(part.shape[0] for part in parts)
    return pl.pallas_call(
        join_kernel,
        out_shape=jax.ShapeDtypeStruct((rows,) + parts[0].shape[1:], jnp.float32),
        in_specs=in_vmem(len(parts)),
        out_specs=in_vmem(1)[0],
        compiler_params=pltpu.CompilerParams(vmem_limit_bytes=8 << 20),
        name="join",
    )(*parts)


def finish_kernel(fold, place, orbitals, local_pot, *refs):
    out_ref = refs[-1]
    planes, slabs, cells = orbitals.shape
    part = cells // fold
    for f in range(fold):
        rows = slice(f * planes, (f + 1) * planes)
        cols = slice(f * part, (f + 1) * part)
        pieces = [ref[rows, :] for ref in refs[:-1]]
        local = local_pot[rows, :]
        for j in range(slabs):
            out_ref[:, j, cols] = local * orbitals[:, j, cols] + pick(place[0] ^ j, pieces)


def finish(place, orbitals, local_pot, pieces):
    planes, _, cells = orbitals.shape
    return pl.pallas_call(
        functools.partial(finish_kernel, fold_of(planes, cells)),
        out_shape=jax.ShapeDtypeStruct(orbitals.shape, jnp.float32),
        in_specs=with_scalar(2 + len(pieces)),
        out_specs=in_vmem(1)[0],
        compiler_params=pltpu.CompilerParams(vmem_limit_bytes=8 << 20),
        name="finish",
    )(place, orbitals, local_pot, *pieces)


def slab_swap(value, reach):
    size = lax.axis_size("slab")
    return lax.ppermute(value, "slab", [(i, i ^ reach) for i in range(size)])


def total_kernel(scale, shared, out_ref):
    summed = jnp.sum(shared[...], axis=0)
    out_ref[...] = scale * jnp.sum(summed, axis=1, keepdims=True)


def total_of(shared, scale):
    return pl.pallas_call(
        functools.partial(total_kernel, scale),
        out_shape=jax.ShapeDtypeStruct((1, 1), jnp.float32),
        in_specs=in_vmem(1),
        out_specs=in_vmem(1)[0],
        compiler_params=pltpu.CompilerParams(vmem_limit_bytes=8 << 20),
        name="total",
    )(shared)


def gather_ring(halves, band_index, bands):
    groups = [2 * p if p < bands // 2 else 2 * (bands - 1 - p) + 1 for p in range(bands)]
    place = band_index // 2
    position = jnp.where(band_index % 2 == 0, place, bands - 1 - place)

    def group_at(position):
        position = position % bands
        return jnp.where(position < bands // 2, 2 * position, 2 * (bands - 1 - position) + 1)

    def shift(value, by):
        moves = [(groups[p], groups[(p + by) % bands]) for p in range(bands)]
        return lax.ppermute(value, "band", moves)

    def pass_on(halves, by):
        return [shift(half, by) for half in halves]

    ahead = behind = halves
    blocks = []
    steps = bands // 2 - 1
    for step in range(steps):
        ahead = pass_on(ahead, 1)
        behind = pass_on(behind, -1)
        joined = join(*ahead), join(*behind)
        blocks.append((joined[0], group_at(position - step - 1)))
        blocks.append((joined[1], group_at(position + step + 1)))
    head = shift(ahead[0], 1)
    tail = shift(behind[1], -1)
    blocks.append((join(head, tail), group_at(position + steps + 1)))
    return blocks


def body(orbitals, partners, counts):
    bands = lax.axis_size("band")
    slabs = lax.axis_size("slab")
    band_index = lax.axis_index("band")
    slab_index = lax.axis_index("slab")
    orb_group, _, _ = orbitals.shape
    total_orbs = orb_group * bands
    assert orb_group == slabs

    place = slab_index.astype(jnp.int32).reshape(1)
    by_plane = jnp.transpose(orbitals, (1, 0, 2))
    sends = prepare(place, by_plane)
    pieces = [sends[0]] + [slab_swap(sends[r], r) for r in range(1, slabs)]
    halves = [assemble(pieces[: slabs // 2]), assemble(pieces[slabs // 2 :])]
    own = join(*halves)
    others = gather_ring(halves, band_index, bands)
    force = clear((NX, NY * NZ))

    own, partners, counts = lax.optimization_barrier((own, partners, counts))
    tables = stage(place, slabs)

    groups = jnp.stack([group for _, group in others]).astype(jnp.int32)
    active = (slab_index < counts).astype(jnp.float32)
    mine = jnp.arange(bands, dtype=jnp.int32)[:, None] == band_index
    my_partners = jnp.sum(jnp.where(mine, partners, 0), axis=0)
    my_active = jnp.sum(jnp.where(mine, active, 0.0), axis=0)
    requested = jnp.sum(
        jnp.where(groups[:, None] == my_partners[None, :], my_active[None, :], 0.0), axis=1
    )
    wanted_by = jnp.sum(jnp.where(partners == band_index, active, 0.0), axis=1)
    chosen = groups[:, None] == jnp.arange(bands, dtype=jnp.int32)[None, :]
    returned = jnp.sum(jnp.where(chosen, wanted_by[None, :], 0.0), axis=1)
    weights = jnp.stack([requested + returned, requested], axis=1).reshape(-1)
    weights = jnp.broadcast_to(weights[:, None], weights.shape + (128,))

    energy = jnp.zeros((1, 128), jnp.float32)
    even, odd = squares_of([own] + [other for other, _ in others], slabs)
    from_core = slab_swap(odd, 1)
    for slot, (other, _) in enumerate(others):
        if slot < len(others) - 1:
            energy, force = pair_step(slot, weights, own, other, tables, force, energy)
        else:
            energy, *outgoing = pair_step(
                slot, weights, own, other, tables, force, energy, slabs, bands * slabs
            )

    for r in range(2, slabs, 2):
        outgoing[r] = pack(r // 2, outgoing[r], even, from_core)
    arrived = [outgoing[0]] + [slab_swap(outgoing[r], r) for r in range(1, slabs)]
    shared = lax.all_to_all(energy, ("band", "slab"), 0, 0)
    rows = arrived[0].shape[0]
    squares = even[0] + from_core[0] + sum(arrived[r][rows:] for r in range(2, slabs, 2))
    density = 2.0 / total_orbs * squares
    local_pot = slater_coeff * jnp.cbrt(density)
    forces = finish(place, by_plane, local_pot, arrived)
    total = total_of(shared, -1.0 / (2.0 * total_orbs * NX * NY * NZ))
    return jnp.transpose(forces, (1, 0, 2)), total.reshape(())


def solution(mesh):
    placed = (P("band", "slab", None), P(), P())
    return jax.shard_map(
        body, mesh=mesh, in_specs=placed, out_specs=(P("band", "slab", None), P()), check_vma=False
    )
```
